128 devices in a mesh: outer: 8 (over z, core), inner: 16 (over y, x).
Axes of the slice: x: 4, y: 4, z: 4, core: 2. Of those that a mesh axis runs over, the one named last changes fastest.
Arguments:
- tokens_in: bfloat16 [16384, 2048], P(('outer', 'inner')), may hold values from -6 to 6
- expert_ids: int32 [16384, 10], P(('outer', 'inner')), may hold values from 0 to 255, all different within a row; in each aligned block of 128 rows (0 to 127, 128 to 255, ...) at most 6 rows name the same one
- route_weight: float32 [16384, 10], P(('outer', 'inner')), may hold values from 0.05 to 1
- first_gain: float32 [2048], replicated, may hold values from 0.5 to 1.5
- gate_weight: bfloat16 [256, 2048, 512], P(('outer', 'inner')), may hold values from -0.125 to 0.125
- up_weight: bfloat16 [256, 2048, 512], P(('outer', 'inner')), may hold values from -0.125 to 0.125
- down_weight: bfloat16 [256, 512, 2048], P(('outer', 'inner')), may hold values from -0.25 to 0.25
- second_gain: float32 [2048], replicated, may hold values from 0.5 to 1.5
- mixer_weight: bfloat16 [2048, 4096], P(None, 'inner'), may hold values from -0.125 to 0.125
- gating_weight: bfloat16 [2048, 32], replicated, may hold values from -0.125 to 0.125
- filter_taps: bfloat16 [4, 4096], replicated, may hold values from -3 to 3
- decay_log: float32 [16], replicated, may hold values from -9 to -3
- decay_bias: float32 [16], replicated, may hold values from -1 to 1
- output_gain: float32 [128], replicated, may hold values from 0.5 to 1.5
Outputs:
- hidden_out: bfloat16 [16384, 2048], P(('outer', 'inner'))
- core_out: bfloat16 [16384, 2048], P(('outer', 'inner'))
The draws below stay inside these ranges and needn't reach their ends.
Inputs may be any that keep to these rules, and one draw needn't show every extreme that they name: `expert_ids`: each token names 10 different experts; the 128 rows of one device name any one expert at most 6 times, a bound that some block reaches.
All inputs are finite; a program needn't handle non-finite values.
Results may differ from the reference program's by a relative error of at most 0.015.
Values may be sent and summed in bfloat16 or wider, within the bound.
A program may use at most 576 MiB of HBM per device.

```python
import math
import jax
import jax.numpy as jnp
import numpy as np
from jax import lax

D = 2048
FF = 512
TOPK = 10
HD = 128
KH = 8
VH = 16
CONV = 4
TOK_DEV = 128
TOKENS = 16384
EXPERTS = 256
CAP = 6
QKVW = 4096
N_OUTER = 8
N_INNER = 16


def levels(rng, shape, split, least, high):
    factor_of, own = 1.0, jax.random.fold_in(rng, 6)
    for dim, blocks in split:
        draws = jnp.exp(jax.random.uniform(jax.random.fold_in(own, dim), (blocks,), jnp.float32, least / len(split), high / len(split)))
        factor_of = factor_of * jnp.repeat(draws, shape[dim] // blocks).reshape([-1 if axis == dim else 1 for axis in range(len(shape))])
    return factor_of


def deal_out(key, own, number, rows, count, top, bound, lean):
    ranking = jax.random.permutation(key, count)
    packed, common = shares(count, rows * top, bound, lean, True), shares(count, rows * top, bound, lean, False)
    places = jnp.arange(count)

    def named(tallies, offset_by):
        used = int((tallies > 0).sum())
        fixed = max(1, used // 4)
        passed = fixed + (places - fixed + offset_by * (used - fixed)) % max(1, count - fixed)
        return jnp.zeros((count,), jnp.int32).at[ranking[jnp.where(places < fixed, places, passed)]].set(jnp.asarray(tallies, jnp.int32))

    tallies = jnp.where(number % 4 == 0, named(packed, number // 4), named(common, number - number // 4 - 1))
    mixed = jax.random.permutation(jax.random.fold_in(own, 3), count)
    donor, sink = mixed[0:count // 2 * 2:2], mixed[1:count // 2 * 2:2]
    slack = jnp.minimum(tallies[donor] - 1, bound - tallies[sink]) // 2
    slack = jnp.where((donor == ranking[0]) | (sink == ranking[0]) | (tallies[sink] == 0), 0, jnp.maximum(slack, 0))
    passed = jax.random.randint(jax.random.fold_in(own, 4), (count // 2,), 0, 1 << 20) % (slack + 1)
    tallies = tallies.at[donor].add(-passed).at[sink].add(passed)
    members = jnp.searchsorted(jnp.cumsum(tallies), jnp.arange(rows * top), side="right").astype(jnp.int32)
    table = members.reshape(top, rows).T
    table = table[jax.random.permutation(jax.random.fold_in(own, 1), rows)]
    offset_by = jax.random.randint(jax.random.fold_in(own, 2), (rows, 1), 0, top)
    return jnp.take_along_axis(table, (jnp.arange(top)[None, :] + offset_by) % top, axis=1)


def shares(amount, total, bound, skew, full):
    weights = [(1 << 20) // math.isqrt(standing ** skew) + 1 for standing in range(1, amount + 1)]
    largest = bound if full else min(bound, max(-(-total // amount), total * weights[0] // sum(weights)))
    least = 1 if total - largest >= amount - 1 else 0
    holding, spare = [largest] + [least] * (amount - 1), total - largest - least * (amount - 1)
    while spare > 0:
        candidates = [i for i in range(1, amount) if holding[i] < largest] or [i for i in range(1, amount) if holding[i] < bound]
        pool, left = sum([weights[i] for i in candidates]), spare
        for i in candidates:
            more = min(bound - holding[i], max(1, left * weights[i] // pool), spare)
            holding[i] = holding[i] + more
            spare = spare - more
    return np.array(holding)


def normal_values(rng, shape, width, bound, shards=(), kind=jnp.bfloat16):
    values = jax.random.normal(rng, shape, jnp.float32) * width
    if len(shards) > 0:
        values = levels(rng, shape, shards, -0.22, 0.18) * values
    return jnp.clip(values, min=-bound, max=bound).astype(kind)


def setup_inputs(seed: int = 0) -> dict:
    arg_keys = jax.random.split(jax.random.key(seed), 15)
    tokens_in = normal_values(arg_keys[0], (TOKENS, D), 1.0, 6.0, ((0, 128),))
    expert_ids_keys = jax.random.split(jax.random.fold_in(arg_keys[1], 1), TOKENS // TOK_DEV)
    expert_ids_turns = jax.random.permutation(jax.random.fold_in(arg_keys[1], 3), TOKENS // TOK_DEV)
    expert_ids = jax.vmap(lambda own, number: deal_out(jax.random.fold_in(arg_keys[1], 2), own, number, TOK_DEV, EXPERTS, TOPK, CAP, 2))(expert_ids_keys, expert_ids_turns).reshape((TOKENS, TOPK))
    route_weight = jnp.clip(jnp.exp(math.log(1.0) - 2.9957323 * jax.random.uniform(arg_keys[2], (TOKENS, TOPK), jnp.float32) ** levels(arg_keys[2], (TOKENS, TOPK), ((0, 128),), -0.2, 0.2)), 0.05, 1.0)
    first_gain = jnp.clip(1.0 + 0.1 * jax.random.normal(arg_keys[3], (D,), jnp.float32), 0.5, 1.5)
    gate_weight = normal_values(arg_keys[4], (EXPERTS, D, FF), D ** -0.5, 0.125, ((0, 128),))
    up_weight = normal_values(arg_keys[5], (EXPERTS, D, FF), D ** -0.5, 0.125, ((0, 128),))
    down_weight = normal_values(arg_keys[6], (EXPERTS, FF, D), FF ** -0.5, 0.25, ((0, 128),))
    second_gain = jnp.clip(1.0 + 0.1 * jax.random.normal(arg_keys[7], (D,), jnp.float32), 0.5, 1.5)
    mixer_weight = normal_values(arg_keys[8], (D, QKVW), D ** -0.5, 0.125, ((1, 16),))
    gating_weight = normal_values(arg_keys[9], (D, 2 * VH), D ** -0.5, 0.125)
    filter_taps = normal_values(arg_keys[10], (CONV, QKVW), 0.5, 3.0)
    decay_log = jnp.clip(jax.random.uniform(arg_keys[11], (VH,), jnp.float32, -9.0, -3.0), -9.0, -3.0)
    decay_bias = jnp.clip(jax.random.uniform(arg_keys[12], (VH,), jnp.float32, -1.0, 1.0), -1.0, 1.0)
    output_gain = jnp.clip(1.0 + 0.1 * jax.random.normal(arg_keys[13], (HD,), jnp.float32), 0.5, 1.5)
    return {"tokens_in": tokens_in, "expert_ids": expert_ids, "route_weight": route_weight, "first_gain": first_gain, "gate_weight": gate_weight, "up_weight": up_weight, "down_weight": down_weight, "second_gain": second_gain, "mixer_weight": mixer_weight, "gating_weight": gating_weight, "filter_taps": filter_taps, "decay_log": decay_log, "decay_bias": decay_bias, "output_gain": output_gain}


def rms_scale(values, gain):
    wide = values.astype(jnp.float32)
    return wide * lax.rsqrt(lax.optimization_barrier(jnp.mean(wide * wide, axis=-1, keepdims=True)) + 1e-06) * gain

def unit_heads(values):
    return values * lax.rsqrt(lax.optimization_barrier(jnp.sum(values * values, axis=-1, keepdims=True)) + 1e-06)

def reference(tokens_in, expert_ids, route_weight, first_gain, gate_weight, up_weight, down_weight, second_gain, mixer_weight, gating_weight, filter_taps, decay_log, decay_bias, output_gain):
    normed_first = rms_scale(tokens_in, first_gain).astype(jnp.bfloat16)
    mix_weight = route_weight / lax.optimization_barrier(jnp.sum(route_weight, axis=1, keepdims=True))
    pairs = TOKENS * TOPK
    capacity_rows = N_OUTER * N_INNER * CAP
    flat = expert_ids.reshape(-1).astype(jnp.int32)
    order = jnp.argsort(flat, stable=True).astype(jnp.int32)
    counts = jnp.zeros((EXPERTS,), jnp.int32).at[flat].add(1)
    starts = jnp.cumsum(counts) - counts
    sorted_ids = flat[order]
    position = jnp.arange(pairs, dtype=jnp.int32) - starts[sorted_ids]
    table = jnp.full((EXPERTS, capacity_rows), pairs, jnp.int32).at[sorted_ids, position].set(order)
    pair_token = jnp.concatenate([jnp.arange(pairs, dtype=jnp.int32) // TOPK, jnp.full((1,), TOKENS, jnp.int32)])
    pair_weight = jnp.concatenate([mix_weight.reshape(-1), jnp.zeros((1,), jnp.float32)])
    padded_rows = jnp.concatenate([normed_first, jnp.zeros((1, D), jnp.bfloat16)], axis=0)

    def expert_step(total, item):
        gate_mat, up_mat, down_mat, rows = item
        owner = pair_token[rows]
        chosen = padded_rows[owner]
        gate = jnp.dot(chosen, gate_mat, preferred_element_type=jnp.float32)
        upper = jnp.dot(chosen, up_mat, preferred_element_type=jnp.float32)
        hidden = (jax.nn.silu(gate) * upper).astype(jnp.bfloat16)
        result = jnp.dot(hidden, down_mat, preferred_element_type=jnp.float32).astype(jnp.bfloat16)
        result = lax.optimization_barrier(result).astype(jnp.float32)
        total = total.at[owner].add(result * pair_weight[rows][:, None])
        return (total, None)
    totals, _ = lax.scan(expert_step, jnp.zeros((TOKENS + 1, D), jnp.float32), (gate_weight, up_weight, down_weight, table))
    hidden_out = (tokens_in.astype(jnp.float32) + totals[:TOKENS]).astype(jnp.bfloat16)
    normed_second = rms_scale(hidden_out, second_gain).astype(jnp.bfloat16)
    projected = jnp.dot(normed_second, mixer_weight, preferred_element_type=jnp.float32).astype(jnp.bfloat16)
    gating = jnp.dot(normed_second, gating_weight, preferred_element_type=jnp.float32)
    padded = jnp.concatenate([jnp.zeros((CONV - 1, QKVW), jnp.float32), projected.astype(jnp.float32)], axis=0)
    filtered = jnp.zeros((TOKENS, QKVW), jnp.float32)
    for tap_index in range(CONV):
        filtered = filtered + filter_taps[tap_index].astype(jnp.float32) * padded[tap_index:tap_index + TOKENS]
    filtered = jax.nn.silu(filtered)
    ratio = VH // KH
    queries = unit_heads(filtered[:, :KH * HD].reshape(TOKENS, KH, HD)) * HD ** (-0.5)
    keys = unit_heads(filtered[:, KH * HD:2 * KH * HD].reshape(TOKENS, KH, HD))
    values = filtered[:, 2 * KH * HD:].reshape(TOKENS, VH, HD)
    queries = jnp.repeat(queries, ratio, axis=1)
    keys = jnp.repeat(keys, ratio, axis=1)
    strength = jax.nn.sigmoid(gating[:, :VH])
    log_decay = -jnp.exp(decay_log) * jax.nn.softplus(gating[:, VH:] + decay_bias)

    def token_step(running_state, item):
        query_at_step, key_at_step, value_t, strength_t, log_t = item
        decay = jnp.exp(log_t)
        running_state = decay[:, None, None] * running_state
        initial_estimate = jnp.einsum('jgn,jg->jn', running_state, key_at_step, precision=lax.Precision.HIGHEST)
        running_state = running_state + strength_t[:, None, None] * key_at_step[:, :, None] * (value_t - initial_estimate)[:, None, :]
        output_at_step = jnp.einsum('jgn,jg->jn', running_state, query_at_step, precision=lax.Precision.HIGHEST)
        return (running_state, output_at_step)
    _, attended = lax.scan(token_step, jnp.zeros((VH, HD, HD), jnp.float32), (queries, keys, values, strength, log_decay))
    core_out = rms_scale(attended, output_gain).astype(jnp.bfloat16).reshape(TOKENS, VH * HD)
    return (hidden_out, core_out)
```

```python
import jax
import jax.numpy as jnp
from jax import lax
from jax.sharding import PartitionSpec as P


def shifted(value, axis, steps):
    count = lax.axis_size(axis)
    leading, last = (max(0, -steps), min(count, count - steps))
    return lax.ppermute(value, axis, [(source, source + steps) for source in range(leading, last)])


def prefix_2(x, axis, join, neutral):
    place = lax.axis_index(axis)
    gathered = jax.tree.map(
        lambda a, kind: lax.all_gather(a.astype(kind), axis), x, (jnp.bfloat16, jnp.bfloat16)
    )
    state = jax.tree.map(lambda a, e: jnp.zeros_like(a) + jnp.asarray(e, a.dtype), x, neutral)

    def one(lap, state):
        return join(
            state,
            jax.tree.map(
                lambda a, own: lax.dynamic_index_in_dim(a, lap, 0, False).astype(own.dtype),
                gathered,
                x,
            ),
        )

    return lax.fori_loop(0, place, one, state)


def shortened(x):

    def short(part):
        return part.astype(jnp.bfloat16) if part.dtype == jnp.float32 else part

    return jax.tree.map(short, x)


def spread_2(value, axis, source):
    kept = jnp.where(lax.axis_index(axis) == source, value, 0).astype(value.dtype)
    return lax.psum(kept, axis)


def entering(x, axis, combine, identity):
    length, place = (lax.axis_size(axis), lax.axis_index(axis))
    everything = jax.tree.map(
        lambda part, kind: lax.all_gather(part.astype(kind), axis),
        x,
        jax.tree.map(lambda a: jnp.bfloat16 if a.dtype == jnp.float32 else a.dtype, x),
    )
    start = jax.tree.map(
        lambda part, zero: jnp.broadcast_to(jnp.asarray(zero, part.dtype), part.shape), x, identity
    )

    def lap(k, before):
        reached = k < place
        new = combine(
            before, jax.tree.map(lambda part, own: part[k].astype(own.dtype), everything, x)
        )
        return jax.tree.map(lambda a, b: jnp.where(reached, a, b), new, before)

    return lax.fori_loop(0, length, lap, start)


def rms_scale(values, gain):
    wide = values.astype(jnp.float32)
    return wide * lax.rsqrt(jnp.mean(wide * wide, axis=-1, keepdims=True) + 1e-06) * gain


def unit_heads(values):
    return values * lax.rsqrt(jnp.sum(values * values, axis=-1, keepdims=True) + 1e-06)


def run_experts(piece, gate_weight, up_weight, down_weight):
    gate = jnp.einsum("esd,edf->esf", piece, gate_weight, preferred_element_type=jnp.float32)
    upper = jnp.einsum("esd,edf->esf", piece, up_weight, preferred_element_type=jnp.float32)
    hidden = (jax.nn.silu(gate) * upper).astype(jnp.bfloat16)
    return jnp.einsum(
        "esf,efd->esd", hidden, down_weight, preferred_element_type=jnp.float32
    ).astype(jnp.bfloat16)


def unit_lower_inverse(system):
    size = system.shape[-1]
    if size == 1:
        return jnp.ones_like(system)
    half = size // 2
    both = unit_lower_inverse(jnp.stack([system[..., :half, :half], system[..., half:, half:]]))
    first, second = both[0], both[1]
    corner = -jnp.einsum(
        "...ij,...jk->...ik",
        second,
        jnp.einsum("...ij,...jk->...ik", system[..., half:, :half], first, precision=lax.Precision.HIGHEST),
        precision=lax.Precision.HIGHEST,
    )
    top = jnp.concatenate([first, jnp.zeros_like(first)], axis=-1)
    bottom = jnp.concatenate([corner, second], axis=-1)
    return jnp.concatenate([top, bottom], axis=-2)


def join_maps(earlier, later):
    first_map, first_state = earlier
    next_map, next_state = later
    joined_map = jnp.einsum("hij,hjk->hik", next_map, first_map, precision=lax.Precision.HIGHEST)
    joined_state = (
        jnp.einsum("hij,hjv->hiv", next_map, first_state, precision=lax.Precision.HIGHEST)
        + next_state
    )
    return (joined_map, joined_state)


def per_device(
    tokens_in,
    expert_ids,
    route_weight,
    first_gain,
    gate_weight,
    up_weight,
    down_weight,
    second_gain,
    mixer_weight,
    gating_weight,
    filter_taps,
    decay_log,
    decay_bias,
    output_gain,
):
    n_outer = lax.axis_size("outer")
    n_inner = lax.axis_size("inner")
    n_dev = n_outer * n_inner
    tok_count, width = tokens_in.shape
    top_count = expert_ids.shape[1]
    local_experts = gate_weight.shape[0]
    experts_all = local_experts * n_dev
    capacity = max(2, 6 * tok_count * top_count // (5 * experts_all))
    normed_first = rms_scale(tokens_in, first_gain).astype(jnp.bfloat16)
    mix_weight = route_weight / jnp.sum(route_weight, axis=1, keepdims=True)
    flat_ids = expert_ids
    target = (
        flat_ids % local_experts * (n_dev * capacity)
        + flat_ids // local_experts * capacity
    )
    onehot = (flat_ids[:, :, None] == jnp.arange(experts_all, dtype=jnp.int32)[None, None, :]).astype(
        jnp.int32
    )
    counted = jnp.sum(onehot, axis=1)
    before = jnp.cumsum(counted, axis=0) - counted
    slot_index = jnp.sum(before[:, None, :] * onehot, axis=2)
    target = target + slot_index
    slots = jnp.arange(n_dev * local_experts * capacity, dtype=jnp.int32)
    hits = target[:, :, None] == slots[None, None, :]
    dispatch = jnp.any(hits, axis=1).astype(jnp.bfloat16)
    outgoing = jnp.einsum(
        "ts,td->sd", dispatch, normed_first, preferred_element_type=jnp.float32
    ).astype(jnp.bfloat16)
    outgoing = outgoing.reshape(local_experts, n_dev * capacity, width)
    served = run_experts(
        lax.all_to_all(outgoing, ("outer", "inner"), split_axis=1, concat_axis=1, tiled=True),
        gate_weight,
        up_weight,
        down_weight,
    )
    returned = lax.all_to_all(served, ("outer", "inner"), split_axis=1, concat_axis=1, tiled=True)
    returned = returned.reshape(-1, width)
    combine = jnp.sum(jnp.where(hits, mix_weight[:, :, None], 0.0), axis=1)
    combine_hi = combine.astype(jnp.bfloat16)
    combine_lo = (combine - combine_hi.astype(jnp.float32)).astype(jnp.bfloat16)
    mixture = jnp.dot(combine_hi, returned, preferred_element_type=jnp.float32) + jnp.dot(
        combine_lo, returned, preferred_element_type=jnp.float32
    )
    hidden_out = (tokens_in.astype(jnp.float32) + mixture).astype(jnp.bfloat16)
    normed_second = rms_scale(hidden_out, second_gain).astype(jnp.bfloat16)
    mixed = jnp.dot(
        normed_second,
        lax.all_gather(mixer_weight, "inner", axis=1, tiled=True),
        preferred_element_type=jnp.float32,
    )
    projected = mixed.astype(jnp.bfloat16)
    gating = jnp.dot(normed_second, gating_weight, preferred_element_type=jnp.float32)
    taps = filter_taps.shape[0]
    rim = shifted(projected[tok_count - (taps - 1) :], ("outer", "inner"), 1)
    padded = jnp.concatenate([rim, projected], axis=0).astype(jnp.float32)
    filtered = jnp.zeros(projected.shape, jnp.float32)
    for tap_index in range(taps):
        filtered = (
            filtered
            + filter_taps[tap_index].astype(jnp.float32) * padded[tap_index : tap_index + tok_count]
        )
    filtered = jax.nn.silu(filtered)
    head_dim = output_gain.shape[0]
    value_heads = decay_log.shape[0]
    key_heads = (projected.shape[1] - value_heads * head_dim) // (2 * head_dim)
    ratio = value_heads // key_heads
    queries = unit_heads(
        filtered[:, : key_heads * head_dim].reshape(tok_count, key_heads, head_dim)
    ) * head_dim ** (-0.5)
    keys = unit_heads(
        filtered[:, key_heads * head_dim : 2 * key_heads * head_dim].reshape(
            tok_count, key_heads, head_dim
        )
    )
    values = filtered[:, 2 * key_heads * head_dim :].reshape(tok_count, value_heads, head_dim)
    queries = jnp.repeat(queries, ratio, axis=1)
    keys = jnp.repeat(keys, ratio, axis=1)
    strength = jax.nn.sigmoid(gating[:, :value_heads]).T
    log_decay = (-jnp.exp(decay_log) * jax.nn.softplus(gating[:, value_heads:] + decay_bias)).T
    cumulative = jnp.cumsum(log_decay, axis=1)
    positions = jnp.arange(tok_count)
    lower_incl = positions[:, None] >= positions[None, :]
    lower_strict = positions[:, None] > positions[None, :]
    spread = cumulative[:, :, None] - cumulative[:, None, :]
    decay_mat = jnp.where(lower_incl, jnp.exp(jnp.where(lower_incl, spread, 0.0)), 0.0)
    key_major = keys.transpose(1, 0, 2)
    query_leading = queries.transpose(1, 0, 2)
    value_major = values.transpose(1, 0, 2)
    key_inner = jnp.einsum("htd,hid->hti", key_major, key_major, precision=lax.Precision.HIGHEST)
    lower_part = jnp.where(lower_strict, decay_mat * key_inner, 0.0) * strength[:, :, None]
    system = lower_part + jnp.eye(tok_count, dtype=jnp.float32)
    growth = jnp.exp(cumulative)
    scaled_keys = key_major * (strength * growth)[:, :, None]
    scaled_values = value_major * strength[:, :, None]
    inverse = unit_lower_inverse(system)
    key_resolved = jnp.einsum(
        "hts,hsd->htd", inverse, scaled_keys, precision=lax.Precision.HIGHEST
    )
    value_resolved = jnp.einsum(
        "hts,hsd->htd", inverse, scaled_values, precision=lax.Precision.HIGHEST
    )
    tail = jnp.exp(cumulative[:, -1:] - cumulative)
    trailing_keys = key_major * tail[:, :, None]
    eye_heads = jnp.broadcast_to(
        jnp.eye(head_dim, dtype=jnp.float32), (value_heads, head_dim, head_dim)
    )
    state_map = growth[:, -1][:, None, None] * eye_heads - jnp.einsum(
        "htk,htj->hkj", trailing_keys, key_resolved, precision=lax.Precision.HIGHEST
    )
    state_increment = jnp.einsum(
        "xbe,xbz->xez", trailing_keys, value_resolved, precision=lax.Precision.HIGHEST
    )
    identity = (eye_heads, jnp.zeros_like(state_increment))
    inner_pre = prefix_2((state_map, state_increment), "inner", join_maps, identity)
    inclusive = join_maps(inner_pre, (state_map, state_increment))
    group = spread_2(shortened(jnp.stack(inclusive)), "inner", n_inner - 1)
    outer_pre = entering((group[0], group[1]), "outer", join_maps, identity)
    prefix = join_maps(outer_pre, inner_pre)
    initial_state = prefix[1]
    updates = value_resolved - jnp.einsum(
        "mwx,mxd->mwd", key_resolved, initial_state, precision=lax.Precision.HIGHEST
    )
    query_key = (
        jnp.einsum("htd,hid->hti", query_leading, key_major, precision=lax.Precision.HIGHEST)
        * decay_mat
    )
    carried = (
        jnp.einsum("mwx,mxd->mwd", query_leading, initial_state, precision=lax.Precision.HIGHEST)
        * growth[:, :, None]
    )
    attended = carried + jnp.einsum(
        "hti,hiv->htv", query_key, updates, precision=lax.Precision.HIGHEST
    )
    attended = attended.transpose(1, 0, 2)
    core_out = (
        rms_scale(attended, output_gain)
        .astype(jnp.bfloat16)
        .reshape(tok_count, value_heads * head_dim)
    )
    return (hidden_out, core_out)


def solution(mesh):
    return jax.shard_map(
        per_device,
        mesh=mesh,
        in_specs=(
            P(("outer", "inner"), None),
            P(("outer", "inner"), None),
            P(("outer", "inner"), None),
            P(),
            P(("outer", "inner"), None, None),
            P(("outer", "inner"), None, None),
            P(("outer", "inner"), None, None),
            P(),
            P(None, "inner"),
            P(),
            P(),
            P(),
            P(),
            P(),
        ),
        out_specs=(P(("outer", "inner"), None), P(("outer", "inner"), None)),
        check_vma=False,
    )
```

```python
import jax
import jax.numpy as jnp
from jax import lax
from jax.sharding import PartitionSpec as P


def shifted(value, axis, steps):
    count = lax.axis_size(axis)
    leading, last = (max(0, -steps), min(count, count - steps))
    return lax.ppermute(value, axis, [(source, source + steps) for source in range(leading, last)])


def prefix_2(x, axis, join, neutral):
    place = lax.axis_index(axis)
    gathered = jax.tree.map(
        lambda a, kind: lax.all_gather(a.astype(kind), axis), x, (jnp.bfloat16, jnp.bfloat16)
    )
    state = jax.tree.map(lambda a, e: jnp.zeros_like(a) + jnp.asarray(e, a.dtype), x, neutral)

    def one(lap, state):
        return join(
            state,
            jax.tree.map(
                lambda a, own: lax.dynamic_index_in_dim(a, lap, 0, False).astype(own.dtype),
                gathered,
                x,
            ),
        )

    return lax.fori_loop(0, place, one, state)


def shortened(x):

    def short(part):
        return part.astype(jnp.bfloat16) if part.dtype == jnp.float32 else part

    return jax.tree.map(short, x)


def spread_2(value, axis, source):
    kept = jnp.where(lax.axis_index(axis) == source, value, 0).astype(value.dtype)
    return lax.psum(kept, axis)


def entering(x, axis, combine, identity):
    length, place = (lax.axis_size(axis), lax.axis_index(axis))
    everything = jax.tree.map(
        lambda part, kind: lax.all_gather(part.astype(kind), axis),
        x,
        jax.tree.map(lambda a: jnp.bfloat16 if a.dtype == jnp.float32 else a.dtype, x),
    )
    start = jax.tree.map(
        lambda part, zero: jnp.broadcast_to(jnp.asarray(zero, part.dtype), part.shape), x, identity
    )

    def lap(k, before):
        reached = k < place
        new = combine(
            before, jax.tree.map(lambda part, own: part[k].astype(own.dtype), everything, x)
        )
        return jax.tree.map(lambda a, b: jnp.where(reached, a, b), new, before)

    return lax.fori_loop(0, length, lap, start)


def rms_scale(values, gain):
    wide = values.astype(jnp.float32)
    return wide * lax.rsqrt(jnp.mean(wide * wide, axis=-1, keepdims=True) + 1e-06) * gain


def unit_heads(values):
    return values * lax.rsqrt(jnp.sum(values * values, axis=-1, keepdims=True) + 1e-06)


def run_experts(piece, gate_weight, up_weight, down_weight):
    gate = jnp.einsum("esd,edf->esf", piece, gate_weight, preferred_element_type=jnp.float32)
    upper = jnp.einsum("esd,edf->esf", piece, up_weight, preferred_element_type=jnp.float32)
    hidden = (jax.nn.silu(gate) * upper).astype(jnp.bfloat16)
    return jnp.einsum(
        "esf,efd->esd", hidden, down_weight, preferred_element_type=jnp.float32
    ).astype(jnp.bfloat16)


def unit_lower_inverse(system):
    size = system.shape[-1]
    if size == 1:
        return jnp.ones_like(system)
    half = size // 2
    both = unit_lower_inverse(jnp.stack([system[..., :half, :half], system[..., half:, half:]]))
    first, second = both[0], both[1]
    corner = -jnp.einsum(
        "...ij,...jk->...ik",
        second,
        jnp.einsum("...ij,...jk->...ik", system[..., half:, :half], first, precision=lax.Precision.HIGHEST),
        precision=lax.Precision.HIGHEST,
    )
    top = jnp.concatenate([first, jnp.zeros_like(first)], axis=-1)
    bottom = jnp.concatenate([corner, second], axis=-1)
    return jnp.concatenate([top, bottom], axis=-2)


def join_maps(earlier, later):
    first_map, first_state = earlier
    next_map, next_state = later
    joined_map = jnp.einsum("hij,hjk->hik", next_map, first_map, precision=lax.Precision.HIGHEST)
    joined_state = (
        jnp.einsum("hij,hjv->hiv", next_map, first_state, precision=lax.Precision.HIGHEST)
        + next_state
    )
    return (joined_map, joined_state)


def shifted_linear(value, axes, count, steps):
    return lax.ppermute(value, axes, [(source, source + steps) for source in range(count - steps)])


def chained_state(state_map, state_increment, axes, count):
    place = lax.axis_index(axes)
    steps = 1
    while steps < count:
        last = steps * 2 >= count
        far_state = shifted_linear(state_increment.astype(jnp.bfloat16), axes, count, steps)
        reached = place >= steps
        joined_state = (
            jnp.einsum(
                "hij,hjv->hiv", state_map, far_state.astype(jnp.float32), precision=lax.Precision.HIGHEST
            )
            + state_increment
        )
        if not last:
            far_map = shifted_linear(state_map.astype(jnp.bfloat16), axes, count, steps)
            joined_map = jnp.einsum(
                "hij,hjk->hik", state_map, far_map.astype(jnp.float32), precision=lax.Precision.HIGHEST
            )
            state_map = jnp.where(reached, joined_map, state_map)
        state_increment = jnp.where(reached, joined_state, state_increment)
        steps *= 2
    return shifted_linear(state_increment.astype(jnp.bfloat16), axes, count, 1).astype(jnp.float32)


def per_device(
    tokens_in,
    expert_ids,
    route_weight,
    first_gain,
    gate_weight,
    up_weight,
    down_weight,
    second_gain,
    mixer_weight,
    gating_weight,
    filter_taps,
    decay_log,
    decay_bias,
    output_gain,
):
    n_outer = lax.axis_size("outer")
    n_inner = lax.axis_size("inner")
    n_dev = n_outer * n_inner
    tok_count, width = tokens_in.shape
    top_count = expert_ids.shape[1]
    local_experts = gate_weight.shape[0]
    experts_all = local_experts * n_dev
    capacity = max(2, 6 * tok_count * top_count // (5 * experts_all))
    normed_first = rms_scale(tokens_in, first_gain).astype(jnp.bfloat16)
    mix_weight = route_weight / jnp.sum(route_weight, axis=1, keepdims=True)
    flat_ids = expert_ids
    target = (
        flat_ids % local_experts * (n_dev * capacity)
        + flat_ids // local_experts * capacity
    )
    onehot = (flat_ids[:, :, None] == jnp.arange(experts_all, dtype=jnp.int32)[None, None, :]).astype(
        jnp.int32
    )
    counted = jnp.sum(onehot, axis=1)
    before = jnp.cumsum(counted, axis=0) - counted
    slot_index = jnp.sum(before[:, None, :] * onehot, axis=2)
    target = target + slot_index
    slots = jnp.arange(n_dev * local_experts * capacity, dtype=jnp.int32)
    hits = target[:, :, None] == slots[None, None, :]
    dispatch = jnp.any(hits, axis=1).astype(jnp.bfloat16)
    outgoing = jnp.einsum(
        "ts,td->sd", dispatch, normed_first, preferred_element_type=jnp.float32
    ).astype(jnp.bfloat16)
    outgoing = outgoing.reshape(local_experts, n_dev * capacity, width)
    served = run_experts(
        lax.all_to_all(outgoing, ("outer", "inner"), split_axis=1, concat_axis=1, tiled=True),
        gate_weight,
        up_weight,
        down_weight,
    )
    returned = lax.all_to_all(served, ("outer", "inner"), split_axis=1, concat_axis=1, tiled=True)
    returned = returned.reshape(-1, width)
    combine = jnp.sum(jnp.where(hits, mix_weight[:, :, None], 0.0), axis=1)
    combine_hi = combine.astype(jnp.bfloat16)
    combine_lo = (combine - combine_hi.astype(jnp.float32)).astype(jnp.bfloat16)
    mixture = jnp.dot(combine_hi, returned, preferred_element_type=jnp.float32) + jnp.dot(
        combine_lo, returned, preferred_element_type=jnp.float32
    )
    hidden_out = (tokens_in.astype(jnp.float32) + mixture).astype(jnp.bfloat16)
    normed_second = rms_scale(hidden_out, second_gain).astype(jnp.bfloat16)
    mixed = jnp.dot(
        normed_second,
        lax.all_gather(mixer_weight, "inner", axis=1, tiled=True),
        preferred_element_type=jnp.float32,
    )
    projected = mixed.astype(jnp.bfloat16)
    gating = jnp.dot(normed_second, gating_weight, preferred_element_type=jnp.float32)
    taps = filter_taps.shape[0]
    rim = shifted(projected[tok_count - (taps - 1) :], ("outer", "inner"), 1)
    padded = jnp.concatenate([rim, projected], axis=0).astype(jnp.float32)
    filtered = jnp.zeros(projected.shape, jnp.float32)
    for tap_index in range(taps):
        filtered = (
            filtered
            + filter_taps[tap_index].astype(jnp.float32) * padded[tap_index : tap_index + tok_count]
        )
    filtered = jax.nn.silu(filtered)
    head_dim = output_gain.shape[0]
    value_heads = decay_log.shape[0]
    key_heads = (projected.shape[1] - value_heads * head_dim) // (2 * head_dim)
    ratio = value_heads // key_heads
    queries = unit_heads(
        filtered[:, : key_heads * head_dim].reshape(tok_count, key_heads, head_dim)
    ) * head_dim ** (-0.5)
    keys = unit_heads(
        filtered[:, key_heads * head_dim : 2 * key_heads * head_dim].reshape(
            tok_count, key_heads, head_dim
        )
    )
    values = filtered[:, 2 * key_heads * head_dim :].reshape(tok_count, value_heads, head_dim)
    queries = jnp.repeat(queries, ratio, axis=1)
    keys = jnp.repeat(keys, ratio, axis=1)
    strength = jax.nn.sigmoid(gating[:, :value_heads]).T
    log_decay = (-jnp.exp(decay_log) * jax.nn.softplus(gating[:, value_heads:] + decay_bias)).T
    cumulative = jnp.cumsum(log_decay, axis=1)
    positions = jnp.arange(tok_count)
    lower_incl = positions[:, None] >= positions[None, :]
    lower_strict = positions[:, None] > positions[None, :]
    spread = cumulative[:, :, None] - cumulative[:, None, :]
    decay_mat = jnp.where(lower_incl, jnp.exp(jnp.where(lower_incl, spread, 0.0)), 0.0)
    key_major = keys.transpose(1, 0, 2)
    query_leading = queries.transpose(1, 0, 2)
    value_major = values.transpose(1, 0, 2)
    key_inner = jnp.einsum("htd,hid->hti", key_major, key_major, precision=lax.Precision.HIGHEST)
    lower_part = jnp.where(lower_strict, decay_mat * key_inner, 0.0) * strength[:, :, None]
    system = lower_part + jnp.eye(tok_count, dtype=jnp.float32)
    growth = jnp.exp(cumulative)
    scaled_keys = key_major * (strength * growth)[:, :, None]
    scaled_values = value_major * strength[:, :, None]
    inverse = unit_lower_inverse(system)
    key_resolved = jnp.einsum(
        "hts,hsd->htd", inverse, scaled_keys, precision=lax.Precision.HIGHEST
    )
    value_resolved = jnp.einsum(
        "hts,hsd->htd", inverse, scaled_values, precision=lax.Precision.HIGHEST
    )
    tail = jnp.exp(cumulative[:, -1:] - cumulative)
    trailing_keys = key_major * tail[:, :, None]
    eye_heads = jnp.broadcast_to(
        jnp.eye(head_dim, dtype=jnp.float32), (value_heads, head_dim, head_dim)
    )
    state_map = growth[:, -1][:, None, None] * eye_heads - jnp.einsum(
        "htk,htj->hkj", trailing_keys, key_resolved, precision=lax.Precision.HIGHEST
    )
    state_increment = jnp.einsum(
        "xbe,xbz->xez", trailing_keys, value_resolved, precision=lax.Precision.HIGHEST
    )
    initial_state = chained_state(state_map, state_increment, ("outer", "inner"), n_dev)
    updates = value_resolved - jnp.einsum(
        "mwx,mxd->mwd", key_resolved, initial_state, precision=lax.Precision.HIGHEST
    )
    query_key = (
        jnp.einsum("htd,hid->hti", query_leading, key_major, precision=lax.Precision.HIGHEST)
        * decay_mat
    )
    carried = (
        jnp.einsum("mwx,mxd->mwd", query_leading, initial_state, precision=lax.Precision.HIGHEST)
        * growth[:, :, None]
    )
    attended = carried + jnp.einsum(
        "hti,hiv->htv", query_key, updates, precision=lax.Precision.HIGHEST
    )
    attended = attended.transpose(1, 0, 2)
    core_out = (
        rms_scale(attended, output_gain)
        .astype(jnp.bfloat16)
        .reshape(tok_count, value_heads * head_dim)
    )
    return (hidden_out, core_out)


def solution(mesh):
    return jax.shard_map(
        per_device,
        mesh=mesh,
        in_specs=(
            P(("outer", "inner"), None),
            P(("outer", "inner"), None),
            P(("outer", "inner"), None),
            P(),
            P(("outer", "inner"), None, None),
            P(("outer", "inner"), None, None),
            P(("outer", "inner"), None, None),
            P(),
            P(None, "inner"),
            P(),
            P(),
            P(),
            P(),
            P(),
        ),
        out_specs=(P(("outer", "inner"), None), P(("outer", "inner"), None)),
        check_vma=False,
    )
```

```python
import jax
import jax.numpy as jnp
from jax import lax
from jax.sharding import PartitionSpec as P


def shifted(value, axis, steps):
    count = lax.axis_size(axis)
    leading, last = (max(0, -steps), min(count, count - steps))
    return lax.ppermute(value, axis, [(source, source + steps) for source in range(leading, last)])


def prefix_2(x, axis, join, neutral):
    place = lax.axis_index(axis)
    gathered = jax.tree.map(
        lambda a, kind: lax.all_gather(a.astype(kind), axis), x, (jnp.bfloat16, jnp.bfloat16)
    )
    state = jax.tree.map(lambda a, e: jnp.zeros_like(a) + jnp.asarray(e, a.dtype), x, neutral)

    def one(lap, state):
        return join(
            state,
            jax.tree.map(
                lambda a, own: lax.dynamic_index_in_dim(a, lap, 0, False).astype(own.dtype),
                gathered,
                x,
            ),
        )

    return lax.fori_loop(0, place, one, state)


def shortened(x):

    def short(part):
        return part.astype(jnp.bfloat16) if part.dtype == jnp.float32 else part

    return jax.tree.map(short, x)


def spread_2(value, axis, source):
    kept = jnp.where(lax.axis_index(axis) == source, value, 0).astype(value.dtype)
    return lax.psum(kept, axis)


def entering(x, axis, combine, identity):
    length, place = (lax.axis_size(axis), lax.axis_index(axis))
    everything = jax.tree.map(
        lambda part, kind: lax.all_gather(part.astype(kind), axis),
        x,
        jax.tree.map(lambda a: jnp.bfloat16 if a.dtype == jnp.float32 else a.dtype, x),
    )
    start = jax.tree.map(
        lambda part, zero: jnp.broadcast_to(jnp.asarray(zero, part.dtype), part.shape), x, identity
    )

    def lap(k, before):
        reached = k < place
        new = combine(
            before, jax.tree.map(lambda part, own: part[k].astype(own.dtype), everything, x)
        )
        return jax.tree.map(lambda a, b: jnp.where(reached, a, b), new, before)

    return lax.fori_loop(0, length, lap, start)


def rms_scale(values, gain):
    wide = values.astype(jnp.float32)
    return wide * lax.rsqrt(jnp.mean(wide * wide, axis=-1, keepdims=True) + 1e-06) * gain


def unit_heads(values):
    return values * lax.rsqrt(jnp.sum(values * values, axis=-1, keepdims=True) + 1e-06)


def run_experts(piece, gate_weight, up_weight, down_weight):
    gate = jnp.einsum("sed,edf->esf", piece, gate_weight, preferred_element_type=jnp.float32)
    upper = jnp.einsum("sed,edf->esf", piece, up_weight, preferred_element_type=jnp.float32)
    hidden = (jax.nn.silu(gate) * upper).astype(jnp.bfloat16)
    return jnp.einsum(
        "esf,efd->sed", hidden, down_weight, preferred_element_type=jnp.float32
    ).astype(jnp.bfloat16)


def unit_lower_inverse(system):
    size = system.shape[-1]
    if size == 1:
        return jnp.ones_like(system)
    half = size // 2
    both = unit_lower_inverse(jnp.stack([system[..., :half, :half], system[..., half:, half:]]))
    first, second = both[0], both[1]
    corner = -jnp.einsum(
        "...ij,...jk->...ik",
        second,
        jnp.einsum("...ij,...jk->...ik", system[..., half:, :half], first, precision=lax.Precision.HIGHEST),
        precision=lax.Precision.HIGHEST,
    )
    top = jnp.concatenate([first, jnp.zeros_like(first)], axis=-1)
    bottom = jnp.concatenate([corner, second], axis=-1)
    return jnp.concatenate([top, bottom], axis=-2)


def join_maps(earlier, later):
    first_map, first_state = earlier
    next_map, next_state = later
    joined_map = jnp.einsum("hij,hjk->hik", next_map, first_map, precision=lax.Precision.HIGHEST)
    joined_state = (
        jnp.einsum("hij,hjv->hiv", next_map, first_state, precision=lax.Precision.HIGHEST)
        + next_state
    )
    return (joined_map, joined_state)


def shifted_linear(value, axes, count, steps):
    return lax.ppermute(value, axes, [(source, source + steps) for source in range(count - steps)])


def chained_state(state_map, state_increment, axes, count):
    place = lax.axis_index(axes)
    steps = 1
    while steps < count:
        reached = place >= steps
        if steps * 2 >= count:
            far_state = shifted_linear(state_increment.astype(jnp.bfloat16), axes, count, steps)
        else:
            far = shifted_linear(
                jnp.stack([state_map, state_increment]).astype(jnp.bfloat16), axes, count, steps
            ).astype(jnp.float32)
            far_state = far[1]
            joined_map = jnp.einsum(
                "hij,hjk->hik", state_map, far[0], precision=lax.Precision.HIGHEST
            )
        joined_state = (
            jnp.einsum(
                "hij,hjv->hiv", state_map, far_state.astype(jnp.float32), precision=lax.Precision.HIGHEST
            )
            + state_increment
        )
        if steps * 2 < count:
            state_map = jnp.where(reached, joined_map, state_map)
        state_increment = jnp.where(reached, joined_state, state_increment)
        steps *= 2
    return shifted_linear(state_increment.astype(jnp.bfloat16), axes, count, 1).astype(jnp.float32)


def per_device(
    tokens_in,
    expert_ids,
    route_weight,
    first_gain,
    gate_weight,
    up_weight,
    down_weight,
    second_gain,
    mixer_weight,
    gating_weight,
    filter_taps,
    decay_log,
    decay_bias,
    output_gain,
):
    n_outer = lax.axis_size("outer")
    n_inner = lax.axis_size("inner")
    n_dev = n_outer * n_inner
    tok_count, width = tokens_in.shape
    top_count = expert_ids.shape[1]
    local_experts = gate_weight.shape[0]
    experts_all = local_experts * n_dev
    capacity = max(2, 6 * tok_count * top_count // (5 * experts_all))
    normed_first = rms_scale(tokens_in, first_gain).astype(jnp.bfloat16)
    mix_weight = route_weight / jnp.sum(route_weight, axis=1, keepdims=True)
    flat_ids = expert_ids
    target = flat_ids // local_experts * (capacity * local_experts) + flat_ids % local_experts
    onehot = (flat_ids[:, :, None] == jnp.arange(experts_all, dtype=jnp.int32)[None, None, :]).astype(
        jnp.int32
    )
    counted = jnp.sum(onehot, axis=1)
    before = jnp.cumsum(counted, axis=0) - counted
    slot_index = jnp.sum(before[:, None, :] * onehot, axis=2)
    target = target + slot_index * local_experts
    slots = jnp.arange(n_dev * local_experts * capacity, dtype=jnp.int32)
    hits = target[:, :, None] == slots[None, None, :]
    dispatch = jnp.any(hits, axis=1).astype(jnp.bfloat16)
    outgoing = jnp.einsum(
        "ts,td->sd", dispatch, normed_first, preferred_element_type=jnp.float32
    ).astype(jnp.bfloat16)
    outgoing = outgoing.reshape(n_dev * capacity, local_experts, width)
    served = run_experts(
        lax.all_to_all(outgoing, ("outer", "inner"), split_axis=0, concat_axis=0, tiled=True),
        gate_weight,
        up_weight,
        down_weight,
    )
    returned = lax.all_to_all(served, ("outer", "inner"), split_axis=0, concat_axis=0, tiled=True)
    returned = returned.reshape(-1, width)
    combine = jnp.sum(jnp.where(hits, mix_weight[:, :, None], 0.0), axis=1)
    combine_hi = combine.astype(jnp.bfloat16)
    combine_lo = (combine - combine_hi.astype(jnp.float32)).astype(jnp.bfloat16)
    mixture = jnp.dot(combine_hi, returned, preferred_element_type=jnp.float32) + jnp.dot(
        combine_lo, returned, preferred_element_type=jnp.float32
    )
    hidden_out = (tokens_in.astype(jnp.float32) + mixture).astype(jnp.bfloat16)
    normed_second = rms_scale(hidden_out, second_gain).astype(jnp.bfloat16)
    mixed = jnp.dot(
        normed_second,
        lax.all_gather(mixer_weight, "inner", axis=1, tiled=True),
        preferred_element_type=jnp.float32,
    )
    projected = mixed.astype(jnp.bfloat16)
    gating = jnp.dot(normed_second, gating_weight, preferred_element_type=jnp.float32)
    taps = filter_taps.shape[0]
    rim = shifted(projected[tok_count - (taps - 1) :], ("outer", "inner"), 1)
    padded = jnp.concatenate([rim, projected], axis=0).astype(jnp.float32)
    filtered = jnp.zeros(projected.shape, jnp.float32)
    for tap_index in range(taps):
        filtered = (
            filtered
            + filter_taps[tap_index].astype(jnp.float32) * padded[tap_index : tap_index + tok_count]
        )
    filtered = jax.nn.silu(filtered)
    head_dim = output_gain.shape[0]
    value_heads = decay_log.shape[0]
    key_heads = (projected.shape[1] - value_heads * head_dim) // (2 * head_dim)
    ratio = value_heads // key_heads
    queries = unit_heads(
        filtered[:, : key_heads * head_dim].reshape(tok_count, key_heads, head_dim)
    ) * head_dim ** (-0.5)
    keys = unit_heads(
        filtered[:, key_heads * head_dim : 2 * key_heads * head_dim].reshape(
            tok_count, key_heads, head_dim
        )
    )
    values = filtered[:, 2 * key_heads * head_dim :].reshape(tok_count, value_heads, head_dim)
    queries = jnp.repeat(queries, ratio, axis=1)
    keys = jnp.repeat(keys, ratio, axis=1)
    strength = jax.nn.sigmoid(gating[:, :value_heads]).T
    log_decay = (-jnp.exp(decay_log) * jax.nn.softplus(gating[:, value_heads:] + decay_bias)).T
    cumulative = jnp.cumsum(log_decay, axis=1)
    positions = jnp.arange(tok_count)
    lower_incl = positions[:, None] >= positions[None, :]
    lower_strict = positions[:, None] > positions[None, :]
    spread = cumulative[:, :, None] - cumulative[:, None, :]
    decay_mat = jnp.where(lower_incl, jnp.exp(jnp.where(lower_incl, spread, 0.0)), 0.0)
    key_major = keys.transpose(1, 0, 2)
    query_leading = queries.transpose(1, 0, 2)
    value_major = values.transpose(1, 0, 2)
    key_inner = jnp.einsum("htd,hid->hti", key_major, key_major, precision=lax.Precision.HIGHEST)
    lower_part = jnp.where(lower_strict, decay_mat * key_inner, 0.0) * strength[:, :, None]
    system = lower_part + jnp.eye(tok_count, dtype=jnp.float32)
    growth = jnp.exp(cumulative)
    scaled_keys = key_major * (strength * growth)[:, :, None]
    scaled_values = value_major * strength[:, :, None]
    inverse = unit_lower_inverse(system)
    key_resolved = jnp.einsum(
        "hts,hsd->htd", inverse, scaled_keys, precision=lax.Precision.HIGHEST
    )
    value_resolved = jnp.einsum(
        "hts,hsd->htd", inverse, scaled_values, precision=lax.Precision.HIGHEST
    )
    tail = jnp.exp(cumulative[:, -1:] - cumulative)
    trailing_keys = key_major * tail[:, :, None]
    eye_heads = jnp.broadcast_to(
        jnp.eye(head_dim, dtype=jnp.float32), (value_heads, head_dim, head_dim)
    )
    state_map = growth[:, -1][:, None, None] * eye_heads - jnp.einsum(
        "htk,htj->hkj", trailing_keys, key_resolved, precision=lax.Precision.HIGHEST
    )
    state_increment = jnp.einsum(
        "xbe,xbz->xez", trailing_keys, value_resolved, precision=lax.Precision.HIGHEST
    )
    initial_state = chained_state(state_map, state_increment, ("outer", "inner"), n_dev)
    updates = value_resolved - jnp.einsum(
        "mwx,mxd->mwd", key_resolved, initial_state, precision=lax.Precision.HIGHEST
    )
    query_key = (
        jnp.einsum("htd,hid->hti", query_leading, key_major, precision=lax.Precision.HIGHEST)
        * decay_mat
    )
    carried = (
        jnp.einsum("mwx,mxd->mwd", query_leading, initial_state, precision=lax.Precision.HIGHEST)
        * growth[:, :, None]
    )
    attended = carried + jnp.einsum(
        "hti,hiv->htv", query_key, updates, precision=lax.Precision.HIGHEST
    )
    attended = attended.transpose(1, 0, 2)
    core_out = (
        rms_scale(attended, output_gain)
        .astype(jnp.bfloat16)
        .reshape(tok_count, value_heads * head_dim)
    )
    return (hidden_out, core_out)


def solution(mesh):
    return jax.shard_map(
        per_device,
        mesh=mesh,
        in_specs=(
            P(("outer", "inner"), None),
            P(("outer", "inner"), None),
            P(("outer", "inner"), None),
            P(),
            P(("outer", "inner"), None, None),
            P(("outer", "inner"), None, None),
            P(("outer", "inner"), None, None),
            P(),
            P(None, "inner"),
            P(),
            P(),
            P(),
            P(),
            P(),
        ),
        out_specs=(P(("outer", "inner"), None), P(("outer", "inner"), None)),
        check_vma=False,
    )
```

```python
import jax
import jax.numpy as jnp
from jax import lax
from jax.sharding import PartitionSpec as P
from jax.experimental import pallas as pl
from jax.experimental.pallas import tpu as pltpu
import functools


def shifted(value, axis, steps):
    count = lax.axis_size(axis)
    leading, last = (max(0, -steps), min(count, count - steps))
    return lax.ppermute(value, axis, [(source, source + steps) for source in range(leading, last)])


def prefix_2(x, axis, join, neutral):
    place = lax.axis_index(axis)
    gathered = jax.tree.map(
        lambda a, kind: lax.all_gather(a.astype(kind), axis), x, (jnp.bfloat16, jnp.bfloat16)
    )
    state = jax.tree.map(lambda a, e: jnp.zeros_like(a) + jnp.asarray(e, a.dtype), x, neutral)

    def one(lap, state):
        return join(
            state,
            jax.tree.map(
                lambda a, own: lax.dynamic_index_in_dim(a, lap, 0, False).astype(own.dtype),
                gathered,
                x,
            ),
        )

    return lax.fori_loop(0, place, one, state)


def shortened(x):

    def short(part):
        return part.astype(jnp.bfloat16) if part.dtype == jnp.float32 else part

    return jax.tree.map(short, x)


def spread_2(value, axis, source):
    kept = jnp.where(lax.axis_index(axis) == source, value, 0).astype(value.dtype)
    return lax.psum(kept, axis)


def entering(x, axis, combine, identity):
    length, place = (lax.axis_size(axis), lax.axis_index(axis))
    everything = jax.tree.map(
        lambda part, kind: lax.all_gather(part.astype(kind), axis),
        x,
        jax.tree.map(lambda a: jnp.bfloat16 if a.dtype == jnp.float32 else a.dtype, x),
    )
    start = jax.tree.map(
        lambda part, zero: jnp.broadcast_to(jnp.asarray(zero, part.dtype), part.shape), x, identity
    )

    def lap(k, before):
        reached = k < place
        new = combine(
            before, jax.tree.map(lambda part, own: part[k].astype(own.dtype), everything, x)
        )
        return jax.tree.map(lambda a, b: jnp.where(reached, a, b), new, before)

    return lax.fori_loop(0, length, lap, start)


def rms_scale(values, gain):
    wide = values.astype(jnp.float32)
    return wide * lax.rsqrt(jnp.mean(wide * wide, axis=-1, keepdims=True) + 1e-06) * gain


def unit_heads(values):
    return values * lax.rsqrt(jnp.sum(values * values, axis=-1, keepdims=True) + 1e-06)


def run_experts(piece, gate_weight, up_weight, down_weight):
    gate = jnp.einsum("esd,edf->esf", piece, gate_weight, preferred_element_type=jnp.float32)
    upper = jnp.einsum("esd,edf->esf", piece, up_weight, preferred_element_type=jnp.float32)
    hidden = (jax.nn.silu(gate) * upper).astype(jnp.bfloat16)
    return jnp.einsum(
        "esf,efd->esd", hidden, down_weight, preferred_element_type=jnp.float32
    ).astype(jnp.bfloat16)


def unit_lower_inverse(system):
    size = system.shape[-1]
    if size == 1:
        return jnp.ones_like(system)
    half = size // 2
    both = unit_lower_inverse(jnp.stack([system[..., :half, :half], system[..., half:, half:]]))
    first, second = both[0], both[1]
    corner = -jnp.einsum(
        "...ij,...jk->...ik",
        second,
        jnp.einsum("...ij,...jk->...ik", system[..., half:, :half], first, precision=lax.Precision.HIGHEST),
        precision=lax.Precision.HIGHEST,
    )
    top = jnp.concatenate([first, jnp.zeros_like(first)], axis=-1)
    bottom = jnp.concatenate([corner, second], axis=-1)
    return jnp.concatenate([top, bottom], axis=-2)


def join_maps(earlier, later):
    first_map, first_state = earlier
    next_map, next_state = later
    joined_map = jnp.einsum("hij,hjk->hik", next_map, first_map, precision=lax.Precision.HIGHEST)
    joined_state = (
        jnp.einsum("hij,hjv->hiv", next_map, first_state, precision=lax.Precision.HIGHEST)
        + next_state
    )
    return (joined_map, joined_state)


def shifted_linear(value, axes, count, steps):
    return lax.ppermute(value, axes, [(source, source + steps) for source in range(count - steps)])


def scan_kernel(count, axes, map_ref, state_ref, out_ref, own_map, own_state, send_map, send_state,
                land_map, land_state, send_sems, recv_sems):
    place = lax.axis_index(axes)
    heads = map_ref.shape[0]
    own_map[...] = map_ref[...]
    own_state[...] = state_ref[...]
    rounds = []
    steps = 1
    while steps < count:
        rounds.append(steps)
        steps *= 2
    rounds.append(1)
    total = len(rounds)

    def target(steps):
        other = place + steps
        return (other // lax.axis_size(axes[1]), other % lax.axis_size(axes[1]))

    for number, steps in enumerate(rounds):
        with_map = number < total - 2
        final = number == total - 1
        send_state[number] = own_state[...].astype(jnp.bfloat16)
        if with_map:
            send_map[number] = own_map[...].astype(jnp.bfloat16)
        copies = [
            pltpu.make_async_remote_copy(
                src_ref=send_state.at[number], dst_ref=land_state.at[number],
                send_sem=send_sems.at[2 * number], recv_sem=recv_sems.at[2 * number],
                device_id=target(steps), device_id_type=pl.DeviceIdType.MESH)
        ]
        if with_map:
            copies.append(
                pltpu.make_async_remote_copy(
                    src_ref=send_map.at[number], dst_ref=land_map.at[number],
                    send_sem=send_sems.at[2 * number + 1], recv_sem=recv_sems.at[2 * number + 1],
                    device_id=target(steps), device_id_type=pl.DeviceIdType.MESH)
            )

        @pl.when(place + steps < count)
        def _():
            for copy in copies:
                copy.start()

        @pl.when(place >= steps)
        def _():
            for copy in copies:
                copy.wait_recv()
            if final:
                out_ref[...] = land_state[number].astype(jnp.float32)
            else:
                def head(h, carry):
                    mine = own_map[h]
                    new_state = jnp.dot(mine, land_state[number, h].astype(jnp.float32),
                                        preferred_element_type=jnp.float32,
                                        precision=lax.Precision.HIGHEST) + own_state[h]
                    if with_map:
                        own_map[h] = jnp.dot(mine, land_map[number, h].astype(jnp.float32),
                                             preferred_element_type=jnp.float32,
                                             precision=lax.Precision.HIGHEST)
                    own_state[h] = new_state
                    return carry
                lax.fori_loop(0, heads, head, 0)

        if final:
            @pl.when(place < steps)
            def _():
                out_ref[...] = jnp.zeros_like(out_ref)

        @pl.when(place + steps < count)
        def _():
            for copy in copies:
                copy.wait_send()


def chained_state(state_map, state_increment, axes, count):
    heads, size, width = state_increment.shape
    rounds = 1
    while (1 << (rounds - 1)) < count:
        rounds += 1
    block = pltpu.VMEM((rounds, heads, size, width), jnp.bfloat16)
    return pl.pallas_call(
        functools.partial(scan_kernel, count, axes),
        out_shape=jax.ShapeDtypeStruct(state_increment.shape, jnp.float32),
        in_specs=[pl.BlockSpec(memory_space=pltpu.VMEM)] * 2,
        out_specs=pl.BlockSpec(memory_space=pltpu.VMEM),
        scratch_shapes=[
            pltpu.VMEM(state_map.shape, jnp.float32),
            pltpu.VMEM(state_increment.shape, jnp.float32),
            pltpu.VMEM((rounds, heads, size, size), jnp.bfloat16),
            block,
            pltpu.VMEM((rounds, heads, size, size), jnp.bfloat16),
            block,
            pltpu.SemaphoreType.DMA((2 * rounds,)),
            pltpu.SemaphoreType.DMA((2 * rounds,)),
        ],
        compiler_params=pltpu.CompilerParams(has_side_effects=True, vmem_limit_bytes=48 * 1024 * 1024),
    )(state_map, state_increment)


def per_device(
    tokens_in,
    expert_ids,
    route_weight,
    first_gain,
    gate_weight,
    up_weight,
    down_weight,
    second_gain,
    mixer_weight,
    gating_weight,
    filter_taps,
    decay_log,
    decay_bias,
    output_gain,
):
    n_outer = lax.axis_size("outer")
    n_inner = lax.axis_size("inner")
    n_dev = n_outer * n_inner
    tok_count, width = tokens_in.shape
    top_count = expert_ids.shape[1]
    local_experts = gate_weight.shape[0]
    experts_all = local_experts * n_dev
    capacity = max(2, 6 * tok_count * top_count // (5 * experts_all))
    normed_first = rms_scale(tokens_in, first_gain).astype(jnp.bfloat16)
    mix_weight = route_weight / jnp.sum(route_weight, axis=1, keepdims=True)
    flat_ids = expert_ids
    target = (
        flat_ids % local_experts * (n_dev * capacity)
        + flat_ids // local_experts * capacity
    )
    onehot = (flat_ids[:, :, None] == jnp.arange(experts_all, dtype=jnp.int32)[None, None, :]).astype(
        jnp.int32
    )
    counted = jnp.sum(onehot, axis=1)
    before = jnp.cumsum(counted, axis=0) - counted
    slot_index = jnp.sum(before[:, None, :] * onehot, axis=2)
    target = target + slot_index
    slots = jnp.arange(n_dev * local_experts * capacity, dtype=jnp.int32)
    hits = target[:, :, None] == slots[None, None, :]
    dispatch = jnp.any(hits, axis=1).astype(jnp.bfloat16)
    outgoing = jnp.einsum(
        "ts,td->sd", dispatch, normed_first, preferred_element_type=jnp.float32
    ).astype(jnp.bfloat16)
    outgoing = outgoing.reshape(local_experts, n_dev * capacity, width)
    served = run_experts(
        lax.all_to_all(outgoing, ("outer", "inner"), split_axis=1, concat_axis=1, tiled=True),
        gate_weight,
        up_weight,
        down_weight,
    )
    returned = lax.all_to_all(served, ("outer", "inner"), split_axis=1, concat_axis=1, tiled=True)
    returned = returned.reshape(-1, width)
    combine = jnp.sum(jnp.where(hits, mix_weight[:, :, None], 0.0), axis=1)
    combine_hi = combine.astype(jnp.bfloat16)
    combine_lo = (combine - combine_hi.astype(jnp.float32)).astype(jnp.bfloat16)
    mixture = jnp.dot(combine_hi, returned, preferred_element_type=jnp.float32) + jnp.dot(
        combine_lo, returned, preferred_element_type=jnp.float32
    )
    hidden_out = (tokens_in.astype(jnp.float32) + mixture).astype(jnp.bfloat16)
    normed_second = rms_scale(hidden_out, second_gain).astype(jnp.bfloat16)
    mixed = jnp.dot(
        normed_second,
        lax.all_gather(mixer_weight, "inner", axis=1, tiled=True),
        preferred_element_type=jnp.float32,
    )
    projected = mixed.astype(jnp.bfloat16)
    gating = jnp.dot(normed_second, gating_weight, preferred_element_type=jnp.float32)
    taps = filter_taps.shape[0]
    rim = shifted(projected[tok_count - (taps - 1) :], ("outer", "inner"), 1)
    padded = jnp.concatenate([rim, projected], axis=0).astype(jnp.float32)
    filtered = jnp.zeros(projected.shape, jnp.float32)
    for tap_index in range(taps):
        filtered = (
            filtered
            + filter_taps[tap_index].astype(jnp.float32) * padded[tap_index : tap_index + tok_count]
        )
    filtered = jax.nn.silu(filtered)
    head_dim = output_gain.shape[0]
    value_heads = decay_log.shape[0]
    key_heads = (projected.shape[1] - value_heads * head_dim) // (2 * head_dim)
    ratio = value_heads // key_heads
    queries = unit_heads(
        filtered[:, : key_heads * head_dim].reshape(tok_count, key_heads, head_dim)
    ) * head_dim ** (-0.5)
    keys = unit_heads(
        filtered[:, key_heads * head_dim : 2 * key_heads * head_dim].reshape(
            tok_count, key_heads, head_dim
        )
    )
    values = filtered[:, 2 * key_heads * head_dim :].reshape(tok_count, value_heads, head_dim)
    queries = jnp.repeat(queries, ratio, axis=1)
    keys = jnp.repeat(keys, ratio, axis=1)
    strength = jax.nn.sigmoid(gating[:, :value_heads]).T
    log_decay = (-jnp.exp(decay_log) * jax.nn.softplus(gating[:, value_heads:] + decay_bias)).T
    cumulative = jnp.cumsum(log_decay, axis=1)
    positions = jnp.arange(tok_count)
    lower_incl = positions[:, None] >= positions[None, :]
    lower_strict = positions[:, None] > positions[None, :]
    spread = cumulative[:, :, None] - cumulative[:, None, :]
    decay_mat = jnp.where(lower_incl, jnp.exp(jnp.where(lower_incl, spread, 0.0)), 0.0)
    key_major = keys.transpose(1, 0, 2)
    query_leading = queries.transpose(1, 0, 2)
    value_major = values.transpose(1, 0, 2)
    key_inner = jnp.einsum("htd,hid->hti", key_major, key_major, precision=lax.Precision.HIGHEST)
    lower_part = jnp.where(lower_strict, decay_mat * key_inner, 0.0) * strength[:, :, None]
    system = lower_part + jnp.eye(tok_count, dtype=jnp.float32)
    growth = jnp.exp(cumulative)
    scaled_keys = key_major * (strength * growth)[:, :, None]
    scaled_values = value_major * strength[:, :, None]
    inverse = unit_lower_inverse(system)
    key_resolved = jnp.einsum(
        "hts,hsd->htd", inverse, scaled_keys, precision=lax.Precision.HIGHEST
    )
    value_resolved = jnp.einsum(
        "hts,hsd->htd", inverse, scaled_values, precision=lax.Precision.HIGHEST
    )
    tail = jnp.exp(cumulative[:, -1:] - cumulative)
    trailing_keys = key_major * tail[:, :, None]
    eye_heads = jnp.broadcast_to(
        jnp.eye(head_dim, dtype=jnp.float32), (value_heads, head_dim, head_dim)
    )
    state_map = growth[:, -1][:, None, None] * eye_heads - jnp.einsum(
        "htk,htj->hkj", trailing_keys, key_resolved, precision=lax.Precision.HIGHEST
    )
    state_increment = jnp.einsum(
        "xbe,xbz->xez", trailing_keys, value_resolved, precision=lax.Precision.HIGHEST
    )
    initial_state = chained_state(state_map, state_increment, ("outer", "inner"), n_dev)
    updates = value_resolved - jnp.einsum(
        "mwx,mxd->mwd", key_resolved, initial_state, precision=lax.Precision.HIGHEST
    )
    query_key = (
        jnp.einsum("htd,hid->hti", query_leading, key_major, precision=lax.Precision.HIGHEST)
        * decay_mat
    )
    carried = (
        jnp.einsum("mwx,mxd->mwd", query_leading, initial_state, precision=lax.Precision.HIGHEST)
        * growth[:, :, None]
    )
    attended = carried + jnp.einsum(
        "hti,hiv->htv", query_key, updates, precision=lax.Precision.HIGHEST
    )
    attended = attended.transpose(1, 0, 2)
    core_out = (
        rms_scale(attended, output_gain)
        .astype(jnp.bfloat16)
        .reshape(tok_count, value_heads * head_dim)
    )
    return (hidden_out, core_out)


def solution(mesh):
    return jax.shard_map(
        per_device,
        mesh=mesh,
        in_specs=(
            P(("outer", "inner"), None),
            P(("outer", "inner"), None),
            P(("outer", "inner"), None),
            P(),
            P(("outer", "inner"), None, None),
            P(("outer", "inner"), None, None),
            P(("outer", "inner"), None, None),
            P(),
            P(None, "inner"),
            P(),
            P(),
            P(),
            P(),
            P(),
        ),
        out_specs=(P(("outer", "inner"), None), P(("outer", "inner"), None)),
        check_vma=False,
    )
```

```python
import jax
import jax.numpy as jnp
from jax import lax
from jax.sharding import PartitionSpec as P
from jax.experimental import pallas as pl
from jax.experimental.pallas import tpu as pltpu
import functools


def shifted(value, axis, steps):
    count = lax.axis_size(axis)
    leading, last = (max(0, -steps), min(count, count - steps))
    return lax.ppermute(value, axis, [(source, source + steps) for source in range(leading, last)])


def prefix_2(x, axis, join, neutral):
    place = lax.axis_index(axis)
    gathered = jax.tree.map(
        lambda a, kind: lax.all_gather(a.astype(kind), axis), x, (jnp.bfloat16, jnp.bfloat16)
    )
    state = jax.tree.map(lambda a, e: jnp.zeros_like(a) + jnp.asarray(e, a.dtype), x, neutral)

    def one(lap, state):
        return join(
            state,
            jax.tree.map(
                lambda a, own: lax.dynamic_index_in_dim(a, lap, 0, False).astype(own.dtype),
                gathered,
                x,
            ),
        )

    return lax.fori_loop(0, place, one, state)


def shortened(x):

    def short(part):
        return part.astype(jnp.bfloat16) if part.dtype == jnp.float32 else part

    return jax.tree.map(short, x)


def spread_2(value, axis, source):
    kept = jnp.where(lax.axis_index(axis) == source, value, 0).astype(value.dtype)
    return lax.psum(kept, axis)


def entering(x, axis, combine, identity):
    length, place = (lax.axis_size(axis), lax.axis_index(axis))
    everything = jax.tree.map(
        lambda part, kind: lax.all_gather(part.astype(kind), axis),
        x,
        jax.tree.map(lambda a: jnp.bfloat16 if a.dtype == jnp.float32 else a.dtype, x),
    )
    start = jax.tree.map(
        lambda part, zero: jnp.broadcast_to(jnp.asarray(zero, part.dtype), part.shape), x, identity
    )

    def lap(k, before):
        reached = k < place
        new = combine(
            before, jax.tree.map(lambda part, own: part[k].astype(own.dtype), everything, x)
        )
        return jax.tree.map(lambda a, b: jnp.where(reached, a, b), new, before)

    return lax.fori_loop(0, length, lap, start)


def rms_scale(values, gain):
    wide = values.astype(jnp.float32)
    return wide * lax.rsqrt(jnp.mean(wide * wide, axis=-1, keepdims=True) + 1e-06) * gain


def unit_heads(values):
    return values * lax.rsqrt(jnp.sum(values * values, axis=-1, keepdims=True) + 1e-06)


def run_experts(piece, gate_weight, up_weight, down_weight):
    gate = jnp.einsum("esd,edf->esf", piece, gate_weight, preferred_element_type=jnp.float32)
    upper = jnp.einsum("esd,edf->esf", piece, up_weight, preferred_element_type=jnp.float32)
    hidden = (jax.nn.silu(gate) * upper).astype(jnp.bfloat16)
    return jnp.einsum(
        "esf,efd->esd", hidden, down_weight, preferred_element_type=jnp.float32
    ).astype(jnp.bfloat16)


def unit_lower_inverse(system):
    size = system.shape[-1]
    if size == 1:
        return jnp.ones_like(system)
    half = size // 2
    both = unit_lower_inverse(jnp.stack([system[..., :half, :half], system[..., half:, half:]]))
    first, second = both[0], both[1]
    corner = -jnp.einsum(
        "...ij,...jk->...ik",
        second,
        jnp.einsum("...ij,...jk->...ik", system[..., half:, :half], first, precision=lax.Precision.HIGHEST),
        precision=lax.Precision.HIGHEST,
    )
    top = jnp.concatenate([first, jnp.zeros_like(first)], axis=-1)
    bottom = jnp.concatenate([corner, second], axis=-1)
    return jnp.concatenate([top, bottom], axis=-2)


def join_maps(earlier, later):
    first_map, first_state = earlier
    next_map, next_state = later
    joined_map = jnp.einsum("hij,hjk->hik", next_map, first_map, precision=lax.Precision.HIGHEST)
    joined_state = (
        jnp.einsum("hij,hjv->hiv", next_map, first_state, precision=lax.Precision.HIGHEST)
        + next_state
    )
    return (joined_map, joined_state)


def shifted_linear(value, axes, count, steps):
    return lax.ppermute(value, axes, [(source, source + steps) for source in range(count - steps)])


def scan_kernel(count, axes, groups, map_ref, state_ref, out_ref, own_map, own_state, send_map,
                send_state, land_map, land_state, send_sems, recv_sems):
    place = lax.axis_index(axes)
    span = map_ref.shape[0] // groups
    own_map[...] = map_ref[...]
    own_state[...] = state_ref[...]
    rounds = []
    steps = 1
    while steps < count:
        rounds.append(steps)
        steps *= 2
    rounds.append(1)
    total = len(rounds)
    inner = lax.axis_size(axes[1])

    def copies(number, group):
        other = place + rounds[number]
        heads = pl.ds(group * span, span)
        found = [
            pltpu.make_async_remote_copy(
                src_ref=send_state.at[number, heads], dst_ref=land_state.at[number, heads],
                send_sem=send_sems.at[number, group, 0], recv_sem=recv_sems.at[number, group, 0],
                device_id=(other // inner, other % inner), device_id_type=pl.DeviceIdType.MESH)
        ]
        if number < total - 2:
            found.append(
                pltpu.make_async_remote_copy(
                    src_ref=send_map.at[number, heads], dst_ref=land_map.at[number, heads],
                    send_sem=send_sems.at[number, group, 1], recv_sem=recv_sems.at[number, group, 1],
                    device_id=(other // inner, other % inner), device_id_type=pl.DeviceIdType.MESH)
            )
        return found

    def joined(number, group):
        def head(h, carry):
            mine = own_map[h]
            high = mine.astype(jnp.bfloat16)
            low = (mine - high.astype(jnp.float32)).astype(jnp.bfloat16)

            def apply(far):
                return jnp.dot(high, far, preferred_element_type=jnp.float32) + jnp.dot(
                    low, far, preferred_element_type=jnp.float32)

            own_state[h] = apply(land_state[number, h]) + own_state[h]
            if number < total - 2:
                own_map[h] = apply(land_map[number, h])
            return carry

        lax.fori_loop(group * span, group * span + span, head, 0)

    for number in range(total):
        for group in range(groups):
            heads = pl.ds(group * span, span)
            if number > 0:
                @pl.when(place >= rounds[number - 1])
                def _():
                    for copy in copies(number - 1, group):
                        copy.wait_recv()
                    joined(number - 1, group)
            send_state[number, heads] = own_state[heads].astype(jnp.bfloat16)
            if number < total - 2:
                send_map[number, heads] = own_map[heads].astype(jnp.bfloat16)

            @pl.when(place + rounds[number] < count)
            def _():
                for copy in copies(number, group):
                    copy.start()

    for group in range(groups):
        heads = pl.ds(group * span, span)

        @pl.when(place >= 1)
        def _():
            for copy in copies(total - 1, group):
                copy.wait_recv()
            out_ref[heads] = land_state[total - 1, heads].astype(jnp.float32)

        @pl.when(place < 1)
        def _():
            out_ref[heads] = jnp.zeros_like(out_ref[heads])

    for number in range(total):
        @pl.when(place + rounds[number] < count)
        def _():
            for group in range(groups):
                for copy in copies(number, group):
                    copy.wait_send()


def chained_state(state_map, state_increment, axes, count):
    heads, size, width = state_increment.shape
    rounds = 1
    while (1 << (rounds - 1)) < count:
        rounds += 1
    groups = 4
    block = pltpu.VMEM((rounds, heads, size, width), jnp.bfloat16)
    return pl.pallas_call(
        functools.partial(scan_kernel, count, axes, groups),
        out_shape=jax.ShapeDtypeStruct(state_increment.shape, jnp.float32),
        in_specs=[pl.BlockSpec(memory_space=pltpu.VMEM)] * 2,
        out_specs=pl.BlockSpec(memory_space=pltpu.VMEM),
        scratch_shapes=[
            pltpu.VMEM(state_map.shape, jnp.float32),
            pltpu.VMEM(state_increment.shape, jnp.float32),
            pltpu.VMEM((rounds, heads, size, size), jnp.bfloat16),
            block,
            pltpu.VMEM((rounds, heads, size, size), jnp.bfloat16),
            block,
            pltpu.SemaphoreType.DMA((rounds, groups, 2)),
            pltpu.SemaphoreType.DMA((rounds, groups, 2)),
        ],
        compiler_params=pltpu.CompilerParams(has_side_effects=True, vmem_limit_bytes=48 * 1024 * 1024),
    )(state_map, state_increment)


def per_device(
    tokens_in,
    expert_ids,
    route_weight,
    first_gain,
    gate_weight,
    up_weight,
    down_weight,
    second_gain,
    mixer_weight,
    gating_weight,
    filter_taps,
    decay_log,
    decay_bias,
    output_gain,
):
    n_outer = lax.axis_size("outer")
    n_inner = lax.axis_size("inner")
    n_dev = n_outer * n_inner
    tok_count, width = tokens_in.shape
    top_count = expert_ids.shape[1]
    local_experts = gate_weight.shape[0]
    experts_all = local_experts * n_dev
    capacity = max(2, 6 * tok_count * top_count // (5 * experts_all))
    normed_first = rms_scale(tokens_in, first_gain).astype(jnp.bfloat16)
    mix_weight = route_weight / jnp.sum(route_weight, axis=1, keepdims=True)
    flat_ids = expert_ids
    target = (
        flat_ids % local_experts * (n_dev * capacity)
        + flat_ids // local_experts * capacity
    )
    onehot = (flat_ids[:, :, None] == jnp.arange(experts_all, dtype=jnp.int32)[None, None, :]).astype(
        jnp.int32
    )
    counted = jnp.sum(onehot, axis=1)
    before = jnp.cumsum(counted, axis=0) - counted
    slot_index = jnp.sum(before[:, None, :] * onehot, axis=2)
    target = target + slot_index
    slots = jnp.arange(n_dev * local_experts * capacity, dtype=jnp.int32)
    hits = target[:, :, None] == slots[None, None, :]
    dispatch = jnp.any(hits, axis=1).astype(jnp.bfloat16)
    outgoing = jnp.einsum(
        "ts,td->sd", dispatch, normed_first, preferred_element_type=jnp.float32
    ).astype(jnp.bfloat16)
    outgoing = outgoing.reshape(local_experts, n_dev * capacity, width)
    served = run_experts(
        lax.all_to_all(outgoing, ("outer", "inner"), split_axis=1, concat_axis=1, tiled=True),
        gate_weight,
        up_weight,
        down_weight,
    )
    returned = lax.all_to_all(served, ("outer", "inner"), split_axis=1, concat_axis=1, tiled=True)
    returned = returned.reshape(-1, width)
    combine = jnp.sum(jnp.where(hits, mix_weight[:, :, None], 0.0), axis=1)
    combine_hi = combine.astype(jnp.bfloat16)
    combine_lo = (combine - combine_hi.astype(jnp.float32)).astype(jnp.bfloat16)
    mixture = jnp.dot(combine_hi, returned, preferred_element_type=jnp.float32) + jnp.dot(
        combine_lo, returned, preferred_element_type=jnp.float32
    )
    hidden_out = (tokens_in.astype(jnp.float32) + mixture).astype(jnp.bfloat16)
    normed_second = rms_scale(hidden_out, second_gain).astype(jnp.bfloat16)
    mixed = jnp.dot(
        normed_second,
        lax.all_gather(mixer_weight, "inner", axis=1, tiled=True),
        preferred_element_type=jnp.float32,
    )
    projected = mixed.astype(jnp.bfloat16)
    gating = jnp.dot(normed_second, gating_weight, preferred_element_type=jnp.float32)
    taps = filter_taps.shape[0]
    rim = shifted(projected[tok_count - (taps - 1) :], ("outer", "inner"), 1)
    padded = jnp.concatenate([rim, projected], axis=0).astype(jnp.float32)
    filtered = jnp.zeros(projected.shape, jnp.float32)
    for tap_index in range(taps):
        filtered = (
            filtered
            + filter_taps[tap_index].astype(jnp.float32) * padded[tap_index : tap_index + tok_count]
        )
    filtered = jax.nn.silu(filtered)
    head_dim = output_gain.shape[0]
    value_heads = decay_log.shape[0]
    key_heads = (projected.shape[1] - value_heads * head_dim) // (2 * head_dim)
    ratio = value_heads // key_heads
    queries = unit_heads(
        filtered[:, : key_heads * head_dim].reshape(tok_count, key_heads, head_dim)
    ) * head_dim ** (-0.5)
    keys = unit_heads(
        filtered[:, key_heads * head_dim : 2 * key_heads * head_dim].reshape(
            tok_count, key_heads, head_dim
        )
    )
    values = filtered[:, 2 * key_heads * head_dim :].reshape(tok_count, value_heads, head_dim)
    queries = jnp.repeat(queries, ratio, axis=1)
    keys = jnp.repeat(keys, ratio, axis=1)
    strength = jax.nn.sigmoid(gating[:, :value_heads]).T
    log_decay = (-jnp.exp(decay_log) * jax.nn.softplus(gating[:, value_heads:] + decay_bias)).T
    cumulative = jnp.cumsum(log_decay, axis=1)
    positions = jnp.arange(tok_count)
    lower_incl = positions[:, None] >= positions[None, :]
    lower_strict = positions[:, None] > positions[None, :]
    spread = cumulative[:, :, None] - cumulative[:, None, :]
    decay_mat = jnp.where(lower_incl, jnp.exp(jnp.where(lower_incl, spread, 0.0)), 0.0)
    key_major = keys.transpose(1, 0, 2)
    query_leading = queries.transpose(1, 0, 2)
    value_major = values.transpose(1, 0, 2)
    key_inner = jnp.einsum("htd,hid->hti", key_major, key_major, precision=lax.Precision.HIGHEST)
    lower_part = jnp.where(lower_strict, decay_mat * key_inner, 0.0) * strength[:, :, None]
    system = lower_part + jnp.eye(tok_count, dtype=jnp.float32)
    growth = jnp.exp(cumulative)
    scaled_keys = key_major * (strength * growth)[:, :, None]
    scaled_values = value_major * strength[:, :, None]
    inverse = unit_lower_inverse(system)
    key_resolved = jnp.einsum(
        "hts,hsd->htd", inverse, scaled_keys, precision=lax.Precision.HIGHEST
    )
    value_resolved = jnp.einsum(
        "hts,hsd->htd", inverse, scaled_values, precision=lax.Precision.HIGHEST
    )
    tail = jnp.exp(cumulative[:, -1:] - cumulative)
    trailing_keys = key_major * tail[:, :, None]
    eye_heads = jnp.broadcast_to(
        jnp.eye(head_dim, dtype=jnp.float32), (value_heads, head_dim, head_dim)
    )
    state_map = growth[:, -1][:, None, None] * eye_heads - jnp.einsum(
        "htk,htj->hkj", trailing_keys, key_resolved, precision=lax.Precision.HIGHEST
    )
    state_increment = jnp.einsum(
        "xbe,xbz->xez", trailing_keys, value_resolved, precision=lax.Precision.HIGHEST
    )
    initial_state = chained_state(state_map, state_increment, ("outer", "inner"), n_dev)
    updates = value_resolved - jnp.einsum(
        "mwx,mxd->mwd", key_resolved, initial_state, precision=lax.Precision.HIGHEST
    )
    query_key = (
        jnp.einsum("htd,hid->hti", query_leading, key_major, precision=lax.Precision.HIGHEST)
        * decay_mat
    )
    carried = (
        jnp.einsum("mwx,mxd->mwd", query_leading, initial_state, precision=lax.Precision.HIGHEST)
        * growth[:, :, None]
    )
    attended = carried + jnp.einsum(
        "hti,hiv->htv", query_key, updates, precision=lax.Precision.HIGHEST
    )
    attended = attended.transpose(1, 0, 2)
    core_out = (
        rms_scale(attended, output_gain)
        .astype(jnp.bfloat16)
        .reshape(tok_count, value_heads * head_dim)
    )
    return (hidden_out, core_out)


def solution(mesh):
    return jax.shard_map(
        per_device,
        mesh=mesh,
        in_specs=(
            P(("outer", "inner"), None),
            P(("outer", "inner"), None),
            P(("outer", "inner"), None),
            P(),
            P(("outer", "inner"), None, None),
            P(("outer", "inner"), None, None),
            P(("outer", "inner"), None, None),
            P(),
            P(None, "inner"),
            P(),
            P(),
            P(),
            P(),
            P(),
        ),
        out_specs=(P(("outer", "inner"), None), P(("outer", "inner"), None)),
        check_vma=False,
    )
```

```python
import jax
import jax.numpy as jnp
from jax import lax
from jax.sharding import PartitionSpec as P
from jax.experimental import pallas as pl
from jax.experimental.pallas import tpu as pltpu
import functools


def shifted(value, axis, steps):
    count = lax.axis_size(axis)
    leading, last = (max(0, -steps), min(count, count - steps))
    return lax.ppermute(value, axis, [(source, source + steps) for source in range(leading, last)])


def prefix_2(x, axis, join, neutral):
    place = lax.axis_index(axis)
    gathered = jax.tree.map(
        lambda a, kind: lax.all_gather(a.astype(kind), axis), x, (jnp.bfloat16, jnp.bfloat16)
    )
    state = jax.tree.map(lambda a, e: jnp.zeros_like(a) + jnp.asarray(e, a.dtype), x, neutral)

    def one(lap, state):
        return join(
            state,
            jax.tree.map(
                lambda a, own: lax.dynamic_index_in_dim(a, lap, 0, False).astype(own.dtype),
                gathered,
                x,
            ),
        )

    return lax.fori_loop(0, place, one, state)


def shortened(x):

    def short(part):
        return part.astype(jnp.bfloat16) if part.dtype == jnp.float32 else part

    return jax.tree.map(short, x)


def spread_2(value, axis, source):
    kept = jnp.where(lax.axis_index(axis) == source, value, 0).astype(value.dtype)
    return lax.psum(kept, axis)


def entering(x, axis, combine, identity):
    length, place = (lax.axis_size(axis), lax.axis_index(axis))
    everything = jax.tree.map(
        lambda part, kind: lax.all_gather(part.astype(kind), axis),
        x,
        jax.tree.map(lambda a: jnp.bfloat16 if a.dtype == jnp.float32 else a.dtype, x),
    )
    start = jax.tree.map(
        lambda part, zero: jnp.broadcast_to(jnp.asarray(zero, part.dtype), part.shape), x, identity
    )

    def lap(k, before):
        reached = k < place
        new = combine(
            before, jax.tree.map(lambda part, own: part[k].astype(own.dtype), everything, x)
        )
        return jax.tree.map(lambda a, b: jnp.where(reached, a, b), new, before)

    return lax.fori_loop(0, length, lap, start)


def rms_scale(values, gain):
    wide = values.astype(jnp.float32)
    return wide * lax.rsqrt(jnp.mean(wide * wide, axis=-1, keepdims=True) + 1e-06) * gain


def unit_heads(values):
    return values * lax.rsqrt(jnp.sum(values * values, axis=-1, keepdims=True) + 1e-06)


def run_experts(piece, gate_weight, up_weight, down_weight):
    gate = jnp.einsum("esd,edf->esf", piece, gate_weight, preferred_element_type=jnp.float32)
    upper = jnp.einsum("esd,edf->esf", piece, up_weight, preferred_element_type=jnp.float32)
    hidden = (jax.nn.silu(gate) * upper).astype(jnp.bfloat16)
    return jnp.einsum(
        "esf,efd->esd", hidden, down_weight, preferred_element_type=jnp.float32
    ).astype(jnp.bfloat16)


def unit_lower_inverse(system):
    size = system.shape[-1]
    if size == 1:
        return jnp.ones_like(system)
    half = size // 2
    both = unit_lower_inverse(jnp.stack([system[..., :half, :half], system[..., half:, half:]]))
    first, second = both[0], both[1]
    corner = -jnp.einsum(
        "...ij,...jk->...ik",
        second,
        jnp.einsum("...ij,...jk->...ik", system[..., half:, :half], first, precision=lax.Precision.HIGHEST),
        precision=lax.Precision.HIGHEST,
    )
    top = jnp.concatenate([first, jnp.zeros_like(first)], axis=-1)
    bottom = jnp.concatenate([corner, second], axis=-1)
    return jnp.concatenate([top, bottom], axis=-2)


def join_maps(earlier, later):
    first_map, first_state = earlier
    next_map, next_state = later
    joined_map = jnp.einsum("hij,hjk->hik", next_map, first_map, precision=lax.Precision.HIGHEST)
    joined_state = (
        jnp.einsum("hij,hjv->hiv", next_map, first_state, precision=lax.Precision.HIGHEST)
        + next_state
    )
    return (joined_map, joined_state)


def shifted_linear(value, axes, count, steps):
    return lax.ppermute(value, axes, [(source, source + steps) for source in range(count - steps)])


def scan_kernel(count, axes, groups, map_ref, state_ref, out_ref, own_map, own_state, send_map,
                send_state, land_map, land_state, send_sems, recv_sems):
    place = lax.axis_index(axes)
    span = map_ref.shape[0] // groups
    own_map[...] = map_ref[...]
    own_state[...] = state_ref[...]
    rounds = []
    steps = 1
    while steps < count:
        rounds.append(steps)
        steps *= 2
    rounds.append(1)
    total = len(rounds)
    inner = lax.axis_size(axes[1])

    def copies(number, group):
        other = place + rounds[number]
        heads = pl.ds(group * span, span)
        found = [
            pltpu.make_async_remote_copy(
                src_ref=send_state.at[number, heads], dst_ref=land_state.at[number, heads],
                send_sem=send_sems.at[number, group, 0], recv_sem=recv_sems.at[number, group, 0],
                device_id=(other // inner, other % inner), device_id_type=pl.DeviceIdType.MESH)
        ]
        if number < total - 2:
            found.append(
                pltpu.make_async_remote_copy(
                    src_ref=send_map.at[number, heads], dst_ref=land_map.at[number, heads],
                    send_sem=send_sems.at[number, group, 1], recv_sem=recv_sems.at[number, group, 1],
                    device_id=(other // inner, other % inner), device_id_type=pl.DeviceIdType.MESH)
            )
        return found

    def joined(number, group):
        def head(h, carry):
            mine = own_map[h]
            high = mine.astype(jnp.bfloat16)
            low = (mine - high.astype(jnp.float32)).astype(jnp.bfloat16)

            def apply(far):
                return jnp.dot(high, far, preferred_element_type=jnp.float32) + jnp.dot(
                    low, far, preferred_element_type=jnp.float32)

            own_state[h] = apply(land_state[number, h]) + own_state[h]
            if number < total - 2:
                own_map[h] = apply(land_map[number, h])
            return carry

        lax.fori_loop(group * span, group * span + span, head, 0)

    for number in range(total):
        for group in range(groups):
            heads = pl.ds(group * span, span)
            if number > 0:
                @pl.when(place >= rounds[number - 1])
                def _():
                    for copy in copies(number - 1, group):
                        copy.wait_recv()
                    joined(number - 1, group)
            send_state[number, heads] = own_state[heads].astype(jnp.bfloat16)
            if number < total - 2:
                send_map[number, heads] = own_map[heads].astype(jnp.bfloat16)

            @pl.when(place + rounds[number] < count)
            def _():
                for copy in copies(number, group):
                    copy.start()

    for group in range(groups):
        heads = pl.ds(group * span, span)

        @pl.when(place >= 1)
        def _():
            for copy in copies(total - 1, group):
                copy.wait_recv()
            out_ref[heads] = land_state[total - 1, heads].astype(jnp.float32)

        @pl.when(place < 1)
        def _():
            out_ref[heads] = jnp.zeros_like(out_ref[heads])

    for number in range(total):
        @pl.when(place + rounds[number] < count)
        def _():
            for group in range(groups):
                for copy in copies(number, group):
                    copy.wait_send()


def chained_state(state_map, state_increment, axes, count):
    heads, size, width = state_increment.shape
    rounds = 1
    while (1 << (rounds - 1)) < count:
        rounds += 1
    groups = 4
    block = pltpu.VMEM((rounds, heads, size, width), jnp.bfloat16)
    return pl.pallas_call(
        functools.partial(scan_kernel, count, axes, groups),
        out_shape=jax.ShapeDtypeStruct(state_increment.shape, jnp.float32),
        in_specs=[pl.BlockSpec(memory_space=pltpu.VMEM)] * 2,
        out_specs=pl.BlockSpec(memory_space=pltpu.VMEM),
        scratch_shapes=[
            pltpu.VMEM(state_map.shape, jnp.float32),
            pltpu.VMEM(state_increment.shape, jnp.float32),
            pltpu.VMEM((rounds, heads, size, size), jnp.bfloat16),
            block,
            pltpu.VMEM((rounds, heads, size, size), jnp.bfloat16),
            block,
            pltpu.SemaphoreType.DMA((rounds, groups, 2)),
            pltpu.SemaphoreType.DMA((rounds, groups, 2)),
        ],
        compiler_params=pltpu.CompilerParams(has_side_effects=True, vmem_limit_bytes=48 * 1024 * 1024),
    )(state_map, state_increment)


def per_device(
    tokens_in,
    expert_ids,
    route_weight,
    first_gain,
    gate_weight,
    up_weight,
    down_weight,
    second_gain,
    mixer_weight,
    gating_weight,
    filter_taps,
    decay_log,
    decay_bias,
    output_gain,
):
    n_outer = lax.axis_size("outer")
    n_inner = lax.axis_size("inner")
    n_dev = n_outer * n_inner
    tok_count, width = tokens_in.shape
    top_count = expert_ids.shape[1]
    local_experts = gate_weight.shape[0]
    experts_all = local_experts * n_dev
    capacity = max(2, 6 * tok_count * top_count // (5 * experts_all))
    rows_half = mixer_weight.shape[0] // 2
    side = lax.axis_index("outer") % 2
    own_rows = lax.dynamic_slice_in_dim(mixer_weight, side * rows_half, rows_half, axis=0)
    own_half = lax.all_gather(own_rows, "inner", axis=1, tiled=True)
    other_half = lax.ppermute(
        own_half, "outer", [(source, source ^ 1) for source in range(n_outer)]
    )
    normed_first = rms_scale(tokens_in, first_gain).astype(jnp.bfloat16)
    mix_weight = route_weight / jnp.sum(route_weight, axis=1, keepdims=True)
    flat_ids = expert_ids
    target = (
        flat_ids % local_experts * (n_dev * capacity)
        + flat_ids // local_experts * capacity
    )
    onehot = (flat_ids[:, :, None] == jnp.arange(experts_all, dtype=jnp.int32)[None, None, :]).astype(
        jnp.int32
    )
    counted = jnp.sum(onehot, axis=1)
    before = jnp.cumsum(counted, axis=0) - counted
    slot_index = jnp.sum(before[:, None, :] * onehot, axis=2)
    target = target + slot_index
    slots = jnp.arange(n_dev * local_experts * capacity, dtype=jnp.int32)
    hits = target[:, :, None] == slots[None, None, :]
    dispatch = jnp.any(hits, axis=1).astype(jnp.bfloat16)
    outgoing = jnp.einsum(
        "ts,td->sd", dispatch, normed_first, preferred_element_type=jnp.float32
    ).astype(jnp.bfloat16)
    outgoing = outgoing.reshape(local_experts, n_dev * capacity, width)
    served = run_experts(
        lax.all_to_all(outgoing, ("outer", "inner"), split_axis=1, concat_axis=1, tiled=True),
        gate_weight,
        up_weight,
        down_weight,
    )
    returned = lax.all_to_all(served, ("outer", "inner"), split_axis=1, concat_axis=1, tiled=True)
    returned = returned.reshape(-1, width)
    combine = jnp.sum(jnp.where(hits, mix_weight[:, :, None], 0.0), axis=1)
    combine_hi = combine.astype(jnp.bfloat16)
    combine_lo = (combine - combine_hi.astype(jnp.float32)).astype(jnp.bfloat16)
    mixture = jnp.dot(combine_hi, returned, preferred_element_type=jnp.float32) + jnp.dot(
        combine_lo, returned, preferred_element_type=jnp.float32
    )
    hidden_out = (tokens_in.astype(jnp.float32) + mixture).astype(jnp.bfloat16)
    normed_second = rms_scale(hidden_out, second_gain).astype(jnp.bfloat16)
    mixed = jnp.dot(
        lax.dynamic_slice_in_dim(normed_second, side * rows_half, rows_half, axis=1),
        own_half,
        preferred_element_type=jnp.float32,
    ) + jnp.dot(
        lax.dynamic_slice_in_dim(normed_second, (1 - side) * rows_half, rows_half, axis=1),
        other_half,
        preferred_element_type=jnp.float32,
    )
    projected = mixed.astype(jnp.bfloat16)
    gating = jnp.dot(normed_second, gating_weight, preferred_element_type=jnp.float32)
    taps = filter_taps.shape[0]
    rim = shifted(projected[tok_count - (taps - 1) :], ("outer", "inner"), 1)
    padded = jnp.concatenate([rim, projected], axis=0).astype(jnp.float32)
    filtered = jnp.zeros(projected.shape, jnp.float32)
    for tap_index in range(taps):
        filtered = (
            filtered
            + filter_taps[tap_index].astype(jnp.float32) * padded[tap_index : tap_index + tok_count]
        )
    filtered = jax.nn.silu(filtered)
    head_dim = output_gain.shape[0]
    value_heads = decay_log.shape[0]
    key_heads = (projected.shape[1] - value_heads * head_dim) // (2 * head_dim)
    ratio = value_heads // key_heads
    queries = unit_heads(
        filtered[:, : key_heads * head_dim].reshape(tok_count, key_heads, head_dim)
    ) * head_dim ** (-0.5)
    keys = unit_heads(
        filtered[:, key_heads * head_dim : 2 * key_heads * head_dim].reshape(
            tok_count, key_heads, head_dim
        )
    )
    values = filtered[:, 2 * key_heads * head_dim :].reshape(tok_count, value_heads, head_dim)
    queries = jnp.repeat(queries, ratio, axis=1)
    keys = jnp.repeat(keys, ratio, axis=1)
    strength = jax.nn.sigmoid(gating[:, :value_heads]).T
    log_decay = (-jnp.exp(decay_log) * jax.nn.softplus(gating[:, value_heads:] + decay_bias)).T
    cumulative = jnp.cumsum(log_decay, axis=1)
    positions = jnp.arange(tok_count)
    lower_incl = positions[:, None] >= positions[None, :]
    lower_strict = positions[:, None] > positions[None, :]
    spread = cumulative[:, :, None] - cumulative[:, None, :]
    decay_mat = jnp.where(lower_incl, jnp.exp(jnp.where(lower_incl, spread, 0.0)), 0.0)
    key_major = keys.transpose(1, 0, 2)
    query_leading = queries.transpose(1, 0, 2)
    value_major = values.transpose(1, 0, 2)
    key_inner = jnp.einsum("htd,hid->hti", key_major, key_major, precision=lax.Precision.HIGHEST)
    lower_part = jnp.where(lower_strict, decay_mat * key_inner, 0.0) * strength[:, :, None]
    system = lower_part + jnp.eye(tok_count, dtype=jnp.float32)
    growth = jnp.exp(cumulative)
    scaled_keys = key_major * (strength * growth)[:, :, None]
    scaled_values = value_major * strength[:, :, None]
    inverse = unit_lower_inverse(system)
    key_resolved = jnp.einsum(
        "hts,hsd->htd", inverse, scaled_keys, precision=lax.Precision.HIGHEST
    )
    value_resolved = jnp.einsum(
        "hts,hsd->htd", inverse, scaled_values, precision=lax.Precision.HIGHEST
    )
    tail = jnp.exp(cumulative[:, -1:] - cumulative)
    trailing_keys = key_major * tail[:, :, None]
    eye_heads = jnp.broadcast_to(
        jnp.eye(head_dim, dtype=jnp.float32), (value_heads, head_dim, head_dim)
    )
    state_map = growth[:, -1][:, None, None] * eye_heads - jnp.einsum(
        "htk,htj->hkj", trailing_keys, key_resolved, precision=lax.Precision.HIGHEST
    )
    state_increment = jnp.einsum(
        "xbe,xbz->xez", trailing_keys, value_resolved, precision=lax.Precision.HIGHEST
    )
    initial_state = chained_state(state_map, state_increment, ("outer", "inner"), n_dev)
    updates = value_resolved - jnp.einsum(
        "mwx,mxd->mwd", key_resolved, initial_state, precision=lax.Precision.HIGHEST
    )
    query_key = (
        jnp.einsum("htd,hid->hti", query_leading, key_major, precision=lax.Precision.HIGHEST)
        * decay_mat
    )
    carried = (
        jnp.einsum("mwx,mxd->mwd", query_leading, initial_state, precision=lax.Precision.HIGHEST)
        * growth[:, :, None]
    )
    attended = carried + jnp.einsum(
        "hti,hiv->htv", query_key, updates, precision=lax.Precision.HIGHEST
    )
    attended = attended.transpose(1, 0, 2)
    core_out = (
        rms_scale(attended, output_gain)
        .astype(jnp.bfloat16)
        .reshape(tok_count, value_heads * head_dim)
    )
    return (hidden_out, core_out)


def solution(mesh):
    return jax.shard_map(
        per_device,
        mesh=mesh,
        in_specs=(
            P(("outer", "inner"), None),
            P(("outer", "inner"), None),
            P(("outer", "inner"), None),
            P(),
            P(("outer", "inner"), None, None),
            P(("outer", "inner"), None, None),
            P(("outer", "inner"), None, None),
            P(),
            P(None, "inner"),
            P(),
            P(),
            P(),
            P(),
            P(),
        ),
        out_specs=(P(("outer", "inner"), None), P(("outer", "inner"), None)),
        check_vma=False,
    )
```

```python
import jax
import jax.numpy as jnp
from jax import lax
from jax.sharding import PartitionSpec as P
from jax.experimental import pallas as pl
from jax.experimental.pallas import tpu as pltpu
import functools


def shifted(value, axis, steps):
    count = lax.axis_size(axis)
    leading, last = (max(0, -steps), min(count, count - steps))
    return lax.ppermute(value, axis, [(source, source + steps) for source in range(leading, last)])


def prefix_2(x, axis, join, neutral):
    place = lax.axis_index(axis)
    gathered = jax.tree.map(
        lambda a, kind: lax.all_gather(a.astype(kind), axis), x, (jnp.bfloat16, jnp.bfloat16)
    )
    state = jax.tree.map(lambda a, e: jnp.zeros_like(a) + jnp.asarray(e, a.dtype), x, neutral)

    def one(lap, state):
        return join(
            state,
            jax.tree.map(
                lambda a, own: lax.dynamic_index_in_dim(a, lap, 0, False).astype(own.dtype),
                gathered,
                x,
            ),
        )

    return lax.fori_loop(0, place, one, state)


def shortened(x):

    def short(part):
        return part.astype(jnp.bfloat16) if part.dtype == jnp.float32 else part

    return jax.tree.map(short, x)


def spread_2(value, axis, source):
    kept = jnp.where(lax.axis_index(axis) == source, value, 0).astype(value.dtype)
    return lax.psum(kept, axis)


def entering(x, axis, combine, identity):
    length, place = (lax.axis_size(axis), lax.axis_index(axis))
    everything = jax.tree.map(
        lambda part, kind: lax.all_gather(part.astype(kind), axis),
        x,
        jax.tree.map(lambda a: jnp.bfloat16 if a.dtype == jnp.float32 else a.dtype, x),
    )
    start = jax.tree.map(
        lambda part, zero: jnp.broadcast_to(jnp.asarray(zero, part.dtype), part.shape), x, identity
    )

    def lap(k, before):
        reached = k < place
        new = combine(
            before, jax.tree.map(lambda part, own: part[k].astype(own.dtype), everything, x)
        )
        return jax.tree.map(lambda a, b: jnp.where(reached, a, b), new, before)

    return lax.fori_loop(0, length, lap, start)


def rms_scale(values, gain):
    wide = values.astype(jnp.float32)
    return wide * lax.rsqrt(jnp.mean(wide * wide, axis=-1, keepdims=True) + 1e-06) * gain


def unit_heads(values):
    return values * lax.rsqrt(jnp.sum(values * values, axis=-1, keepdims=True) + 1e-06)


def run_experts(piece, gate_weight, up_weight, down_weight):
    gate = jnp.einsum("esd,edf->esf", piece, gate_weight, preferred_element_type=jnp.float32)
    upper = jnp.einsum("esd,edf->esf", piece, up_weight, preferred_element_type=jnp.float32)
    hidden = (jax.nn.silu(gate) * upper).astype(jnp.bfloat16)
    return jnp.einsum(
        "esf,efd->esd", hidden, down_weight, preferred_element_type=jnp.float32
    ).astype(jnp.bfloat16)


def unit_lower_inverse(system):
    size = system.shape[-1]
    if size == 1:
        return jnp.ones_like(system)
    half = size // 2
    both = unit_lower_inverse(jnp.stack([system[..., :half, :half], system[..., half:, half:]]))
    first, second = both[0], both[1]
    corner = -jnp.einsum(
        "...ij,...jk->...ik",
        second,
        jnp.einsum("...ij,...jk->...ik", system[..., half:, :half], first, precision=lax.Precision.HIGHEST),
        precision=lax.Precision.HIGHEST,
    )
    top = jnp.concatenate([first, jnp.zeros_like(first)], axis=-1)
    bottom = jnp.concatenate([corner, second], axis=-1)
    return jnp.concatenate([top, bottom], axis=-2)


def join_maps(earlier, later):
    first_map, first_state = earlier
    next_map, next_state = later
    joined_map = jnp.einsum("hij,hjk->hik", next_map, first_map, precision=lax.Precision.HIGHEST)
    joined_state = (
        jnp.einsum("hij,hjv->hiv", next_map, first_state, precision=lax.Precision.HIGHEST)
        + next_state
    )
    return (joined_map, joined_state)


def shifted_linear(value, axes, count, steps):
    return lax.ppermute(value, axes, [(source, source + steps) for source in range(count - steps)])


def scan_kernel(count, axes, groups, map_ref, state_ref, out_ref, own_map, own_state, send_map,
                send_state, land_map, land_state, send_sems, recv_sems):
    place = lax.axis_index(axes)
    span = map_ref.shape[0] // groups
    own_map[...] = map_ref[...]
    own_state[...] = state_ref[...]
    rounds = []
    steps = 1
    while steps < count:
        rounds.append(steps)
        steps *= 2
    rounds.append(1)
    total = len(rounds)
    inner = lax.axis_size(axes[1])

    def copies(number, group):
        other = place + rounds[number]
        heads = pl.ds(group * span, span)
        found = [
            pltpu.make_async_remote_copy(
                src_ref=send_state.at[number, heads], dst_ref=land_state.at[number, heads],
                send_sem=send_sems.at[number, group, 0], recv_sem=recv_sems.at[number, group, 0],
                device_id=(other // inner, other % inner), device_id_type=pl.DeviceIdType.MESH)
        ]
        if number < total - 2:
            found.append(
                pltpu.make_async_remote_copy(
                    src_ref=send_map.at[number, heads], dst_ref=land_map.at[number, heads],
                    send_sem=send_sems.at[number, group, 1], recv_sem=recv_sems.at[number, group, 1],
                    device_id=(other // inner, other % inner), device_id_type=pl.DeviceIdType.MESH)
            )
        return found

    def joined(number, group):
        def head(h, carry):
            mine = own_map[h]
            high = mine.astype(jnp.bfloat16)
            low = (mine - high.astype(jnp.float32)).astype(jnp.bfloat16)

            def apply(far):
                return jnp.dot(high, far, preferred_element_type=jnp.float32) + jnp.dot(
                    low, far, preferred_element_type=jnp.float32)

            own_state[h] = apply(land_state[number, h]) + own_state[h]
            if number < total - 2:
                own_map[h] = apply(land_map[number, h])
            return carry

        lax.fori_loop(group * span, group * span + span, head, 0)

    for number in range(total):
        for group in range(groups):
            heads = pl.ds(group * span, span)
            if number > 0:
                @pl.when(place >= rounds[number - 1])
                def _():
                    for copy in copies(number - 1, group):
                        copy.wait_recv()
                    joined(number - 1, group)
            send_state[number, heads] = own_state[heads].astype(jnp.bfloat16)
            if number < total - 2:
                send_map[number, heads] = own_map[heads].astype(jnp.bfloat16)

            @pl.when(place + rounds[number] < count)
            def _():
                for copy in copies(number, group):
                    copy.start()

    for group in range(groups):
        heads = pl.ds(group * span, span)

        @pl.when(place >= 1)
        def _():
            for copy in copies(total - 1, group):
                copy.wait_recv()
            out_ref[heads] = land_state[total - 1, heads].astype(jnp.float32)

        @pl.when(place < 1)
        def _():
            out_ref[heads] = jnp.zeros_like(out_ref[heads])

    for number in range(total):
        @pl.when(place + rounds[number] < count)
        def _():
            for group in range(groups):
                for copy in copies(number, group):
                    copy.wait_send()


def chained_state(state_map, state_increment, axes, count):
    heads, size, width = state_increment.shape
    rounds = 1
    while (1 << (rounds - 1)) < count:
        rounds += 1
    groups = 8
    block = pltpu.VMEM((rounds, heads, size, width), jnp.bfloat16)
    return pl.pallas_call(
        functools.partial(scan_kernel, count, axes, groups),
        out_shape=jax.ShapeDtypeStruct(state_increment.shape, jnp.float32),
        in_specs=[pl.BlockSpec(memory_space=pltpu.VMEM)] * 2,
        out_specs=pl.BlockSpec(memory_space=pltpu.VMEM),
        scratch_shapes=[
            pltpu.VMEM(state_map.shape, jnp.float32),
            pltpu.VMEM(state_increment.shape, jnp.float32),
            pltpu.VMEM((rounds, heads, size, size), jnp.bfloat16),
            block,
            pltpu.VMEM((rounds, heads, size, size), jnp.bfloat16),
            block,
            pltpu.SemaphoreType.DMA((rounds, groups, 2)),
            pltpu.SemaphoreType.DMA((rounds, groups, 2)),
        ],
        compiler_params=pltpu.CompilerParams(has_side_effects=True, vmem_limit_bytes=48 * 1024 * 1024),
    )(state_map, state_increment)


def per_device(
    tokens_in,
    expert_ids,
    route_weight,
    first_gain,
    gate_weight,
    up_weight,
    down_weight,
    second_gain,
    mixer_weight,
    gating_weight,
    filter_taps,
    decay_log,
    decay_bias,
    output_gain,
):
    n_outer = lax.axis_size("outer")
    n_inner = lax.axis_size("inner")
    n_dev = n_outer * n_inner
    tok_count, width = tokens_in.shape
    top_count = expert_ids.shape[1]
    local_experts = gate_weight.shape[0]
    experts_all = local_experts * n_dev
    capacity = max(2, 6 * tok_count * top_count // (5 * experts_all))
    rows_half = mixer_weight.shape[0] // 2
    side = lax.axis_index("outer") % 2
    own_rows = lax.dynamic_slice_in_dim(mixer_weight, side * rows_half, rows_half, axis=0)
    own_half = lax.all_gather(own_rows, "inner", axis=1, tiled=True)
    other_half = lax.ppermute(
        own_half, "outer", [(source, source ^ 1) for source in range(n_outer)]
    )
    normed_first = rms_scale(tokens_in, first_gain).astype(jnp.bfloat16)
    mix_weight = route_weight / jnp.sum(route_weight, axis=1, keepdims=True)
    flat_ids = expert_ids
    target = (
        flat_ids % local_experts * (n_dev * capacity)
        + flat_ids // local_experts * capacity
    )
    onehot = (flat_ids[:, :, None] == jnp.arange(experts_all, dtype=jnp.int32)[None, None, :]).astype(
        jnp.int32
    )
    counted = jnp.sum(onehot, axis=1)
    before = jnp.cumsum(counted, axis=0) - counted
    slot_index = jnp.sum(before[:, None, :] * onehot, axis=2)
    target = target + slot_index
    slots = jnp.arange(n_dev * local_experts * capacity, dtype=jnp.int32)
    hits = target[:, :, None] == slots[None, None, :]
    dispatch = jnp.any(hits, axis=1).astype(jnp.bfloat16)
    outgoing = jnp.einsum(
        "ts,td->sd", dispatch, normed_first, preferred_element_type=jnp.float32
    ).astype(jnp.bfloat16)
    outgoing = outgoing.reshape(local_experts, n_dev * capacity, width)
    served = run_experts(
        lax.all_to_all(outgoing, ("outer", "inner"), split_axis=1, concat_axis=1, tiled=True),
        gate_weight,
        up_weight,
        down_weight,
    )
    returned = lax.all_to_all(served, ("outer", "inner"), split_axis=1, concat_axis=1, tiled=True)
    returned = returned.reshape(-1, width)
    combine = jnp.sum(jnp.where(hits, mix_weight[:, :, None], 0.0), axis=1)
    combine_hi = combine.astype(jnp.bfloat16)
    combine_lo = (combine - combine_hi.astype(jnp.float32)).astype(jnp.bfloat16)
    mixture = jnp.dot(combine_hi, returned, preferred_element_type=jnp.float32) + jnp.dot(
        combine_lo, returned, preferred_element_type=jnp.float32
    )
    hidden_out = (tokens_in.astype(jnp.float32) + mixture).astype(jnp.bfloat16)
    normed_second = rms_scale(hidden_out, second_gain).astype(jnp.bfloat16)
    mixed = jnp.dot(
        lax.dynamic_slice_in_dim(normed_second, side * rows_half, rows_half, axis=1),
        own_half,
        preferred_element_type=jnp.float32,
    ) + jnp.dot(
        lax.dynamic_slice_in_dim(normed_second, (1 - side) * rows_half, rows_half, axis=1),
        other_half,
        preferred_element_type=jnp.float32,
    )
    projected = mixed.astype(jnp.bfloat16)
    gating = jnp.dot(normed_second, gating_weight, preferred_element_type=jnp.float32)
    taps = filter_taps.shape[0]
    rim = shifted(projected[tok_count - (taps - 1) :], ("outer", "inner"), 1)
    padded = jnp.concatenate([rim, projected], axis=0).astype(jnp.float32)
    filtered = jnp.zeros(projected.shape, jnp.float32)
    for tap_index in range(taps):
        filtered = (
            filtered
            + filter_taps[tap_index].astype(jnp.float32) * padded[tap_index : tap_index + tok_count]
        )
    filtered = jax.nn.silu(filtered)
    head_dim = output_gain.shape[0]
    value_heads = decay_log.shape[0]
    key_heads = (projected.shape[1] - value_heads * head_dim) // (2 * head_dim)
    ratio = value_heads // key_heads
    queries = unit_heads(
        filtered[:, : key_heads * head_dim].reshape(tok_count, key_heads, head_dim)
    ) * head_dim ** (-0.5)
    keys = unit_heads(
        filtered[:, key_heads * head_dim : 2 * key_heads * head_dim].reshape(
            tok_count, key_heads, head_dim
        )
    )
    values = filtered[:, 2 * key_heads * head_dim :].reshape(tok_count, value_heads, head_dim)
    queries = jnp.repeat(queries, ratio, axis=1)
    keys = jnp.repeat(keys, ratio, axis=1)
    strength = jax.nn.sigmoid(gating[:, :value_heads]).T
    log_decay = (-jnp.exp(decay_log) * jax.nn.softplus(gating[:, value_heads:] + decay_bias)).T
    cumulative = jnp.cumsum(log_decay, axis=1)
    positions = jnp.arange(tok_count)
    lower_incl = positions[:, None] >= positions[None, :]
    lower_strict = positions[:, None] > positions[None, :]
    spread = cumulative[:, :, None] - cumulative[:, None, :]
    decay_mat = jnp.where(lower_incl, jnp.exp(jnp.where(lower_incl, spread, 0.0)), 0.0)
    key_major = keys.transpose(1, 0, 2)
    query_leading = queries.transpose(1, 0, 2)
    value_major = values.transpose(1, 0, 2)
    key_inner = jnp.einsum("htd,hid->hti", key_major, key_major, precision=lax.Precision.HIGHEST)
    lower_part = jnp.where(lower_strict, decay_mat * key_inner, 0.0) * strength[:, :, None]
    system = lower_part + jnp.eye(tok_count, dtype=jnp.float32)
    growth = jnp.exp(cumulative)
    scaled_keys = key_major * (strength * growth)[:, :, None]
    scaled_values = value_major * strength[:, :, None]
    inverse = unit_lower_inverse(system)
    key_resolved = jnp.einsum(
        "hts,hsd->htd", inverse, scaled_keys, precision=lax.Precision.HIGHEST
    )
    value_resolved = jnp.einsum(
        "hts,hsd->htd", inverse, scaled_values, precision=lax.Precision.HIGHEST
    )
    tail = jnp.exp(cumulative[:, -1:] - cumulative)
    trailing_keys = key_major * tail[:, :, None]
    eye_heads = jnp.broadcast_to(
        jnp.eye(head_dim, dtype=jnp.float32), (value_heads, head_dim, head_dim)
    )
    state_map = growth[:, -1][:, None, None] * eye_heads - jnp.einsum(
        "htk,htj->hkj", trailing_keys, key_resolved, precision=lax.Precision.HIGHEST
    )
    state_increment = jnp.einsum(
        "xbe,xbz->xez", trailing_keys, value_resolved, precision=lax.Precision.HIGHEST
    )
    initial_state = chained_state(state_map, state_increment, ("outer", "inner"), n_dev)
    updates = value_resolved - jnp.einsum(
        "mwx,mxd->mwd", key_resolved, initial_state, precision=lax.Precision.HIGHEST
    )
    query_key = (
        jnp.einsum("htd,hid->hti", query_leading, key_major, precision=lax.Precision.HIGHEST)
        * decay_mat
    )
    carried = (
        jnp.einsum("mwx,mxd->mwd", query_leading, initial_state, precision=lax.Precision.HIGHEST)
        * growth[:, :, None]
    )
    attended = carried + jnp.einsum(
        "hti,hiv->htv", query_key, updates, precision=lax.Precision.HIGHEST
    )
    attended = attended.transpose(1, 0, 2)
    core_out = (
        rms_scale(attended, output_gain)
        .astype(jnp.bfloat16)
        .reshape(tok_count, value_heads * head_dim)
    )
    return (hidden_out, core_out)


def solution(mesh):
    return jax.shard_map(
        per_device,
        mesh=mesh,
        in_specs=(
            P(("outer", "inner"), None),
            P(("outer", "inner"), None),
            P(("outer", "inner"), None),
            P(),
            P(("outer", "inner"), None, None),
            P(("outer", "inner"), None, None),
            P(("outer", "inner"), None, None),
            P(),
            P(None, "inner"),
            P(),
            P(),
            P(),
            P(),
            P(),
        ),
        out_specs=(P(("outer", "inner"), None), P(("outer", "inner"), None)),
        check_vma=False,
    )
```

```python
import jax
import jax.numpy as jnp
from jax import lax
from jax.sharding import PartitionSpec as P
from jax.experimental import pallas as pl
from jax.experimental.pallas import tpu as pltpu
import functools


def shifted(value, axis, steps):
    count = lax.axis_size(axis)
    leading, last = (max(0, -steps), min(count, count - steps))
    return lax.ppermute(value, axis, [(source, source + steps) for source in range(leading, last)])


def prefix_2(x, axis, join, neutral):
    place = lax.axis_index(axis)
    gathered = jax.tree.map(
        lambda a, kind: lax.all_gather(a.astype(kind), axis), x, (jnp.bfloat16, jnp.bfloat16)
    )
    state = jax.tree.map(lambda a, e: jnp.zeros_like(a) + jnp.asarray(e, a.dtype), x, neutral)

    def one(lap, state):
        return join(
            state,
            jax.tree.map(
                lambda a, own: lax.dynamic_index_in_dim(a, lap, 0, False).astype(own.dtype),
                gathered,
                x,
            ),
        )

    return lax.fori_loop(0, place, one, state)


def shortened(x):

    def short(part):
        return part.astype(jnp.bfloat16) if part.dtype == jnp.float32 else part

    return jax.tree.map(short, x)


def spread_2(value, axis, source):
    kept = jnp.where(lax.axis_index(axis) == source, value, 0).astype(value.dtype)
    return lax.psum(kept, axis)


def entering(x, axis, combine, identity):
    length, place = (lax.axis_size(axis), lax.axis_index(axis))
    everything = jax.tree.map(
        lambda part, kind: lax.all_gather(part.astype(kind), axis),
        x,
        jax.tree.map(lambda a: jnp.bfloat16 if a.dtype == jnp.float32 else a.dtype, x),
    )
    start = jax.tree.map(
        lambda part, zero: jnp.broadcast_to(jnp.asarray(zero, part.dtype), part.shape), x, identity
    )

    def lap(k, before):
        reached = k < place
        new = combine(
            before, jax.tree.map(lambda part, own: part[k].astype(own.dtype), everything, x)
        )
        return jax.tree.map(lambda a, b: jnp.where(reached, a, b), new, before)

    return lax.fori_loop(0, length, lap, start)


def rms_scale(values, gain):
    wide = values.astype(jnp.float32)
    return wide * lax.rsqrt(jnp.mean(wide * wide, axis=-1, keepdims=True) + 1e-06) * gain


def unit_heads(values):
    return values * lax.rsqrt(jnp.sum(values * values, axis=-1, keepdims=True) + 1e-06)


def run_experts(piece, gate_weight, up_weight, down_weight):
    gate = jnp.einsum("esd,edf->esf", piece, gate_weight, preferred_element_type=jnp.float32)
    upper = jnp.einsum("esd,edf->esf", piece, up_weight, preferred_element_type=jnp.float32)
    hidden = (jax.nn.silu(gate) * upper).astype(jnp.bfloat16)
    return jnp.einsum(
        "esf,efd->esd", hidden, down_weight, preferred_element_type=jnp.float32
    ).astype(jnp.bfloat16)


def unit_lower_inverse(system):
    size = system.shape[-1]
    if size == 1:
        return jnp.ones_like(system)
    half = size // 2
    both = unit_lower_inverse(jnp.stack([system[..., :half, :half], system[..., half:, half:]]))
    first, second = both[0], both[1]
    corner = -jnp.einsum(
        "...ij,...jk->...ik",
        second,
        jnp.einsum("...ij,...jk->...ik", system[..., half:, :half], first, precision=lax.Precision.HIGH),
        precision=lax.Precision.HIGH,
    )
    top = jnp.concatenate([first, jnp.zeros_like(first)], axis=-1)
    bottom = jnp.concatenate([corner, second], axis=-1)
    return jnp.concatenate([top, bottom], axis=-2)


def join_maps(earlier, later):
    first_map, first_state = earlier
    next_map, next_state = later
    joined_map = jnp.einsum("hij,hjk->hik", next_map, first_map, precision=lax.Precision.HIGHEST)
    joined_state = (
        jnp.einsum("hij,hjv->hiv", next_map, first_state, precision=lax.Precision.HIGHEST)
        + next_state
    )
    return (joined_map, joined_state)


def shifted_linear(value, axes, count, steps):
    return lax.ppermute(value, axes, [(source, source + steps) for source in range(count - steps)])


def scan_kernel(count, axes, groups, map_ref, state_ref, out_ref, own_map, own_state, send_map,
                send_state, land_map, land_state, send_sems, recv_sems):
    place = lax.axis_index(axes)
    span = map_ref.shape[0] // groups
    own_map[...] = map_ref[...]
    own_state[...] = state_ref[...]
    rounds = []
    steps = 1
    while steps < count:
        rounds.append(steps)
        steps *= 2
    rounds.append(1)
    total = len(rounds)
    inner = lax.axis_size(axes[1])

    def copies(number, group):
        other = place + rounds[number]
        heads = pl.ds(group * span, span)
        found = [
            pltpu.make_async_remote_copy(
                src_ref=send_state.at[number, heads], dst_ref=land_state.at[number, heads],
                send_sem=send_sems.at[number, group, 0], recv_sem=recv_sems.at[number, group, 0],
                device_id=(other // inner, other % inner), device_id_type=pl.DeviceIdType.MESH)
        ]
        if number < total - 2:
            found.append(
                pltpu.make_async_remote_copy(
                    src_ref=send_map.at[number, heads], dst_ref=land_map.at[number, heads],
                    send_sem=send_sems.at[number, group, 1], recv_sem=recv_sems.at[number, group, 1],
                    device_id=(other // inner, other % inner), device_id_type=pl.DeviceIdType.MESH)
            )
        return found

    def joined(number, group):
        def head(h, carry):
            mine = own_map[h]
            high = mine.astype(jnp.bfloat16)
            low = (mine - high.astype(jnp.float32)).astype(jnp.bfloat16)

            def apply(far):
                return jnp.dot(high, far, preferred_element_type=jnp.float32) + jnp.dot(
                    low, far, preferred_element_type=jnp.float32)

            own_state[h] = apply(land_state[number, h]) + own_state[h]
            if number < total - 2:
                own_map[h] = apply(land_map[number, h])
            return carry

        lax.fori_loop(group * span, group * span + span, head, 0)

    for number in range(total):
        for group in range(groups):
            heads = pl.ds(group * span, span)
            if number > 0:
                @pl.when(place >= rounds[number - 1])
                def _():
                    for copy in copies(number - 1, group):
                        copy.wait_recv()
                    joined(number - 1, group)
            send_state[number, heads] = own_state[heads].astype(jnp.bfloat16)
            if number < total - 2:
                send_map[number, heads] = own_map[heads].astype(jnp.bfloat16)

            @pl.when(place + rounds[number] < count)
            def _():
                for copy in copies(number, group):
                    copy.start()

    for group in range(groups):
        heads = pl.ds(group * span, span)

        @pl.when(place >= 1)
        def _():
            for copy in copies(total - 1, group):
                copy.wait_recv()
            out_ref[heads] = land_state[total - 1, heads].astype(jnp.float32)

        @pl.when(place < 1)
        def _():
            out_ref[heads] = jnp.zeros_like(out_ref[heads])

    for number in range(total):
        @pl.when(place + rounds[number] < count)
        def _():
            for group in range(groups):
                for copy in copies(number, group):
                    copy.wait_send()


def chained_state(state_map, state_increment, axes, count):
    heads, size, width = state_increment.shape
    rounds = 1
    while (1 << (rounds - 1)) < count:
        rounds += 1
    groups = 4
    block = pltpu.VMEM((rounds, heads, size, width), jnp.bfloat16)
    return pl.pallas_call(
        functools.partial(scan_kernel, count, axes, groups),
        out_shape=jax.ShapeDtypeStruct(state_increment.shape, jnp.float32),
        in_specs=[pl.BlockSpec(memory_space=pltpu.VMEM)] * 2,
        out_specs=pl.BlockSpec(memory_space=pltpu.VMEM),
        scratch_shapes=[
            pltpu.VMEM(state_map.shape, jnp.float32),
            pltpu.VMEM(state_increment.shape, jnp.float32),
            pltpu.VMEM((rounds, heads, size, size), jnp.bfloat16),
            block,
            pltpu.VMEM((rounds, heads, size, size), jnp.bfloat16),
            block,
            pltpu.SemaphoreType.DMA((rounds, groups, 2)),
            pltpu.SemaphoreType.DMA((rounds, groups, 2)),
        ],
        compiler_params=pltpu.CompilerParams(has_side_effects=True, vmem_limit_bytes=48 * 1024 * 1024),
    )(state_map, state_increment)


def per_device(
    tokens_in,
    expert_ids,
    route_weight,
    first_gain,
    gate_weight,
    up_weight,
    down_weight,
    second_gain,
    mixer_weight,
    gating_weight,
    filter_taps,
    decay_log,
    decay_bias,
    output_gain,
):
    n_outer = lax.axis_size("outer")
    n_inner = lax.axis_size("inner")
    n_dev = n_outer * n_inner
    tok_count, width = tokens_in.shape
    top_count = expert_ids.shape[1]
    local_experts = gate_weight.shape[0]
    experts_all = local_experts * n_dev
    capacity = max(2, 6 * tok_count * top_count // (5 * experts_all))
    rows_half = mixer_weight.shape[0] // 2
    side = lax.axis_index("outer") % 2
    own_rows = lax.dynamic_slice_in_dim(mixer_weight, side * rows_half, rows_half, axis=0)
    own_half = lax.all_gather(own_rows, "inner", axis=1, tiled=True)
    other_half = lax.ppermute(
        own_half, "outer", [(source, source ^ 1) for source in range(n_outer)]
    )
    normed_first = rms_scale(tokens_in, first_gain).astype(jnp.bfloat16)
    mix_weight = route_weight / jnp.sum(route_weight, axis=1, keepdims=True)
    flat_ids = expert_ids
    target = (
        flat_ids % local_experts * (n_dev * capacity)
        + flat_ids // local_experts * capacity
    )
    onehot = (flat_ids[:, :, None] == jnp.arange(experts_all, dtype=jnp.int32)[None, None, :]).astype(
        jnp.int32
    )
    counted = jnp.sum(onehot, axis=1)
    before = jnp.cumsum(counted, axis=0) - counted
    slot_index = jnp.sum(before[:, None, :] * onehot, axis=2)
    target = target + slot_index
    slots = jnp.arange(n_dev * local_experts * capacity, dtype=jnp.int32)
    hits = target[:, :, None] == slots[None, None, :]
    dispatch = jnp.any(hits, axis=1).astype(jnp.bfloat16)
    outgoing = jnp.einsum(
        "ts,td->sd", dispatch, normed_first, preferred_element_type=jnp.float32
    ).astype(jnp.bfloat16)
    outgoing = outgoing.reshape(local_experts, n_dev * capacity, width)
    served = run_experts(
        lax.all_to_all(outgoing, ("outer", "inner"), split_axis=1, concat_axis=1, tiled=True),
        gate_weight,
        up_weight,
        down_weight,
    )
    returned = lax.all_to_all(served, ("outer", "inner"), split_axis=1, concat_axis=1, tiled=True)
    returned = returned.reshape(-1, width)
    combine = jnp.sum(jnp.where(hits, mix_weight[:, :, None], 0.0), axis=1)
    combine_hi = combine.astype(jnp.bfloat16)
    combine_lo = (combine - combine_hi.astype(jnp.float32)).astype(jnp.bfloat16)
    mixture = jnp.dot(combine_hi, returned, preferred_element_type=jnp.float32) + jnp.dot(
        combine_lo, returned, preferred_element_type=jnp.float32
    )
    hidden_out = (tokens_in.astype(jnp.float32) + mixture).astype(jnp.bfloat16)
    normed_second = rms_scale(hidden_out, second_gain).astype(jnp.bfloat16)
    mixed = jnp.dot(
        lax.dynamic_slice_in_dim(normed_second, side * rows_half, rows_half, axis=1),
        own_half,
        preferred_element_type=jnp.float32,
    ) + jnp.dot(
        lax.dynamic_slice_in_dim(normed_second, (1 - side) * rows_half, rows_half, axis=1),
        other_half,
        preferred_element_type=jnp.float32,
    )
    projected = mixed.astype(jnp.bfloat16)
    gating = jnp.dot(normed_second, gating_weight, preferred_element_type=jnp.float32)
    taps = filter_taps.shape[0]
    rim = shifted(projected[tok_count - (taps - 1) :], ("outer", "inner"), 1)
    padded = jnp.concatenate([rim, projected], axis=0).astype(jnp.float32)
    filtered = jnp.zeros(projected.shape, jnp.float32)
    for tap_index in range(taps):
        filtered = (
            filtered
            + filter_taps[tap_index].astype(jnp.float32) * padded[tap_index : tap_index + tok_count]
        )
    filtered = jax.nn.silu(filtered)
    head_dim = output_gain.shape[0]
    value_heads = decay_log.shape[0]
    key_heads = (projected.shape[1] - value_heads * head_dim) // (2 * head_dim)
    ratio = value_heads // key_heads
    queries = unit_heads(
        filtered[:, : key_heads * head_dim].reshape(tok_count, key_heads, head_dim)
    ) * head_dim ** (-0.5)
    keys = unit_heads(
        filtered[:, key_heads * head_dim : 2 * key_heads * head_dim].reshape(
            tok_count, key_heads, head_dim
        )
    )
    values = filtered[:, 2 * key_heads * head_dim :].reshape(tok_count, value_heads, head_dim)
    queries = jnp.repeat(queries, ratio, axis=1)
    keys = jnp.repeat(keys, ratio, axis=1)
    strength = jax.nn.sigmoid(gating[:, :value_heads]).T
    log_decay = (-jnp.exp(decay_log) * jax.nn.softplus(gating[:, value_heads:] + decay_bias)).T
    cumulative = jnp.cumsum(log_decay, axis=1)
    positions = jnp.arange(tok_count)
    lower_incl = positions[:, None] >= positions[None, :]
    lower_strict = positions[:, None] > positions[None, :]
    spread = cumulative[:, :, None] - cumulative[:, None, :]
    decay_mat = jnp.where(lower_incl, jnp.exp(jnp.where(lower_incl, spread, 0.0)), 0.0)
    key_major = keys.transpose(1, 0, 2)
    query_leading = queries.transpose(1, 0, 2)
    value_major = values.transpose(1, 0, 2)
    key_inner = jnp.einsum("htd,hid->hti", key_major, key_major, precision=lax.Precision.HIGH)
    lower_part = jnp.where(lower_strict, decay_mat * key_inner, 0.0) * strength[:, :, None]
    system = lower_part + jnp.eye(tok_count, dtype=jnp.float32)
    growth = jnp.exp(cumulative)
    scaled_keys = key_major * (strength * growth)[:, :, None]
    scaled_values = value_major * strength[:, :, None]
    inverse = unit_lower_inverse(system)
    key_resolved = jnp.einsum(
        "hts,hsd->htd", inverse, scaled_keys, precision=lax.Precision.HIGH
    )
    value_resolved = jnp.einsum(
        "hts,hsd->htd", inverse, scaled_values, precision=lax.Precision.HIGH
    )
    tail = jnp.exp(cumulative[:, -1:] - cumulative)
    trailing_keys = key_major * tail[:, :, None]
    eye_heads = jnp.broadcast_to(
        jnp.eye(head_dim, dtype=jnp.float32), (value_heads, head_dim, head_dim)
    )
    state_map = growth[:, -1][:, None, None] * eye_heads - jnp.einsum(
        "htk,htj->hkj", trailing_keys, key_resolved, precision=lax.Precision.HIGH
    )
    state_increment = jnp.einsum(
        "xbe,xbz->xez", trailing_keys, value_resolved, precision=lax.Precision.HIGH
    )
    initial_state = chained_state(state_map, state_increment, ("outer", "inner"), n_dev)
    updates = value_resolved - jnp.einsum(
        "mwx,mxd->mwd", key_resolved, initial_state, precision=lax.Precision.HIGH
    )
    query_key = (
        jnp.einsum("htd,hid->hti", query_leading, key_major, precision=lax.Precision.HIGH)
        * decay_mat
    )
    carried = (
        jnp.einsum("mwx,mxd->mwd", query_leading, initial_state, precision=lax.Precision.HIGH)
        * growth[:, :, None]
    )
    attended = carried + jnp.einsum(
        "hti,hiv->htv", query_key, updates, precision=lax.Precision.HIGH
    )
    attended = attended.transpose(1, 0, 2)
    core_out = (
        rms_scale(attended, output_gain)
        .astype(jnp.bfloat16)
        .reshape(tok_count, value_heads * head_dim)
    )
    return (hidden_out, core_out)


def solution(mesh):
    return jax.shard_map(
        per_device,
        mesh=mesh,
        in_specs=(
            P(("outer", "inner"), None),
            P(("outer", "inner"), None),
            P(("outer", "inner"), None),
            P(),
            P(("outer", "inner"), None, None),
            P(("outer", "inner"), None, None),
            P(("outer", "inner"), None, None),
            P(),
            P(None, "inner"),
            P(),
            P(),
            P(),
            P(),
            P(),
        ),
        out_specs=(P(("outer", "inner"), None), P(("outer", "inner"), None)),
        check_vma=False,
    )
```

```python
import jax
import jax.numpy as jnp
from jax import lax
from jax.sharding import PartitionSpec as P
from jax.experimental import pallas as pl
from jax.experimental.pallas import tpu as pltpu
import functools


def shifted(value, axis, steps):
    count = lax.axis_size(axis)
    leading, last = (max(0, -steps), min(count, count - steps))
    return lax.ppermute(value, axis, [(source, source + steps) for source in range(leading, last)])


def prefix_2(x, axis, join, neutral):
    place = lax.axis_index(axis)
    gathered = jax.tree.map(
        lambda a, kind: lax.all_gather(a.astype(kind), axis), x, (jnp.bfloat16, jnp.bfloat16)
    )
    state = jax.tree.map(lambda a, e: jnp.zeros_like(a) + jnp.asarray(e, a.dtype), x, neutral)

    def one(lap, state):
        return join(
            state,
            jax.tree.map(
                lambda a, own: lax.dynamic_index_in_dim(a, lap, 0, False).astype(own.dtype),
                gathered,
                x,
            ),
        )

    return lax.fori_loop(0, place, one, state)


def shortened(x):

    def short(part):
        return part.astype(jnp.bfloat16) if part.dtype == jnp.float32 else part

    return jax.tree.map(short, x)


def spread_2(value, axis, source):
    kept = jnp.where(lax.axis_index(axis) == source, value, 0).astype(value.dtype)
    return lax.psum(kept, axis)


def entering(x, axis, combine, identity):
    length, place = (lax.axis_size(axis), lax.axis_index(axis))
    everything = jax.tree.map(
        lambda part, kind: lax.all_gather(part.astype(kind), axis),
        x,
        jax.tree.map(lambda a: jnp.bfloat16 if a.dtype == jnp.float32 else a.dtype, x),
    )
    start = jax.tree.map(
        lambda part, zero: jnp.broadcast_to(jnp.asarray(zero, part.dtype), part.shape), x, identity
    )

    def lap(k, before):
        reached = k < place
        new = combine(
            before, jax.tree.map(lambda part, own: part[k].astype(own.dtype), everything, x)
        )
        return jax.tree.map(lambda a, b: jnp.where(reached, a, b), new, before)

    return lax.fori_loop(0, length, lap, start)


def rms_scale(values, gain):
    wide = values.astype(jnp.float32)
    return wide * lax.rsqrt(jnp.mean(wide * wide, axis=-1, keepdims=True) + 1e-06) * gain


def unit_heads(values):
    return values * lax.rsqrt(jnp.sum(values * values, axis=-1, keepdims=True) + 1e-06)


def run_experts(piece, gate_weight, up_weight, down_weight):
    gate = jnp.einsum("esd,edf->esf", piece, gate_weight, preferred_element_type=jnp.float32)
    upper = jnp.einsum("esd,edf->esf", piece, up_weight, preferred_element_type=jnp.float32)
    hidden = (jax.nn.silu(gate) * upper).astype(jnp.bfloat16)
    return jnp.einsum(
        "esf,efd->esd", hidden, down_weight, preferred_element_type=jnp.float32
    ).astype(jnp.bfloat16)


def unit_lower_inverse(system):
    size = system.shape[-1]
    rows = lax.broadcasted_iota(jnp.int32, (size, size), 0)
    cols = lax.broadcasted_iota(jnp.int32, (size, size), 1)
    lower = system - jnp.eye(size, dtype=system.dtype)
    levels = size.bit_length() - 1

    def level(number, inverse):
        width = jnp.left_shift(1, number)
        corner = (
            (rows // (2 * width) == cols // (2 * width))
            & ((rows // width) % 2 == 1)
            & ((cols // width) % 2 == 0)
        )
        part = jnp.where(corner, lower, 0.0)
        return inverse - jnp.einsum(
            "...ij,...jk->...ik",
            inverse,
            jnp.einsum("...ij,...jk->...ik", part, inverse, precision=lax.Precision.HIGH),
            precision=lax.Precision.HIGH,
        )

    start = jnp.broadcast_to(jnp.eye(size, dtype=system.dtype), system.shape)
    return lax.fori_loop(0, levels, level, start)


def join_maps(earlier, later):
    first_map, first_state = earlier
    next_map, next_state = later
    joined_map = jnp.einsum("hij,hjk->hik", next_map, first_map, precision=lax.Precision.HIGHEST)
    joined_state = (
        jnp.einsum("hij,hjv->hiv", next_map, first_state, precision=lax.Precision.HIGHEST)
        + next_state
    )
    return (joined_map, joined_state)


def shifted_linear(value, axes, count, steps):
    return lax.ppermute(value, axes, [(source, source + steps) for source in range(count - steps)])


def scan_kernel(count, axes, groups, map_ref, state_ref, out_ref, own_map, own_state, send_map,
                send_state, land_map, land_state, send_sems, recv_sems):
    place = lax.axis_index(axes)
    span = map_ref.shape[0] // groups
    own_map[...] = map_ref[...]
    own_state[...] = state_ref[...]
    rounds = []
    steps = 1
    while steps < count:
        rounds.append(steps)
        steps *= 2
    rounds.append(1)
    total = len(rounds)
    inner = lax.axis_size(axes[1])

    def copies(number, group):
        other = place + rounds[number]
        heads = pl.ds(group * span, span)
        found = [
            pltpu.make_async_remote_copy(
                src_ref=send_state.at[number, heads], dst_ref=land_state.at[number, heads],
                send_sem=send_sems.at[number, group, 0], recv_sem=recv_sems.at[number, group, 0],
                device_id=(other // inner, other % inner), device_id_type=pl.DeviceIdType.MESH)
        ]
        if number < total - 2:
            found.append(
                pltpu.make_async_remote_copy(
                    src_ref=send_map.at[number, heads], dst_ref=land_map.at[number, heads],
                    send_sem=send_sems.at[number, group, 1], recv_sem=recv_sems.at[number, group, 1],
                    device_id=(other // inner, other % inner), device_id_type=pl.DeviceIdType.MESH)
            )
        return found

    def joined(number, group):
        def head(h, carry):
            mine = own_map[h]
            high = mine.astype(jnp.bfloat16)
            low = (mine - high.astype(jnp.float32)).astype(jnp.bfloat16)

            def apply(far):
                return jnp.dot(high, far, preferred_element_type=jnp.float32) + jnp.dot(
                    low, far, preferred_element_type=jnp.float32)

            own_state[h] = apply(land_state[number, h]) + own_state[h]
            if number < total - 2:
                own_map[h] = apply(land_map[number, h])
            return carry

        lax.fori_loop(group * span, group * span + span, head, 0)

    for number in range(total):
        for group in range(groups):
            heads = pl.ds(group * span, span)
            if number > 0:
                @pl.when(place >= rounds[number - 1])
                def _():
                    for copy in copies(number - 1, group):
                        copy.wait_recv()
                    joined(number - 1, group)
            send_state[number, heads] = own_state[heads].astype(jnp.bfloat16)
            if number < total - 2:
                send_map[number, heads] = own_map[heads].astype(jnp.bfloat16)

            @pl.when(place + rounds[number] < count)
            def _():
                for copy in copies(number, group):
                    copy.start()

    for group in range(groups):
        heads = pl.ds(group * span, span)

        @pl.when(place >= 1)
        def _():
            for copy in copies(total - 1, group):
                copy.wait_recv()
            out_ref[heads] = land_state[total - 1, heads].astype(jnp.float32)

        @pl.when(place < 1)
        def _():
            out_ref[heads] = jnp.zeros_like(out_ref[heads])

    for number in range(total):
        @pl.when(place + rounds[number] < count)
        def _():
            for group in range(groups):
                for copy in copies(number, group):
                    copy.wait_send()


def chained_state(state_map, state_increment, axes, count):
    heads, size, width = state_increment.shape
    rounds = 1
    while (1 << (rounds - 1)) < count:
        rounds += 1
    groups = 4
    block = pltpu.VMEM((rounds, heads, size, width), jnp.bfloat16)
    return pl.pallas_call(
        functools.partial(scan_kernel, count, axes, groups),
        out_shape=jax.ShapeDtypeStruct(state_increment.shape, jnp.float32),
        in_specs=[pl.BlockSpec(memory_space=pltpu.VMEM)] * 2,
        out_specs=pl.BlockSpec(memory_space=pltpu.VMEM),
        scratch_shapes=[
            pltpu.VMEM(state_map.shape, jnp.float32),
            pltpu.VMEM(state_increment.shape, jnp.float32),
            pltpu.VMEM((rounds, heads, size, size), jnp.bfloat16),
            block,
            pltpu.VMEM((rounds, heads, size, size), jnp.bfloat16),
            block,
            pltpu.SemaphoreType.DMA((rounds, groups, 2)),
            pltpu.SemaphoreType.DMA((rounds, groups, 2)),
        ],
        compiler_params=pltpu.CompilerParams(has_side_effects=True, vmem_limit_bytes=48 * 1024 * 1024),
    )(state_map, state_increment)


def per_device(
    tokens_in,
    expert_ids,
    route_weight,
    first_gain,
    gate_weight,
    up_weight,
    down_weight,
    second_gain,
    mixer_weight,
    gating_weight,
    filter_taps,
    decay_log,
    decay_bias,
    output_gain,
):
    n_outer = lax.axis_size("outer")
    n_inner = lax.axis_size("inner")
    n_dev = n_outer * n_inner
    tok_count, width = tokens_in.shape
    top_count = expert_ids.shape[1]
    local_experts = gate_weight.shape[0]
    experts_all = local_experts * n_dev
    capacity = max(2, 6 * tok_count * top_count // (5 * experts_all))
    rows_half = mixer_weight.shape[0] // 2
    side = lax.axis_index("outer") % 2
    own_rows = lax.dynamic_slice_in_dim(mixer_weight, side * rows_half, rows_half, axis=0)
    own_half = lax.all_gather(own_rows, "inner", axis=1, tiled=True)
    other_half = lax.ppermute(
        own_half, "outer", [(source, source ^ 1) for source in range(n_outer)]
    )
    normed_first = rms_scale(tokens_in, first_gain).astype(jnp.bfloat16)
    mix_weight = route_weight / jnp.sum(route_weight, axis=1, keepdims=True)
    flat_ids = expert_ids
    target = (
        flat_ids % local_experts * (n_dev * capacity)
        + flat_ids // local_experts * capacity
    )
    onehot = (flat_ids[:, :, None] == jnp.arange(experts_all, dtype=jnp.int32)[None, None, :]).astype(
        jnp.int32
    )
    counted = jnp.sum(onehot, axis=1)
    before = jnp.cumsum(counted, axis=0) - counted
    slot_index = jnp.sum(before[:, None, :] * onehot, axis=2)
    target = target + slot_index
    slots = jnp.arange(n_dev * local_experts * capacity, dtype=jnp.int32)
    hits = target[:, :, None] == slots[None, None, :]
    dispatch = jnp.any(hits, axis=1).astype(jnp.bfloat16)
    outgoing = jnp.einsum(
        "ts,td->sd", dispatch, normed_first, preferred_element_type=jnp.float32
    ).astype(jnp.bfloat16)
    outgoing = outgoing.reshape(local_experts, n_dev * capacity, width)
    served = run_experts(
        lax.all_to_all(outgoing, ("outer", "inner"), split_axis=1, concat_axis=1, tiled=True),
        gate_weight,
        up_weight,
        down_weight,
    )
    returned = lax.all_to_all(served, ("outer", "inner"), split_axis=1, concat_axis=1, tiled=True)
    returned = returned.reshape(-1, width)
    combine = jnp.sum(jnp.where(hits, mix_weight[:, :, None], 0.0), axis=1)
    combine_hi = combine.astype(jnp.bfloat16)
    combine_lo = (combine - combine_hi.astype(jnp.float32)).astype(jnp.bfloat16)
    mixture = jnp.dot(combine_hi, returned, preferred_element_type=jnp.float32) + jnp.dot(
        combine_lo, returned, preferred_element_type=jnp.float32
    )
    hidden_out = (tokens_in.astype(jnp.float32) + mixture).astype(jnp.bfloat16)
    normed_second = rms_scale(hidden_out, second_gain).astype(jnp.bfloat16)
    mixed = jnp.dot(
        lax.dynamic_slice_in_dim(normed_second, side * rows_half, rows_half, axis=1),
        own_half,
        preferred_element_type=jnp.float32,
    ) + jnp.dot(
        lax.dynamic_slice_in_dim(normed_second, (1 - side) * rows_half, rows_half, axis=1),
        other_half,
        preferred_element_type=jnp.float32,
    )
    projected = mixed.astype(jnp.bfloat16)
    gating = jnp.dot(normed_second, gating_weight, preferred_element_type=jnp.float32)
    taps = filter_taps.shape[0]
    rim = shifted(projected[tok_count - (taps - 1) :], ("outer", "inner"), 1)
    padded = jnp.concatenate([rim, projected], axis=0).astype(jnp.float32)
    filtered = jnp.zeros(projected.shape, jnp.float32)
    for tap_index in range(taps):
        filtered = (
            filtered
            + filter_taps[tap_index].astype(jnp.float32) * padded[tap_index : tap_index + tok_count]
        )
    filtered = jax.nn.silu(filtered)
    head_dim = output_gain.shape[0]
    value_heads = decay_log.shape[0]
    key_heads = (projected.shape[1] - value_heads * head_dim) // (2 * head_dim)
    ratio = value_heads // key_heads
    queries = unit_heads(
        filtered[:, : key_heads * head_dim].reshape(tok_count, key_heads, head_dim)
    ) * head_dim ** (-0.5)
    keys = unit_heads(
        filtered[:, key_heads * head_dim : 2 * key_heads * head_dim].reshape(
            tok_count, key_heads, head_dim
        )
    )
    values = filtered[:, 2 * key_heads * head_dim :].reshape(tok_count, value_heads, head_dim)
    queries = jnp.repeat(queries, ratio, axis=1)
    keys = jnp.repeat(keys, ratio, axis=1)
    strength = jax.nn.sigmoid(gating[:, :value_heads]).T
    log_decay = (-jnp.exp(decay_log) * jax.nn.softplus(gating[:, value_heads:] + decay_bias)).T
    cumulative = jnp.cumsum(log_decay, axis=1)
    positions = jnp.arange(tok_count)
    lower_incl = positions[:, None] >= positions[None, :]
    lower_strict = positions[:, None] > positions[None, :]
    spread = cumulative[:, :, None] - cumulative[:, None, :]
    decay_mat = jnp.where(lower_incl, jnp.exp(jnp.where(lower_incl, spread, 0.0)), 0.0)
    key_major = keys.transpose(1, 0, 2)
    query_leading = queries.transpose(1, 0, 2)
    value_major = values.transpose(1, 0, 2)
    key_inner = jnp.einsum("htd,hid->hti", key_major, key_major, precision=lax.Precision.HIGH)
    lower_part = jnp.where(lower_strict, decay_mat * key_inner, 0.0) * strength[:, :, None]
    system = lower_part + jnp.eye(tok_count, dtype=jnp.float32)
    growth = jnp.exp(cumulative)
    scaled_keys = key_major * (strength * growth)[:, :, None]
    scaled_values = value_major * strength[:, :, None]
    inverse = unit_lower_inverse(system)
    key_resolved = jnp.einsum(
        "hts,hsd->htd", inverse, scaled_keys, precision=lax.Precision.HIGH
    )
    value_resolved = jnp.einsum(
        "hts,hsd->htd", inverse, scaled_values, precision=lax.Precision.HIGH
    )
    tail = jnp.exp(cumulative[:, -1:] - cumulative)
    trailing_keys = key_major * tail[:, :, None]
    eye_heads = jnp.broadcast_to(
        jnp.eye(head_dim, dtype=jnp.float32), (value_heads, head_dim, head_dim)
    )
    state_map = growth[:, -1][:, None, None] * eye_heads - jnp.einsum(
        "htk,htj->hkj", trailing_keys, key_resolved, precision=lax.Precision.HIGH
    )
    state_increment = jnp.einsum(
        "xbe,xbz->xez", trailing_keys, value_resolved, precision=lax.Precision.HIGH
    )
    initial_state = chained_state(state_map, state_increment, ("outer", "inner"), n_dev)
    updates = value_resolved - jnp.einsum(
        "mwx,mxd->mwd", key_resolved, initial_state, precision=lax.Precision.HIGH
    )
    query_key = (
        jnp.einsum("htd,hid->hti", query_leading, key_major, precision=lax.Precision.HIGH)
        * decay_mat
    )
    carried = (
        jnp.einsum("mwx,mxd->mwd", query_leading, initial_state, precision=lax.Precision.HIGH)
        * growth[:, :, None]
    )
    attended = carried + jnp.einsum(
        "hti,hiv->htv", query_key, updates, precision=lax.Precision.HIGH
    )
    attended = attended.transpose(1, 0, 2)
    core_out = (
        rms_scale(attended, output_gain)
        .astype(jnp.bfloat16)
        .reshape(tok_count, value_heads * head_dim)
    )
    return (hidden_out, core_out)


def solution(mesh):
    return jax.shard_map(
        per_device,
        mesh=mesh,
        in_specs=(
            P(("outer", "inner"), None),
            P(("outer", "inner"), None),
            P(("outer", "inner"), None),
            P(),
            P(("outer", "inner"), None, None),
            P(("outer", "inner"), None, None),
            P(("outer", "inner"), None, None),
            P(),
            P(None, "inner"),
            P(),
            P(),
            P(),
            P(),
            P(),
        ),
        out_specs=(P(("outer", "inner"), None), P(("outer", "inner"), None)),
        check_vma=False,
    )
```

```python
import jax
import jax.numpy as jnp
from jax import lax
from jax.sharding import PartitionSpec as P
from jax.experimental import pallas as pl
from jax.experimental.pallas import tpu as pltpu
import functools


def shifted(value, axis, steps):
    count = lax.axis_size(axis)
    leading, last = (max(0, -steps), min(count, count - steps))
    return lax.ppermute(value, axis, [(source, source + steps) for source in range(leading, last)])


def prefix_2(x, axis, join, neutral):
    place = lax.axis_index(axis)
    gathered = jax.tree.map(
        lambda a, kind: lax.all_gather(a.astype(kind), axis), x, (jnp.bfloat16, jnp.bfloat16)
    )
    state = jax.tree.map(lambda a, e: jnp.zeros_like(a) + jnp.asarray(e, a.dtype), x, neutral)

    def one(lap, state):
        return join(
            state,
            jax.tree.map(
                lambda a, own: lax.dynamic_index_in_dim(a, lap, 0, False).astype(own.dtype),
                gathered,
                x,
            ),
        )

    return lax.fori_loop(0, place, one, state)


def shortened(x):

    def short(part):
        return part.astype(jnp.bfloat16) if part.dtype == jnp.float32 else part

    return jax.tree.map(short, x)


def spread_2(value, axis, source):
    kept = jnp.where(lax.axis_index(axis) == source, value, 0).astype(value.dtype)
    return lax.psum(kept, axis)


def entering(x, axis, combine, identity):
    length, place = (lax.axis_size(axis), lax.axis_index(axis))
    everything = jax.tree.map(
        lambda part, kind: lax.all_gather(part.astype(kind), axis),
        x,
        jax.tree.map(lambda a: jnp.bfloat16 if a.dtype == jnp.float32 else a.dtype, x),
    )
    start = jax.tree.map(
        lambda part, zero: jnp.broadcast_to(jnp.asarray(zero, part.dtype), part.shape), x, identity
    )

    def lap(k, before):
        reached = k < place
        new = combine(
            before, jax.tree.map(lambda part, own: part[k].astype(own.dtype), everything, x)
        )
        return jax.tree.map(lambda a, b: jnp.where(reached, a, b), new, before)

    return lax.fori_loop(0, length, lap, start)


def rms_scale(values, gain):
    wide = values.astype(jnp.float32)
    return wide * lax.rsqrt(jnp.mean(wide * wide, axis=-1, keepdims=True) + 1e-06) * gain


def unit_heads(values):
    return values * lax.rsqrt(jnp.sum(values * values, axis=-1, keepdims=True) + 1e-06)


def run_experts(piece, gate_weight, up_weight, down_weight):
    gate = jnp.einsum("esd,edf->esf", piece, gate_weight, preferred_element_type=jnp.float32)
    upper = jnp.einsum("esd,edf->esf", piece, up_weight, preferred_element_type=jnp.float32)
    hidden = (jax.nn.silu(gate) * upper).astype(jnp.bfloat16)
    return jnp.einsum(
        "esf,efd->esd", hidden, down_weight, preferred_element_type=jnp.float32
    ).astype(jnp.bfloat16)


def unit_lower_inverse(system):
    size = system.shape[-1]
    rows = lax.broadcasted_iota(jnp.int32, (size, size), 0)
    cols = lax.broadcasted_iota(jnp.int32, (size, size), 1)
    lower = system - jnp.eye(size, dtype=system.dtype)
    levels = size.bit_length() - 1

    def level(number, inverse):
        width = jnp.left_shift(1, number)
        corner = (
            (rows // (2 * width) == cols // (2 * width))
            & ((rows // width) % 2 == 1)
            & ((cols // width) % 2 == 0)
        )
        part = jnp.where(corner, lower, 0.0)
        return inverse - jnp.einsum(
            "...ij,...jk->...ik",
            inverse,
            jnp.einsum("...ij,...jk->...ik", part, inverse, precision=lax.Precision.HIGH),
            precision=lax.Precision.HIGH,
        )

    start = jnp.broadcast_to(jnp.eye(size, dtype=system.dtype), system.shape)
    return lax.fori_loop(0, levels, level, start)


def join_maps(earlier, later):
    first_map, first_state = earlier
    next_map, next_state = later
    joined_map = jnp.einsum("hij,hjk->hik", next_map, first_map, precision=lax.Precision.HIGHEST)
    joined_state = (
        jnp.einsum("hij,hjv->hiv", next_map, first_state, precision=lax.Precision.HIGHEST)
        + next_state
    )
    return (joined_map, joined_state)


def shifted_linear(value, axes, count, steps):
    return lax.ppermute(value, axes, [(source, source + steps) for source in range(count - steps)])


def scan_kernel(count, axes, groups, map_ref, state_ref, out_ref, own_map, own_state, send_map,
                send_state, land_map, land_state, send_sems, recv_sems):
    place = lax.axis_index(axes)
    span = map_ref.shape[0] // groups
    own_map[...] = map_ref[...]
    own_state[...] = state_ref[...]
    rounds = []
    steps = 1
    while steps < count:
        rounds.append(steps)
        steps *= 2
    rounds.append(1)
    total = len(rounds)
    inner = lax.axis_size(axes[1])

    def copies(number, group):
        other = place + rounds[number]
        heads = pl.ds(group * span, span)
        found = [
            pltpu.make_async_remote_copy(
                src_ref=send_state.at[number, heads], dst_ref=land_state.at[number, heads],
                send_sem=send_sems.at[number, group, 0], recv_sem=recv_sems.at[number, group, 0],
                device_id=(other // inner, other % inner), device_id_type=pl.DeviceIdType.MESH)
        ]
        if number < total - 2:
            found.append(
                pltpu.make_async_remote_copy(
                    src_ref=send_map.at[number, heads], dst_ref=land_map.at[number, heads],
                    send_sem=send_sems.at[number, group, 1], recv_sem=recv_sems.at[number, group, 1],
                    device_id=(other // inner, other % inner), device_id_type=pl.DeviceIdType.MESH)
            )
        return found

    def joined(number, group):
        def head(h, carry):
            mine = own_map[h]
            high = mine.astype(jnp.bfloat16)
            low = (mine - high.astype(jnp.float32)).astype(jnp.bfloat16)

            def apply(far):
                return jnp.dot(high, far, preferred_element_type=jnp.float32) + jnp.dot(
                    low, far, preferred_element_type=jnp.float32)

            own_state[h] = apply(land_state[number, h]) + own_state[h]
            if number < total - 2:
                own_map[h] = apply(land_map[number, h])
            return carry

        lax.fori_loop(group * span, group * span + span, head, 0)

    for number in range(total):
        for group in range(groups):
            heads = pl.ds(group * span, span)
            if number > 0:
                @pl.when(place >= rounds[number - 1])
                def _():
                    for copy in copies(number - 1, group):
                        copy.wait_recv()
                    joined(number - 1, group)
            send_state[number, heads] = own_state[heads].astype(jnp.bfloat16)
            if number < total - 2:
                send_map[number, heads] = own_map[heads].astype(jnp.bfloat16)

            @pl.when(place + rounds[number] < count)
            def _():
                for copy in copies(number, group):
                    copy.start()

    for group in range(groups):
        heads = pl.ds(group * span, span)

        @pl.when(place >= 1)
        def _():
            for copy in copies(total - 1, group):
                copy.wait_recv()
            out_ref[heads] = land_state[total - 1, heads].astype(jnp.float32)

        @pl.when(place < 1)
        def _():
            out_ref[heads] = jnp.zeros_like(out_ref[heads])

    for number in range(total):
        @pl.when(place + rounds[number] < count)
        def _():
            for group in range(groups):
                for copy in copies(number, group):
                    copy.wait_send()


def chained_state(state_map, state_increment, axes, count):
    heads, size, width = state_increment.shape
    rounds = 1
    while (1 << (rounds - 1)) < count:
        rounds += 1
    groups = 4
    block = pltpu.VMEM((rounds, heads, size, width), jnp.bfloat16)
    return pl.pallas_call(
        functools.partial(scan_kernel, count, axes, groups),
        out_shape=jax.ShapeDtypeStruct(state_increment.shape, jnp.float32),
        in_specs=[pl.BlockSpec(memory_space=pltpu.VMEM)] * 2,
        out_specs=pl.BlockSpec(memory_space=pltpu.VMEM),
        scratch_shapes=[
            pltpu.VMEM(state_map.shape, jnp.float32),
            pltpu.VMEM(state_increment.shape, jnp.float32),
            pltpu.VMEM((rounds, heads, size, size), jnp.bfloat16),
            block,
            pltpu.VMEM((rounds, heads, size, size), jnp.bfloat16),
            block,
            pltpu.SemaphoreType.DMA((rounds, groups, 2)),
            pltpu.SemaphoreType.DMA((rounds, groups, 2)),
        ],
        compiler_params=pltpu.CompilerParams(has_side_effects=True, vmem_limit_bytes=48 * 1024 * 1024),
    )(state_map, state_increment)


def per_device(
    tokens_in,
    expert_ids,
    route_weight,
    first_gain,
    gate_weight,
    up_weight,
    down_weight,
    second_gain,
    mixer_weight,
    gating_weight,
    filter_taps,
    decay_log,
    decay_bias,
    output_gain,
):
    n_outer = lax.axis_size("outer")
    n_inner = lax.axis_size("inner")
    n_dev = n_outer * n_inner
    tok_count, width = tokens_in.shape
    top_count = expert_ids.shape[1]
    local_experts = gate_weight.shape[0]
    experts_all = local_experts * n_dev
    capacity = max(2, 6 * tok_count * top_count // (5 * experts_all))
    rows_half = mixer_weight.shape[0] // 2
    side = lax.axis_index("outer") % 2
    own_rows = lax.dynamic_slice_in_dim(mixer_weight, side * rows_half, rows_half, axis=0)
    own_half = lax.all_gather(own_rows, "inner", axis=1, tiled=True)
    other_half = lax.ppermute(
        own_half, "outer", [(source, source ^ 1) for source in range(n_outer)]
    )
    normed_first = rms_scale(tokens_in, first_gain).astype(jnp.bfloat16)
    mix_weight = route_weight / jnp.sum(route_weight, axis=1, keepdims=True)
    flat_ids = expert_ids
    target = (
        flat_ids % local_experts * (n_dev * capacity)
        + flat_ids // local_experts * capacity
    )
    onehot = (flat_ids[:, :, None] == jnp.arange(experts_all, dtype=jnp.int32)[None, None, :]).astype(
        jnp.int32
    )
    counted = jnp.sum(onehot, axis=1)
    before = jnp.cumsum(counted, axis=0) - counted
    slot_index = jnp.sum(before[:, None, :] * onehot, axis=2)
    target = target + slot_index
    slots = jnp.arange(n_dev * local_experts * capacity, dtype=jnp.int32)
    hits = target[:, :, None] == slots[None, None, :]
    dispatch = jnp.any(hits, axis=1).astype(jnp.bfloat16)
    outgoing = jnp.einsum(
        "ts,td->sd", dispatch, normed_first, preferred_element_type=jnp.float32
    ).astype(jnp.bfloat16)
    outgoing = outgoing.reshape(local_experts, n_dev * capacity, width)
    served = run_experts(
        lax.all_to_all(outgoing, ("outer", "inner"), split_axis=1, concat_axis=1, tiled=True),
        gate_weight,
        up_weight,
        down_weight,
    )
    returned = lax.all_to_all(served, ("outer", "inner"), split_axis=1, concat_axis=1, tiled=True)
    combine = jnp.sum(jnp.where(hits, mix_weight[:, :, None], 0.0), axis=1)
    combine_hi = combine.astype(jnp.bfloat16)
    combine_lo = (combine - combine_hi.astype(jnp.float32)).astype(jnp.bfloat16)
    combine_hi = combine_hi.reshape(tok_count, local_experts, n_dev * capacity)
    combine_lo = combine_lo.reshape(tok_count, local_experts, n_dev * capacity)
    mixture = jnp.einsum(
        "tes,esd->td", combine_hi, returned, preferred_element_type=jnp.float32
    ) + jnp.einsum("tes,esd->td", combine_lo, returned, preferred_element_type=jnp.float32)
    hidden_out = (tokens_in.astype(jnp.float32) + mixture).astype(jnp.bfloat16)
    normed_second = rms_scale(hidden_out, second_gain).astype(jnp.bfloat16)
    mixed = jnp.dot(
        lax.dynamic_slice_in_dim(normed_second, side * rows_half, rows_half, axis=1),
        own_half,
        preferred_element_type=jnp.float32,
    ) + jnp.dot(
        lax.dynamic_slice_in_dim(normed_second, (1 - side) * rows_half, rows_half, axis=1),
        other_half,
        preferred_element_type=jnp.float32,
    )
    projected = mixed.astype(jnp.bfloat16)
    gating = jnp.dot(normed_second, gating_weight, preferred_element_type=jnp.float32)
    taps = filter_taps.shape[0]
    rim = shifted(projected[tok_count - (taps - 1) :], ("outer", "inner"), 1)
    padded = jnp.concatenate([rim, projected], axis=0).astype(jnp.float32)
    filtered = jnp.zeros(projected.shape, jnp.float32)
    for tap_index in range(taps):
        filtered = (
            filtered
            + filter_taps[tap_index].astype(jnp.float32) * padded[tap_index : tap_index + tok_count]
        )
    filtered = jax.nn.silu(filtered)
    head_dim = output_gain.shape[0]
    value_heads = decay_log.shape[0]
    key_heads = (projected.shape[1] - value_heads * head_dim) // (2 * head_dim)
    ratio = value_heads // key_heads
    queries = unit_heads(
        filtered[:, : key_heads * head_dim].reshape(tok_count, key_heads, head_dim)
    ) * head_dim ** (-0.5)
    keys = unit_heads(
        filtered[:, key_heads * head_dim : 2 * key_heads * head_dim].reshape(
            tok_count, key_heads, head_dim
        )
    )
    values = filtered[:, 2 * key_heads * head_dim :].reshape(tok_count, value_heads, head_dim)
    queries = jnp.repeat(queries, ratio, axis=1)
    keys = jnp.repeat(keys, ratio, axis=1)
    strength = jax.nn.sigmoid(gating[:, :value_heads]).T
    log_decay = (-jnp.exp(decay_log) * jax.nn.softplus(gating[:, value_heads:] + decay_bias)).T
    cumulative = jnp.cumsum(log_decay, axis=1)
    positions = jnp.arange(tok_count)
    lower_incl = positions[:, None] >= positions[None, :]
    lower_strict = positions[:, None] > positions[None, :]
    spread = cumulative[:, :, None] - cumulative[:, None, :]
    decay_mat = jnp.where(lower_incl, jnp.exp(jnp.where(lower_incl, spread, 0.0)), 0.0)
    key_major = keys.transpose(1, 0, 2)
    query_leading = queries.transpose(1, 0, 2)
    value_major = values.transpose(1, 0, 2)
    key_inner = jnp.einsum("htd,hid->hti", key_major, key_major, precision=lax.Precision.HIGH)
    lower_part = jnp.where(lower_strict, decay_mat * key_inner, 0.0) * strength[:, :, None]
    system = lower_part + jnp.eye(tok_count, dtype=jnp.float32)
    growth = jnp.exp(cumulative)
    scaled_keys = key_major * (strength * growth)[:, :, None]
    scaled_values = value_major * strength[:, :, None]
    inverse = unit_lower_inverse(system)
    key_resolved = jnp.einsum(
        "hts,hsd->htd", inverse, scaled_keys, precision=lax.Precision.HIGH
    )
    value_resolved = jnp.einsum(
        "hts,hsd->htd", inverse, scaled_values, precision=lax.Precision.HIGH
    )
    tail = jnp.exp(cumulative[:, -1:] - cumulative)
    trailing_keys = key_major * tail[:, :, None]
    eye_heads = jnp.broadcast_to(
        jnp.eye(head_dim, dtype=jnp.float32), (value_heads, head_dim, head_dim)
    )
    state_map = growth[:, -1][:, None, None] * eye_heads - jnp.einsum(
        "htk,htj->hkj", trailing_keys, key_resolved, precision=lax.Precision.HIGH
    )
    state_increment = jnp.einsum(
        "xbe,xbz->xez", trailing_keys, value_resolved, precision=lax.Precision.HIGH
    )
    initial_state = chained_state(state_map, state_increment, ("outer", "inner"), n_dev)
    updates = value_resolved - jnp.einsum(
        "mwx,mxd->mwd", key_resolved, initial_state, precision=lax.Precision.HIGH
    )
    query_key = (
        jnp.einsum("htd,hid->hti", query_leading, key_major, precision=lax.Precision.HIGH)
        * decay_mat
    )
    carried = (
        jnp.einsum("mwx,mxd->mwd", query_leading, initial_state, precision=lax.Precision.HIGH)
        * growth[:, :, None]
    )
    attended = carried + jnp.einsum(
        "hti,hiv->htv", query_key, updates, precision=lax.Precision.HIGH
    )
    attended = attended.transpose(1, 0, 2)
    core_out = (
        rms_scale(attended, output_gain)
        .astype(jnp.bfloat16)
        .reshape(tok_count, value_heads * head_dim)
    )
    return (hidden_out, core_out)


def solution(mesh):
    return jax.shard_map(
        per_device,
        mesh=mesh,
        in_specs=(
            P(("outer", "inner"), None),
            P(("outer", "inner"), None),
            P(("outer", "inner"), None),
            P(),
            P(("outer", "inner"), None, None),
            P(("outer", "inner"), None, None),
            P(("outer", "inner"), None, None),
            P(),
            P(None, "inner"),
            P(),
            P(),
            P(),
            P(),
            P(),
        ),
        out_specs=(P(("outer", "inner"), None), P(("outer", "inner"), None)),
        check_vma=False,
    )
```

```python
import jax
import jax.numpy as jnp
from jax import lax
from jax.sharding import PartitionSpec as P
from jax.experimental import pallas as pl
from jax.experimental.pallas import tpu as pltpu
import functools


def shifted(value, axis, steps):
    count = lax.axis_size(axis)
    leading, last = (max(0, -steps), min(count, count - steps))
    return lax.ppermute(value, axis, [(source, source + steps) for source in range(leading, last)])


def prefix_2(x, axis, join, neutral):
    place = lax.axis_index(axis)
    gathered = jax.tree.map(
        lambda a, kind: lax.all_gather(a.astype(kind), axis), x, (jnp.bfloat16, jnp.bfloat16)
    )
    state = jax.tree.map(lambda a, e: jnp.zeros_like(a) + jnp.asarray(e, a.dtype), x, neutral)

    def one(lap, state):
        return join(
            state,
            jax.tree.map(
                lambda a, own: lax.dynamic_index_in_dim(a, lap, 0, False).astype(own.dtype),
                gathered,
                x,
            ),
        )

    return lax.fori_loop(0, place, one, state)


def shortened(x):

    def short(part):
        return part.astype(jnp.bfloat16) if part.dtype == jnp.float32 else part

    return jax.tree.map(short, x)


def spread_2(value, axis, source):
    kept = jnp.where(lax.axis_index(axis) == source, value, 0).astype(value.dtype)
    return lax.psum(kept, axis)


def entering(x, axis, combine, identity):
    length, place = (lax.axis_size(axis), lax.axis_index(axis))
    everything = jax.tree.map(
        lambda part, kind: lax.all_gather(part.astype(kind), axis),
        x,
        jax.tree.map(lambda a: jnp.bfloat16 if a.dtype == jnp.float32 else a.dtype, x),
    )
    start = jax.tree.map(
        lambda part, zero: jnp.broadcast_to(jnp.asarray(zero, part.dtype), part.shape), x, identity
    )

    def lap(k, before):
        reached = k < place
        new = combine(
            before, jax.tree.map(lambda part, own: part[k].astype(own.dtype), everything, x)
        )
        return jax.tree.map(lambda a, b: jnp.where(reached, a, b), new, before)

    return lax.fori_loop(0, length, lap, start)


def rms_scale(values, gain):
    wide = values.astype(jnp.float32)
    return wide * lax.rsqrt(jnp.mean(wide * wide, axis=-1, keepdims=True) + 1e-06) * gain


def unit_heads(values):
    return values * lax.rsqrt(jnp.sum(values * values, axis=-1, keepdims=True) + 1e-06)


def run_experts(piece, gate_weight, up_weight, down_weight):
    gate = jnp.einsum("esd,edf->esf", piece, gate_weight, preferred_element_type=jnp.float32)
    upper = jnp.einsum("esd,edf->esf", piece, up_weight, preferred_element_type=jnp.float32)
    hidden = (jax.nn.silu(gate) * upper).astype(jnp.bfloat16)
    return jnp.einsum(
        "esf,efd->esd", hidden, down_weight, preferred_element_type=jnp.float32
    ).astype(jnp.bfloat16)


def unit_lower_inverse(system):
    size = system.shape[-1]
    rows = lax.broadcasted_iota(jnp.int32, (size, size), 0)
    cols = lax.broadcasted_iota(jnp.int32, (size, size), 1)
    lower = system - jnp.eye(size, dtype=system.dtype)
    levels = size.bit_length() - 1

    def level(number, inverse):
        width = jnp.left_shift(1, number)
        corner = (
            (rows // (2 * width) == cols // (2 * width))
            & ((rows // width) % 2 == 1)
            & ((cols // width) % 2 == 0)
        )
        part = jnp.where(corner, lower, 0.0)
        return inverse - jnp.einsum(
            "...ij,...jk->...ik",
            inverse,
            jnp.einsum("...ij,...jk->...ik", part, inverse, precision=lax.Precision.HIGH),
            precision=lax.Precision.HIGH,
        )

    first = ((rows // 2 == cols // 2) & (rows % 2 == 1) & (cols % 2 == 0))
    start = jnp.eye(size, dtype=system.dtype) - jnp.where(first, lower, 0.0)
    return lax.fori_loop(1, levels, level, start)


def join_maps(earlier, later):
    first_map, first_state = earlier
    next_map, next_state = later
    joined_map = jnp.einsum("hij,hjk->hik", next_map, first_map, precision=lax.Precision.HIGHEST)
    joined_state = (
        jnp.einsum("hij,hjv->hiv", next_map, first_state, precision=lax.Precision.HIGHEST)
        + next_state
    )
    return (joined_map, joined_state)


def shifted_linear(value, axes, count, steps):
    return lax.ppermute(value, axes, [(source, source + steps) for source in range(count - steps)])


def scan_kernel(count, axes, groups, map_ref, state_ref, out_ref, own_map, own_state, send_map,
                send_state, land_map, land_state, send_sems, recv_sems):
    place = lax.axis_index(axes)
    span = map_ref.shape[0] // groups
    own_map[...] = map_ref[...]
    own_state[...] = state_ref[...]
    rounds = []
    steps = 1
    while steps < count:
        rounds.append(steps)
        steps *= 2
    rounds.append(1)
    total = len(rounds)
    inner = lax.axis_size(axes[1])

    def copies(number, group):
        other = place + rounds[number]
        heads = pl.ds(group * span, span)
        found = [
            pltpu.make_async_remote_copy(
                src_ref=send_state.at[number, heads], dst_ref=land_state.at[number, heads],
                send_sem=send_sems.at[number, group, 0], recv_sem=recv_sems.at[number, group, 0],
                device_id=(other // inner, other % inner), device_id_type=pl.DeviceIdType.MESH)
        ]
        if number < total - 2:
            found.append(
                pltpu.make_async_remote_copy(
                    src_ref=send_map.at[number, heads], dst_ref=land_map.at[number, heads],
                    send_sem=send_sems.at[number, group, 1], recv_sem=recv_sems.at[number, group, 1],
                    device_id=(other // inner, other % inner), device_id_type=pl.DeviceIdType.MESH)
            )
        return found

    def joined(number, group):
        def head(h, carry):
            mine = own_map[h]
            high = mine.astype(jnp.bfloat16)
            low = (mine - high.astype(jnp.float32)).astype(jnp.bfloat16)

            def apply(far):
                return jnp.dot(high, far, preferred_element_type=jnp.float32) + jnp.dot(
                    low, far, preferred_element_type=jnp.float32)

            own_state[h] = apply(land_state[number, h]) + own_state[h]
            if number < total - 2:
                own_map[h] = apply(land_map[number, h])
            return carry

        lax.fori_loop(group * span, group * span + span, head, 0)

    for number in range(total):
        for group in range(groups):
            heads = pl.ds(group * span, span)
            if number > 0:
                @pl.when(place >= rounds[number - 1])
                def _():
                    for copy in copies(number - 1, group):
                        copy.wait_recv()
                    joined(number - 1, group)
            send_state[number, heads] = own_state[heads].astype(jnp.bfloat16)
            if number < total - 2:
                send_map[number, heads] = own_map[heads].astype(jnp.bfloat16)

            @pl.when(place + rounds[number] < count)
            def _():
                for copy in copies(number, group):
                    copy.start()

    for group in range(groups):
        heads = pl.ds(group * span, span)

        @pl.when(place >= 1)
        def _():
            for copy in copies(total - 1, group):
                copy.wait_recv()
            out_ref[heads] = land_state[total - 1, heads].astype(jnp.float32)

        @pl.when(place < 1)
        def _():
            out_ref[heads] = jnp.zeros_like(out_ref[heads])

    for number in range(total):
        @pl.when(place + rounds[number] < count)
        def _():
            for group in range(groups):
                for copy in copies(number, group):
                    copy.wait_send()


def chained_state(state_map, state_increment, axes, count):
    heads, size, width = state_increment.shape
    rounds = 1
    while (1 << (rounds - 1)) < count:
        rounds += 1
    groups = 4
    block = pltpu.VMEM((rounds, heads, size, width), jnp.bfloat16)
    return pl.pallas_call(
        functools.partial(scan_kernel, count, axes, groups),
        out_shape=jax.ShapeDtypeStruct(state_increment.shape, jnp.float32),
        in_specs=[pl.BlockSpec(memory_space=pltpu.VMEM)] * 2,
        out_specs=pl.BlockSpec(memory_space=pltpu.VMEM),
        scratch_shapes=[
            pltpu.VMEM(state_map.shape, jnp.float32),
            pltpu.VMEM(state_increment.shape, jnp.float32),
            pltpu.VMEM((rounds, heads, size, size), jnp.bfloat16),
            block,
            pltpu.VMEM((rounds, heads, size, size), jnp.bfloat16),
            block,
            pltpu.SemaphoreType.DMA((rounds, groups, 2)),
            pltpu.SemaphoreType.DMA((rounds, groups, 2)),
        ],
        compiler_params=pltpu.CompilerParams(has_side_effects=True, vmem_limit_bytes=48 * 1024 * 1024),
    )(state_map, state_increment)


def per_device(
    tokens_in,
    expert_ids,
    route_weight,
    first_gain,
    gate_weight,
    up_weight,
    down_weight,
    second_gain,
    mixer_weight,
    gating_weight,
    filter_taps,
    decay_log,
    decay_bias,
    output_gain,
):
    n_outer = lax.axis_size("outer")
    n_inner = lax.axis_size("inner")
    n_dev = n_outer * n_inner
    tok_count, width = tokens_in.shape
    top_count = expert_ids.shape[1]
    local_experts = gate_weight.shape[0]
    experts_all = local_experts * n_dev
    capacity = max(2, 6 * tok_count * top_count // (5 * experts_all))
    rows_half = mixer_weight.shape[0] // 2
    side = lax.axis_index("outer") % 2
    own_rows = lax.dynamic_slice_in_dim(mixer_weight, side * rows_half, rows_half, axis=0)
    own_half = lax.all_gather(own_rows, "inner", axis=1, tiled=True)
    other_half = lax.ppermute(
        own_half, "outer", [(source, source ^ 1) for source in range(n_outer)]
    )
    normed_first = rms_scale(tokens_in, first_gain).astype(jnp.bfloat16)
    mix_weight = route_weight / jnp.sum(route_weight, axis=1, keepdims=True)
    flat_ids = expert_ids
    target = (
        flat_ids % local_experts * (n_dev * capacity)
        + flat_ids // local_experts * capacity
    )
    onehot = (flat_ids[:, :, None] == jnp.arange(experts_all, dtype=jnp.int32)[None, None, :]).astype(
        jnp.int32
    )
    counted = jnp.sum(onehot, axis=1)
    before = jnp.cumsum(counted, axis=0) - counted
    slot_index = jnp.sum(before[:, None, :] * onehot, axis=2)
    target = target + slot_index
    slots = jnp.arange(n_dev * local_experts * capacity, dtype=jnp.int32)
    hits = target[:, :, None] == slots[None, None, :]
    dispatch = jnp.any(hits, axis=1).astype(jnp.bfloat16)
    outgoing = jnp.einsum(
        "ts,td->sd", dispatch, normed_first, preferred_element_type=jnp.float32
    ).astype(jnp.bfloat16)
    outgoing = outgoing.reshape(local_experts, n_dev * capacity, width)
    served = run_experts(
        lax.all_to_all(outgoing, ("outer", "inner"), split_axis=1, concat_axis=1, tiled=True),
        gate_weight,
        up_weight,
        down_weight,
    )
    returned = lax.all_to_all(served, ("outer", "inner"), split_axis=1, concat_axis=1, tiled=True)
    returned = returned.reshape(-1, width)
    combine = jnp.sum(jnp.where(hits, mix_weight[:, :, None], 0.0), axis=1)
    combine_hi = combine.astype(jnp.bfloat16)
    combine_lo = (combine - combine_hi.astype(jnp.float32)).astype(jnp.bfloat16)
    mixture = jnp.dot(combine_hi, returned, preferred_element_type=jnp.float32) + jnp.dot(
        combine_lo, returned, preferred_element_type=jnp.float32
    )
    hidden_out = (tokens_in.astype(jnp.float32) + mixture).astype(jnp.bfloat16)
    normed_second = rms_scale(hidden_out, second_gain).astype(jnp.bfloat16)
    mixed = jnp.dot(
        lax.dynamic_slice_in_dim(normed_second, side * rows_half, rows_half, axis=1),
        own_half,
        preferred_element_type=jnp.float32,
    ) + jnp.dot(
        lax.dynamic_slice_in_dim(normed_second, (1 - side) * rows_half, rows_half, axis=1),
        other_half,
        preferred_element_type=jnp.float32,
    )
    projected = mixed.astype(jnp.bfloat16)
    gating = jnp.dot(normed_second, gating_weight, preferred_element_type=jnp.float32)
    taps = filter_taps.shape[0]
    rim = shifted(projected[tok_count - (taps - 1) :], ("outer", "inner"), 1)
    padded = jnp.concatenate([rim, projected], axis=0).astype(jnp.float32)
    filtered = jnp.zeros(projected.shape, jnp.float32)
    for tap_index in range(taps):
        filtered = (
            filtered
            + filter_taps[tap_index].astype(jnp.float32) * padded[tap_index : tap_index + tok_count]
        )
    filtered = jax.nn.silu(filtered)
    head_dim = output_gain.shape[0]
    value_heads = decay_log.shape[0]
    key_heads = (projected.shape[1] - value_heads * head_dim) // (2 * head_dim)
    ratio = value_heads // key_heads
    queries = unit_heads(
        filtered[:, : key_heads * head_dim].reshape(tok_count, key_heads, head_dim)
    ) * head_dim ** (-0.5)
    keys = unit_heads(
        filtered[:, key_heads * head_dim : 2 * key_heads * head_dim].reshape(
            tok_count, key_heads, head_dim
        )
    )
    values = filtered[:, 2 * key_heads * head_dim :].reshape(tok_count, value_heads, head_dim)
    queries = jnp.repeat(queries, ratio, axis=1)
    keys = jnp.repeat(keys, ratio, axis=1)
    strength = jax.nn.sigmoid(gating[:, :value_heads]).T
    log_decay = (-jnp.exp(decay_log) * jax.nn.softplus(gating[:, value_heads:] + decay_bias)).T
    cumulative = jnp.cumsum(log_decay, axis=1)
    positions = jnp.arange(tok_count)
    lower_incl = positions[:, None] >= positions[None, :]
    lower_strict = positions[:, None] > positions[None, :]
    spread = cumulative[:, :, None] - cumulative[:, None, :]
    decay_mat = jnp.where(lower_incl, jnp.exp(jnp.where(lower_incl, spread, 0.0)), 0.0)
    key_major = keys.transpose(1, 0, 2)
    query_leading = queries.transpose(1, 0, 2)
    value_major = values.transpose(1, 0, 2)
    key_inner = jnp.einsum("htd,hid->hti", key_major, key_major, precision=lax.Precision.HIGH)
    lower_part = jnp.where(lower_strict, decay_mat * key_inner, 0.0) * strength[:, :, None]
    system = lower_part + jnp.eye(tok_count, dtype=jnp.float32)
    growth = jnp.exp(cumulative)
    scaled_keys = key_major * (strength * growth)[:, :, None]
    scaled_values = value_major * strength[:, :, None]
    inverse = unit_lower_inverse(system)
    key_resolved = jnp.einsum(
        "hts,hsd->htd", inverse, scaled_keys, precision=lax.Precision.HIGH
    )
    value_resolved = jnp.einsum(
        "hts,hsd->htd", inverse, scaled_values, precision=lax.Precision.HIGH
    )
    tail = jnp.exp(cumulative[:, -1:] - cumulative)
    trailing_keys = key_major * tail[:, :, None]
    eye_heads = jnp.broadcast_to(
        jnp.eye(head_dim, dtype=jnp.float32), (value_heads, head_dim, head_dim)
    )
    state_map = growth[:, -1][:, None, None] * eye_heads - jnp.einsum(
        "htk,htj->hkj", trailing_keys, key_resolved, precision=lax.Precision.HIGH
    )
    state_increment = jnp.einsum(
        "xbe,xbz->xez", trailing_keys, value_resolved, precision=lax.Precision.HIGH
    )
    initial_state = chained_state(state_map, state_increment, ("outer", "inner"), n_dev)
    updates = value_resolved - jnp.einsum(
        "mwx,mxd->mwd", key_resolved, initial_state, precision=lax.Precision.HIGH
    )
    query_key = (
        jnp.einsum("htd,hid->hti", query_leading, key_major, precision=lax.Precision.HIGH)
        * decay_mat
    )
    carried = (
        jnp.einsum("mwx,mxd->mwd", query_leading, initial_state, precision=lax.Precision.HIGH)
        * growth[:, :, None]
    )
    attended = carried + jnp.einsum(
        "hti,hiv->htv", query_key, updates, precision=lax.Precision.HIGH
    )
    attended = attended.transpose(1, 0, 2)
    core_out = (
        rms_scale(attended, output_gain)
        .astype(jnp.bfloat16)
        .reshape(tok_count, value_heads * head_dim)
    )
    return (hidden_out, core_out)


def solution(mesh):
    return jax.shard_map(
        per_device,
        mesh=mesh,
        in_specs=(
            P(("outer", "inner"), None),
            P(("outer", "inner"), None),
            P(("outer", "inner"), None),
            P(),
            P(("outer", "inner"), None, None),
            P(("outer", "inner"), None, None),
            P(("outer", "inner"), None, None),
            P(),
            P(None, "inner"),
            P(),
            P(),
            P(),
            P(),
            P(),
        ),
        out_specs=(P(("outer", "inner"), None), P(("outer", "inner"), None)),
        check_vma=False,
    )
```

```python
import jax
import jax.numpy as jnp
from jax import lax
from jax.sharding import PartitionSpec as P
from jax.experimental import pallas as pl
from jax.experimental.pallas import tpu as pltpu
import functools


def shifted(value, axis, steps):
    count = lax.axis_size(axis)
    leading, last = (max(0, -steps), min(count, count - steps))
    return lax.ppermute(value, axis, [(source, source + steps) for source in range(leading, last)])


def prefix_2(x, axis, join, neutral):
    place = lax.axis_index(axis)
    gathered = jax.tree.map(
        lambda a, kind: lax.all_gather(a.astype(kind), axis), x, (jnp.bfloat16, jnp.bfloat16)
    )
    state = jax.tree.map(lambda a, e: jnp.zeros_like(a) + jnp.asarray(e, a.dtype), x, neutral)

    def one(lap, state):
        return join(
            state,
            jax.tree.map(
                lambda a, own: lax.dynamic_index_in_dim(a, lap, 0, False).astype(own.dtype),
                gathered,
                x,
            ),
        )

    return lax.fori_loop(0, place, one, state)


def shortened(x):

    def short(part):
        return part.astype(jnp.bfloat16) if part.dtype == jnp.float32 else part

    return jax.tree.map(short, x)


def spread_2(value, axis, source):
    kept = jnp.where(lax.axis_index(axis) == source, value, 0).astype(value.dtype)
    return lax.psum(kept, axis)


def entering(x, axis, combine, identity):
    length, place = (lax.axis_size(axis), lax.axis_index(axis))
    everything = jax.tree.map(
        lambda part, kind: lax.all_gather(part.astype(kind), axis),
        x,
        jax.tree.map(lambda a: jnp.bfloat16 if a.dtype == jnp.float32 else a.dtype, x),
    )
    start = jax.tree.map(
        lambda part, zero: jnp.broadcast_to(jnp.asarray(zero, part.dtype), part.shape), x, identity
    )

    def lap(k, before):
        reached = k < place
        new = combine(
            before, jax.tree.map(lambda part, own: part[k].astype(own.dtype), everything, x)
        )
        return jax.tree.map(lambda a, b: jnp.where(reached, a, b), new, before)

    return lax.fori_loop(0, length, lap, start)


def rms_scale(values, gain):
    wide = values.astype(jnp.float32)
    return wide * lax.rsqrt(jnp.mean(wide * wide, axis=-1, keepdims=True) + 1e-06) * gain


def unit_heads(values):
    return values * lax.rsqrt(jnp.sum(values * values, axis=-1, keepdims=True) + 1e-06)


def run_experts(piece, gate_weight, up_weight, down_weight):
    gate = jnp.einsum("esd,edf->esf", piece, gate_weight, preferred_element_type=jnp.float32)
    upper = jnp.einsum("esd,edf->esf", piece, up_weight, preferred_element_type=jnp.float32)
    hidden = (jax.nn.silu(gate) * upper).astype(jnp.bfloat16)
    return jnp.einsum(
        "esf,efd->esd", hidden, down_weight, preferred_element_type=jnp.float32
    ).astype(jnp.bfloat16)


def unit_lower_inverse(system):
    size = system.shape[-1]
    rows = lax.broadcasted_iota(jnp.int32, (size, size), 0)
    cols = lax.broadcasted_iota(jnp.int32, (size, size), 1)
    lower = system - jnp.eye(size, dtype=system.dtype)
    levels = size.bit_length() - 1

    def level(number, inverse):
        width = jnp.left_shift(1, number)
        corner = (
            (rows // (2 * width) == cols // (2 * width))
            & ((rows // width) % 2 == 1)
            & ((cols // width) % 2 == 0)
        )
        part = jnp.where(corner, lower, 0.0)
        return inverse - jnp.einsum(
            "...ij,...jk->...ik",
            inverse,
            jnp.einsum("...ij,...jk->...ik", part, inverse, precision=lax.Precision.HIGH),
            precision=lax.Precision.HIGH,
        )

    first = ((rows // 2 == cols // 2) & (rows % 2 == 1) & (cols % 2 == 0))
    start = jnp.eye(size, dtype=system.dtype) - jnp.where(first, lower, 0.0)
    return lax.fori_loop(1, levels, level, start)


def join_maps(earlier, later):
    first_map, first_state = earlier
    next_map, next_state = later
    joined_map = jnp.einsum("hij,hjk->hik", next_map, first_map, precision=lax.Precision.HIGHEST)
    joined_state = (
        jnp.einsum("hij,hjv->hiv", next_map, first_state, precision=lax.Precision.HIGHEST)
        + next_state
    )
    return (joined_map, joined_state)


def shifted_linear(value, axes, count, steps):
    return lax.ppermute(value, axes, [(source, source + steps) for source in range(count - steps)])


def scan_kernel(count, axes, groups, map_ref, state_ref, out_ref, own_map, own_state, send_map,
                send_state, land_map, land_state, send_sems, recv_sems):
    place = lax.axis_index(axes)
    span = map_ref.shape[0] // groups
    own_map[...] = map_ref[...]
    own_state[...] = state_ref[...]
    rounds = []
    steps = 1
    while steps < count:
        rounds.append(steps)
        steps *= 2
    rounds.append(1)
    total = len(rounds)
    inner = lax.axis_size(axes[1])

    def copies(number, group):
        other = place + rounds[number]
        heads = pl.ds(group * span, span)
        found = [
            pltpu.make_async_remote_copy(
                src_ref=send_state.at[number, heads], dst_ref=land_state.at[number, heads],
                send_sem=send_sems.at[number, group, 0], recv_sem=recv_sems.at[number, group, 0],
                device_id=(other // inner, other % inner), device_id_type=pl.DeviceIdType.MESH)
        ]
        if number < total - 2:
            found.append(
                pltpu.make_async_remote_copy(
                    src_ref=send_map.at[number, heads], dst_ref=land_map.at[number, heads],
                    send_sem=send_sems.at[number, group, 1], recv_sem=recv_sems.at[number, group, 1],
                    device_id=(other // inner, other % inner), device_id_type=pl.DeviceIdType.MESH)
            )
        return found

    def joined(number, group):
        def head(h, carry):
            mine = own_map[h]
            high = mine.astype(jnp.bfloat16)
            low = (mine - high.astype(jnp.float32)).astype(jnp.bfloat16)

            def apply(far):
                return jnp.dot(high, far, preferred_element_type=jnp.float32) + jnp.dot(
                    low, far, preferred_element_type=jnp.float32)

            own_state[h] = apply(land_state[number, h]) + own_state[h]
            if number < total - 2:
                own_map[h] = apply(land_map[number, h])
            return carry

        lax.fori_loop(group * span, group * span + span, head, 0)

    for number in range(total):
        for group in range(groups):
            heads = pl.ds(group * span, span)
            if number > 0:
                @pl.when(place >= rounds[number - 1])
                def _():
                    for copy in copies(number - 1, group):
                        copy.wait_recv()
                    joined(number - 1, group)
            send_state[number, heads] = own_state[heads].astype(jnp.bfloat16)
            if number < total - 2:
                send_map[number, heads] = own_map[heads].astype(jnp.bfloat16)

            @pl.when(place + rounds[number] < count)
            def _():
                for copy in copies(number, group):
                    copy.start()

    for group in range(groups):
        heads = pl.ds(group * span, span)

        @pl.when(place >= 1)
        def _():
            for copy in copies(total - 1, group):
                copy.wait_recv()
            out_ref[heads] = land_state[total - 1, heads].astype(jnp.float32)

        @pl.when(place < 1)
        def _():
            out_ref[heads] = jnp.zeros_like(out_ref[heads])

    for number in range(total):
        @pl.when(place + rounds[number] < count)
        def _():
            for group in range(groups):
                for copy in copies(number, group):
                    copy.wait_send()


def chained_state(state_map, state_increment, axes, count):
    heads, size, width = state_increment.shape
    rounds = 1
    while (1 << (rounds - 1)) < count:
        rounds += 1
    groups = 4
    block = pltpu.VMEM((rounds, heads, size, width), jnp.bfloat16)
    return pl.pallas_call(
        functools.partial(scan_kernel, count, axes, groups),
        out_shape=jax.ShapeDtypeStruct(state_increment.shape, jnp.float32),
        in_specs=[pl.BlockSpec(memory_space=pltpu.VMEM)] * 2,
        out_specs=pl.BlockSpec(memory_space=pltpu.VMEM),
        scratch_shapes=[
            pltpu.VMEM(state_map.shape, jnp.float32),
            pltpu.VMEM(state_increment.shape, jnp.float32),
            pltpu.VMEM((rounds, heads, size, size), jnp.bfloat16),
            block,
            pltpu.VMEM((rounds, heads, size, size), jnp.bfloat16),
            block,
            pltpu.SemaphoreType.DMA((rounds, groups, 2)),
            pltpu.SemaphoreType.DMA((rounds, groups, 2)),
        ],
        compiler_params=pltpu.CompilerParams(has_side_effects=True, vmem_limit_bytes=48 * 1024 * 1024),
    )(state_map, state_increment)


def per_device(
    tokens_in,
    expert_ids,
    route_weight,
    first_gain,
    gate_weight,
    up_weight,
    down_weight,
    second_gain,
    mixer_weight,
    gating_weight,
    filter_taps,
    decay_log,
    decay_bias,
    output_gain,
):
    n_outer = lax.axis_size("outer")
    n_inner = lax.axis_size("inner")
    n_dev = n_outer * n_inner
    tok_count, width = tokens_in.shape
    top_count = expert_ids.shape[1]
    local_experts = gate_weight.shape[0]
    experts_all = local_experts * n_dev
    capacity = max(2, 6 * tok_count * top_count // (5 * experts_all))
    rows_half = mixer_weight.shape[0] // 2
    side = lax.axis_index("outer") % 2
    own_rows = lax.dynamic_slice_in_dim(mixer_weight, side * rows_half, rows_half, axis=0)
    own_half = lax.all_gather(own_rows, "inner", axis=1, tiled=True)
    other_half = lax.ppermute(
        own_half, "outer", [(source, source ^ 1) for source in range(n_outer)]
    )
    normed_first = rms_scale(tokens_in, first_gain).astype(jnp.bfloat16)
    mix_weight = route_weight / jnp.sum(route_weight, axis=1, keepdims=True)
    flat_ids = expert_ids
    target = (
        flat_ids % local_experts * (n_dev * capacity)
        + flat_ids // local_experts * capacity
    )
    onehot = (flat_ids[:, :, None] == jnp.arange(experts_all, dtype=jnp.int32)[None, None, :]).astype(
        jnp.int32
    )
    counted = jnp.sum(onehot, axis=1)
    before = jnp.cumsum(counted, axis=0) - counted
    slot_index = jnp.sum(before[:, None, :] * onehot, axis=2)
    target = target + slot_index
    slots = jnp.arange(n_dev * local_experts * capacity, dtype=jnp.int32)
    hits = target[:, :, None] == slots[None, None, :]
    dispatch = jnp.any(hits, axis=1).astype(jnp.bfloat16)
    outgoing = jnp.einsum(
        "ts,td->sd", dispatch, normed_first, preferred_element_type=jnp.float32
    ).astype(jnp.bfloat16)
    outgoing = outgoing.reshape(local_experts, n_dev * capacity, width)
    served = run_experts(
        lax.all_to_all(outgoing, ("outer", "inner"), split_axis=1, concat_axis=1, tiled=True),
        gate_weight,
        up_weight,
        down_weight,
    )
    returned = lax.all_to_all(served, ("outer", "inner"), split_axis=1, concat_axis=1, tiled=True)
    returned = returned.reshape(-1, width)
    combine = jnp.sum(jnp.where(hits, mix_weight[:, :, None], 0.0), axis=1)
    combine_hi = combine.astype(jnp.bfloat16)
    combine_lo = (combine - combine_hi.astype(jnp.float32)).astype(jnp.bfloat16)
    mixture = jnp.dot(combine_hi, returned, preferred_element_type=jnp.float32) + jnp.dot(
        combine_lo, returned, preferred_element_type=jnp.float32
    )
    hidden_out = (tokens_in.astype(jnp.float32) + mixture).astype(jnp.bfloat16)
    normed_second = rms_scale(hidden_out, second_gain).astype(jnp.bfloat16)
    mixed = jnp.dot(
        lax.dynamic_slice_in_dim(normed_second, side * rows_half, rows_half, axis=1),
        own_half,
        preferred_element_type=jnp.float32,
    ) + jnp.dot(
        lax.dynamic_slice_in_dim(normed_second, (1 - side) * rows_half, rows_half, axis=1),
        other_half,
        preferred_element_type=jnp.float32,
    )
    projected = mixed.astype(jnp.bfloat16)
    gating = jnp.dot(normed_second, gating_weight, preferred_element_type=jnp.float32)
    taps = filter_taps.shape[0]
    rim = shifted(projected[tok_count - (taps - 1) :], ("outer", "inner"), 1)
    padded = jnp.concatenate([rim, projected], axis=0).astype(jnp.float32)
    filtered = jnp.zeros(projected.shape, jnp.float32)
    for tap_index in range(taps):
        filtered = (
            filtered
            + filter_taps[tap_index].astype(jnp.float32) * padded[tap_index : tap_index + tok_count]
        )
    filtered = jax.nn.silu(filtered)
    head_dim = output_gain.shape[0]
    value_heads = decay_log.shape[0]
    key_heads = (projected.shape[1] - value_heads * head_dim) // (2 * head_dim)
    ratio = value_heads // key_heads
    queries = unit_heads(
        filtered[:, : key_heads * head_dim].reshape(tok_count, key_heads, head_dim)
    ) * head_dim ** (-0.5)
    keys = unit_heads(
        filtered[:, key_heads * head_dim : 2 * key_heads * head_dim].reshape(
            tok_count, key_heads, head_dim
        )
    )
    values = filtered[:, 2 * key_heads * head_dim :].reshape(tok_count, value_heads, head_dim)
    key_heads_major = keys.transpose(1, 0, 2)
    key_pairs = jnp.repeat(
        jnp.einsum("htd,hsd->hts", key_heads_major, key_heads_major, precision=lax.Precision.HIGH),
        ratio,
        axis=0,
    )
    query_pairs = jnp.repeat(
        jnp.einsum(
            "htd,hsd->hts", queries.transpose(1, 0, 2), key_heads_major, precision=lax.Precision.HIGH
        ),
        ratio,
        axis=0,
    )
    queries = jnp.repeat(queries, ratio, axis=1)
    keys = jnp.repeat(keys, ratio, axis=1)
    strength = jax.nn.sigmoid(gating[:, :value_heads]).T
    log_decay = (-jnp.exp(decay_log) * jax.nn.softplus(gating[:, value_heads:] + decay_bias)).T
    cumulative = jnp.cumsum(log_decay, axis=1)
    positions = jnp.arange(tok_count)
    lower_incl = positions[:, None] >= positions[None, :]
    lower_strict = positions[:, None] > positions[None, :]
    spread = cumulative[:, :, None] - cumulative[:, None, :]
    decay_mat = jnp.where(lower_incl, jnp.exp(jnp.where(lower_incl, spread, 0.0)), 0.0)
    key_major = keys.transpose(1, 0, 2)
    query_leading = queries.transpose(1, 0, 2)
    value_major = values.transpose(1, 0, 2)
    key_inner = key_pairs
    lower_part = jnp.where(lower_strict, decay_mat * key_inner, 0.0) * strength[:, :, None]
    system = lower_part + jnp.eye(tok_count, dtype=jnp.float32)
    growth = jnp.exp(cumulative)
    scaled_keys = key_major * (strength * growth)[:, :, None]
    scaled_values = value_major * strength[:, :, None]
    inverse = unit_lower_inverse(system)
    key_resolved = jnp.einsum(
        "hts,hsd->htd", inverse, scaled_keys, precision=lax.Precision.HIGH
    )
    value_resolved = jnp.einsum(
        "hts,hsd->htd", inverse, scaled_values, precision=lax.Precision.HIGH
    )
    tail = jnp.exp(cumulative[:, -1:] - cumulative)
    trailing_keys = key_major * tail[:, :, None]
    eye_heads = jnp.broadcast_to(
        jnp.eye(head_dim, dtype=jnp.float32), (value_heads, head_dim, head_dim)
    )
    state_map = growth[:, -1][:, None, None] * eye_heads - jnp.einsum(
        "htk,htj->hkj", trailing_keys, key_resolved, precision=lax.Precision.HIGH
    )
    state_increment = jnp.einsum(
        "xbe,xbz->xez", trailing_keys, value_resolved, precision=lax.Precision.HIGH
    )
    initial_state = chained_state(state_map, state_increment, ("outer", "inner"), n_dev)
    updates = value_resolved - jnp.einsum(
        "mwx,mxd->mwd", key_resolved, initial_state, precision=lax.Precision.HIGH
    )
    query_key = query_pairs * decay_mat
    carried = (
        jnp.einsum("mwx,mxd->mwd", query_leading, initial_state, precision=lax.Precision.HIGH)
        * growth[:, :, None]
    )
    attended = carried + jnp.einsum(
        "hti,hiv->htv", query_key, updates, precision=lax.Precision.HIGH
    )
    attended = attended.transpose(1, 0, 2)
    core_out = (
        rms_scale(attended, output_gain)
        .astype(jnp.bfloat16)
        .reshape(tok_count, value_heads * head_dim)
    )
    return (hidden_out, core_out)


def solution(mesh):
    return jax.shard_map(
        per_device,
        mesh=mesh,
        in_specs=(
            P(("outer", "inner"), None),
            P(("outer", "inner"), None),
            P(("outer", "inner"), None),
            P(),
            P(("outer", "inner"), None, None),
            P(("outer", "inner"), None, None),
            P(("outer", "inner"), None, None),
            P(),
            P(None, "inner"),
            P(),
            P(),
            P(),
            P(),
            P(),
        ),
        out_specs=(P(("outer", "inner"), None), P(("outer", "inner"), None)),
        check_vma=False,
    )
```

```python
import jax
import jax.numpy as jnp
from jax import lax
from jax.sharding import PartitionSpec as P
from jax.experimental import pallas as pl
from jax.experimental.pallas import tpu as pltpu
import functools


def shifted(value, axis, steps):
    count = lax.axis_size(axis)
    leading, last = (max(0, -steps), min(count, count - steps))
    return lax.ppermute(value, axis, [(source, source + steps) for source in range(leading, last)])


def prefix_2(x, axis, join, neutral):
    place = lax.axis_index(axis)
    gathered = jax.tree.map(
        lambda a, kind: lax.all_gather(a.astype(kind), axis), x, (jnp.bfloat16, jnp.bfloat16)
    )
    state = jax.tree.map(lambda a, e: jnp.zeros_like(a) + jnp.asarray(e, a.dtype), x, neutral)

    def one(lap, state):
        return join(
            state,
            jax.tree.map(
                lambda a, own: lax.dynamic_index_in_dim(a, lap, 0, False).astype(own.dtype),
                gathered,
                x,
            ),
        )

    return lax.fori_loop(0, place, one, state)


def shortened(x):

    def short(part):
        return part.astype(jnp.bfloat16) if part.dtype == jnp.float32 else part

    return jax.tree.map(short, x)


def spread_2(value, axis, source):
    kept = jnp.where(lax.axis_index(axis) == source, value, 0).astype(value.dtype)
    return lax.psum(kept, axis)


def entering(x, axis, combine, identity):
    length, place = (lax.axis_size(axis), lax.axis_index(axis))
    everything = jax.tree.map(
        lambda part, kind: lax.all_gather(part.astype(kind), axis),
        x,
        jax.tree.map(lambda a: jnp.bfloat16 if a.dtype == jnp.float32 else a.dtype, x),
    )
    start = jax.tree.map(
        lambda part, zero: jnp.broadcast_to(jnp.asarray(zero, part.dtype), part.shape), x, identity
    )

    def lap(k, before):
        reached = k < place
        new = combine(
            before, jax.tree.map(lambda part, own: part[k].astype(own.dtype), everything, x)
        )
        return jax.tree.map(lambda a, b: jnp.where(reached, a, b), new, before)

    return lax.fori_loop(0, length, lap, start)


def rms_scale(values, gain):
    wide = values.astype(jnp.float32)
    return wide * lax.rsqrt(jnp.mean(wide * wide, axis=-1, keepdims=True) + 1e-06) * gain


def unit_heads(values):
    return values * lax.rsqrt(jnp.sum(values * values, axis=-1, keepdims=True) + 1e-06)


def run_experts(piece, gate_weight, up_weight, down_weight):
    gate = jnp.einsum("esd,edf->esf", piece, gate_weight, preferred_element_type=jnp.float32)
    upper = jnp.einsum("esd,edf->esf", piece, up_weight, preferred_element_type=jnp.float32)
    hidden = (jax.nn.silu(gate) * upper).astype(jnp.bfloat16)
    return jnp.einsum(
        "esf,efd->esd", hidden, down_weight, preferred_element_type=jnp.float32
    ).astype(jnp.bfloat16)


def unit_lower_inverse(system):
    size = system.shape[-1]
    rows = lax.broadcasted_iota(jnp.int32, (size, size), 0)
    cols = lax.broadcasted_iota(jnp.int32, (size, size), 1)
    lower = system - jnp.eye(size, dtype=system.dtype)
    levels = size.bit_length() - 1

    def level(number, inverse):
        width = jnp.left_shift(1, number)
        corner = (
            (rows // (2 * width) == cols // (2 * width))
            & ((rows // width) % 2 == 1)
            & ((cols // width) % 2 == 0)
        )
        part = jnp.where(corner, lower, 0.0)
        return inverse - jnp.einsum(
            "...ij,...jk->...ik",
            inverse,
            jnp.einsum("...ij,...jk->...ik", part, inverse, precision=lax.Precision.HIGH),
            precision=lax.Precision.HIGH,
        )

    first = ((rows // 2 == cols // 2) & (rows % 2 == 1) & (cols % 2 == 0))
    start = jnp.eye(size, dtype=system.dtype) - jnp.where(first, lower, 0.0)
    return lax.fori_loop(1, levels, level, start)


def join_maps(earlier, later):
    first_map, first_state = earlier
    next_map, next_state = later
    joined_map = jnp.einsum("hij,hjk->hik", next_map, first_map, precision=lax.Precision.HIGHEST)
    joined_state = (
        jnp.einsum("hij,hjv->hiv", next_map, first_state, precision=lax.Precision.HIGHEST)
        + next_state
    )
    return (joined_map, joined_state)


def shifted_linear(value, axes, count, steps):
    return lax.ppermute(value, axes, [(source, source + steps) for source in range(count - steps)])


def scan_kernel(count, axes, groups, map_ref, state_ref, out_ref, own_map, own_state, send_map,
                send_state, land_map, land_state, send_sems, recv_sems):
    place = lax.axis_index(axes)
    span = map_ref.shape[0] // groups
    own_map[...] = map_ref[...]
    own_state[...] = state_ref[...]
    rounds = []
    steps = 1
    while steps < count:
        rounds.append(steps)
        steps *= 2
    rounds.append(1)
    total = len(rounds)
    inner = lax.axis_size(axes[1])

    def copies(number, group):
        other = place + rounds[number]
        heads = pl.ds(group * span, span)
        found = [
            pltpu.make_async_remote_copy(
                src_ref=send_state.at[number, heads], dst_ref=land_state.at[number, heads],
                send_sem=send_sems.at[number, group, 0], recv_sem=recv_sems.at[number, group, 0],
                device_id=(other // inner, other % inner), device_id_type=pl.DeviceIdType.MESH)
        ]
        if number < total - 2:
            found.append(
                pltpu.make_async_remote_copy(
                    src_ref=send_map.at[number, heads], dst_ref=land_map.at[number, heads],
                    send_sem=send_sems.at[number, group, 1], recv_sem=recv_sems.at[number, group, 1],
                    device_id=(other // inner, other % inner), device_id_type=pl.DeviceIdType.MESH)
            )
        return found

    def joined(number, group):
        def head(h, carry):
            mine = own_map[h]
            high = mine.astype(jnp.bfloat16)
            low = (mine - high.astype(jnp.float32)).astype(jnp.bfloat16)

            def apply(far):
                return jnp.dot(high, far, preferred_element_type=jnp.float32) + jnp.dot(
                    low, far, preferred_element_type=jnp.float32)

            own_state[h] = apply(land_state[number, h]) + own_state[h]
            if number < total - 2:
                own_map[h] = apply(land_map[number, h])
            return carry

        lax.fori_loop(group * span, group * span + span, head, 0)

    for number in range(total):
        for group in range(groups):
            heads = pl.ds(group * span, span)
            if number > 0:
                @pl.when(place >= rounds[number - 1])
                def _():
                    for copy in copies(number - 1, group):
                        copy.wait_recv()
                    joined(number - 1, group)
            send_state[number, heads] = own_state[heads].astype(jnp.bfloat16)
            if number < total - 2:
                send_map[number, heads] = own_map[heads].astype(jnp.bfloat16)

            @pl.when(place + rounds[number] < count)
            def _():
                for copy in copies(number, group):
                    copy.start()

    for group in range(groups):
        heads = pl.ds(group * span, span)

        @pl.when(place >= 1)
        def _():
            for copy in copies(total - 1, group):
                copy.wait_recv()
            out_ref[heads] = land_state[total - 1, heads].astype(jnp.float32)

        @pl.when(place < 1)
        def _():
            out_ref[heads] = jnp.zeros_like(out_ref[heads])

    for number in range(total):
        @pl.when(place + rounds[number] < count)
        def _():
            for group in range(groups):
                for copy in copies(number, group):
                    copy.wait_send()


def chained_state(state_map, state_increment, axes, count):
    heads, size, width = state_increment.shape
    rounds = 1
    while (1 << (rounds - 1)) < count:
        rounds += 1
    groups = 4
    block = pltpu.VMEM((rounds, heads, size, width), jnp.bfloat16)
    return pl.pallas_call(
        functools.partial(scan_kernel, count, axes, groups),
        out_shape=jax.ShapeDtypeStruct(state_increment.shape, jnp.float32),
        in_specs=[pl.BlockSpec(memory_space=pltpu.VMEM)] * 2,
        out_specs=pl.BlockSpec(memory_space=pltpu.VMEM),
        scratch_shapes=[
            pltpu.VMEM(state_map.shape, jnp.float32),
            pltpu.VMEM(state_increment.shape, jnp.float32),
            pltpu.VMEM((rounds, heads, size, size), jnp.bfloat16),
            block,
            pltpu.VMEM((rounds, heads, size, size), jnp.bfloat16),
            block,
            pltpu.SemaphoreType.DMA((rounds, groups, 2)),
            pltpu.SemaphoreType.DMA((rounds, groups, 2)),
        ],
        compiler_params=pltpu.CompilerParams(has_side_effects=True, vmem_limit_bytes=48 * 1024 * 1024),
    )(state_map, state_increment)


def per_device(
    tokens_in,
    expert_ids,
    route_weight,
    first_gain,
    gate_weight,
    up_weight,
    down_weight,
    second_gain,
    mixer_weight,
    gating_weight,
    filter_taps,
    decay_log,
    decay_bias,
    output_gain,
):
    n_outer = lax.axis_size("outer")
    n_inner = lax.axis_size("inner")
    n_dev = n_outer * n_inner
    tok_count, width = tokens_in.shape
    top_count = expert_ids.shape[1]
    local_experts = gate_weight.shape[0]
    experts_all = local_experts * n_dev
    capacity = max(2, 6 * tok_count * top_count // (5 * experts_all))
    rows_half = mixer_weight.shape[0] // 2
    side = lax.axis_index("outer") % 2
    own_rows = lax.dynamic_slice_in_dim(mixer_weight, side * rows_half, rows_half, axis=0)
    own_half = lax.all_gather(own_rows, "inner", axis=1, tiled=True)
    other_half = lax.ppermute(
        own_half, "outer", [(source, source ^ 1) for source in range(n_outer)]
    )
    normed_first = rms_scale(tokens_in, first_gain).astype(jnp.bfloat16)
    mix_weight = route_weight / jnp.sum(route_weight, axis=1, keepdims=True)
    flat_ids = expert_ids
    target = (
        flat_ids % local_experts * (n_dev * capacity)
        + flat_ids // local_experts * capacity
    )
    onehot = (flat_ids[:, :, None] == jnp.arange(experts_all, dtype=jnp.int32)[None, None, :]).astype(
        jnp.int32
    )
    counted = jnp.sum(onehot, axis=1)
    before = jnp.cumsum(counted, axis=0) - counted
    slot_index = jnp.sum(before[:, None, :] * onehot, axis=2)
    target = target + slot_index
    slots = jnp.arange(n_dev * local_experts * capacity, dtype=jnp.int32)
    hits = target[:, :, None] == slots[None, None, :]
    dispatch = jnp.any(hits, axis=1).astype(jnp.bfloat16)
    outgoing = jnp.einsum(
        "ts,td->sd", dispatch, normed_first, preferred_element_type=jnp.float32
    ).astype(jnp.bfloat16)
    outgoing = outgoing.reshape(local_experts, n_dev * capacity, width)
    served = run_experts(
        lax.all_to_all(outgoing, ("outer", "inner"), split_axis=1, concat_axis=1, tiled=True),
        gate_weight,
        up_weight,
        down_weight,
    )
    returned = lax.all_to_all(served, ("outer", "inner"), split_axis=1, concat_axis=1, tiled=True)
    returned = returned.reshape(-1, width)
    combine = jnp.sum(jnp.where(hits, mix_weight[:, :, None], 0.0), axis=1)
    combine_hi = combine.astype(jnp.bfloat16)
    combine_lo = (combine - combine_hi.astype(jnp.float32)).astype(jnp.bfloat16)
    mixture = jnp.dot(combine_hi, returned, preferred_element_type=jnp.float32) + jnp.dot(
        combine_lo, returned, preferred_element_type=jnp.float32
    )
    hidden_out = (tokens_in.astype(jnp.float32) + mixture).astype(jnp.bfloat16)
    normed_second = rms_scale(hidden_out, second_gain).astype(jnp.bfloat16)
    mixed = jnp.dot(
        lax.dynamic_slice_in_dim(normed_second, side * rows_half, rows_half, axis=1),
        own_half,
        preferred_element_type=jnp.float32,
    ) + jnp.dot(
        lax.dynamic_slice_in_dim(normed_second, (1 - side) * rows_half, rows_half, axis=1),
        other_half,
        preferred_element_type=jnp.float32,
    )
    projected = mixed.astype(jnp.bfloat16)
    gating = jnp.dot(normed_second, gating_weight, preferred_element_type=jnp.float32)
    taps = filter_taps.shape[0]
    rim = shifted(projected[tok_count - (taps - 1) :], ("outer", "inner"), 1)
    padded = jnp.concatenate([rim, projected], axis=0).astype(jnp.float32)
    filtered = jnp.zeros(projected.shape, jnp.float32)
    for tap_index in range(taps):
        filtered = (
            filtered
            + filter_taps[tap_index].astype(jnp.float32) * padded[tap_index : tap_index + tok_count]
        )
    filtered = jax.nn.silu(filtered)
    head_dim = output_gain.shape[0]
    value_heads = decay_log.shape[0]
    key_heads = (projected.shape[1] - value_heads * head_dim) // (2 * head_dim)
    ratio = value_heads // key_heads
    queries = unit_heads(
        filtered[:, : key_heads * head_dim].reshape(tok_count, key_heads, head_dim)
    ) * head_dim ** (-0.5)
    keys = unit_heads(
        filtered[:, key_heads * head_dim : 2 * key_heads * head_dim].reshape(
            tok_count, key_heads, head_dim
        )
    )
    values = filtered[:, 2 * key_heads * head_dim :].reshape(tok_count, value_heads, head_dim)
    queries = jnp.repeat(queries, ratio, axis=1)
    keys = jnp.repeat(keys, ratio, axis=1)
    strength = jax.nn.sigmoid(gating[:, :value_heads]).T
    log_decay = (-jnp.exp(decay_log) * jax.nn.softplus(gating[:, value_heads:] + decay_bias)).T
    cumulative = jnp.cumsum(log_decay, axis=1)
    positions = jnp.arange(tok_count)
    lower_incl = positions[:, None] >= positions[None, :]
    lower_strict = positions[:, None] > positions[None, :]
    spread = cumulative[:, :, None] - cumulative[:, None, :]
    decay_mat = jnp.where(lower_incl, jnp.exp(jnp.where(lower_incl, spread, 0.0)), 0.0)
    key_major = keys.transpose(1, 0, 2)
    query_leading = queries.transpose(1, 0, 2)
    value_major = values.transpose(1, 0, 2)
    key_inner = jnp.einsum("htd,hid->hti", key_major, key_major, precision=lax.Precision.HIGH)
    lower_part = jnp.where(lower_strict, decay_mat * key_inner, 0.0) * strength[:, :, None]
    system = lower_part + jnp.eye(tok_count, dtype=jnp.float32)
    growth = jnp.exp(cumulative)
    scaled_keys = key_major * (strength * growth)[:, :, None]
    scaled_values = value_major * strength[:, :, None]
    inverse = unit_lower_inverse(system)
    resolved = jnp.einsum(
        "hts,hsd->htd",
        inverse,
        jnp.concatenate([scaled_keys, scaled_values], axis=-1),
        precision=lax.Precision.HIGH,
    )
    key_resolved, value_resolved = resolved[..., :head_dim], resolved[..., head_dim:]
    tail = jnp.exp(cumulative[:, -1:] - cumulative)
    trailing_keys = key_major * tail[:, :, None]
    eye_heads = jnp.broadcast_to(
        jnp.eye(head_dim, dtype=jnp.float32), (value_heads, head_dim, head_dim)
    )
    state_map = growth[:, -1][:, None, None] * eye_heads - jnp.einsum(
        "htk,htj->hkj", trailing_keys, key_resolved, precision=lax.Precision.HIGH
    )
    state_increment = jnp.einsum(
        "xbe,xbz->xez", trailing_keys, value_resolved, precision=lax.Precision.HIGH
    )
    initial_state = chained_state(state_map, state_increment, ("outer", "inner"), n_dev)
    updates = value_resolved - jnp.einsum(
        "mwx,mxd->mwd", key_resolved, initial_state, precision=lax.Precision.HIGH
    )
    query_key = (
        jnp.einsum("htd,hid->hti", query_leading, key_major, precision=lax.Precision.HIGH)
        * decay_mat
    )
    carried = (
        jnp.einsum("mwx,mxd->mwd", query_leading, initial_state, precision=lax.Precision.HIGH)
        * growth[:, :, None]
    )
    attended = carried + jnp.einsum(
        "hti,hiv->htv", query_key, updates, precision=lax.Precision.HIGH
    )
    attended = attended.transpose(1, 0, 2)
    core_out = (
        rms_scale(attended, output_gain)
        .astype(jnp.bfloat16)
        .reshape(tok_count, value_heads * head_dim)
    )
    return (hidden_out, core_out)


def solution(mesh):
    return jax.shard_map(
        per_device,
        mesh=mesh,
        in_specs=(
            P(("outer", "inner"), None),
            P(("outer", "inner"), None),
            P(("outer", "inner"), None),
            P(),
            P(("outer", "inner"), None, None),
            P(("outer", "inner"), None, None),
            P(("outer", "inner"), None, None),
            P(),
            P(None, "inner"),
            P(),
            P(),
            P(),
            P(),
            P(),
        ),
        out_specs=(P(("outer", "inner"), None), P(("outer", "inner"), None)),
        check_vma=False,
    )
```
